32 devices in a mesh: groups: 2 (over x), gx: 16 (over z, y, core).
Axes of the slice: x: 2, y: 2, z: 4, core: 2. Of those that a mesh axis runs over, the one named last changes fastest.
Arguments:
- points: bfloat16 [32, 6, 1, 128, 512], P(('groups', 'gx')), parts along dimension 0, may hold values from -6 to 6
- order: int32 [32, 6, 1, 128], P(('groups', 'gx')), parts along dimension 0, may hold values from 0 to 127, each once within a row
- masks: int32 [32, 6, 1, 26], P(('groups', 'gx')), parts along dimension 0, may hold values 0 or 1
- counts: int32 [32, 6, 1], P('groups'), parts along dimension 0, may hold values from 1 to 128
- gain: float32 [512], replicated, may hold values from 0.5 to 1.5
- shift_bias: float32 [512], replicated, may hold values from -3 to 3
- w_qkv: bfloat16 [512, 1536], replicated, may hold values from -1.5 to 1.5
- w_out: bfloat16 [512, 512], replicated, may hold values from -0.25 to 0.25
Outputs:
- result: bfloat16 [32, 6, 1, 128, 512], P(('groups', 'gx')), parts along dimension 0
The draws below stay inside these ranges and needn't reach their ends.
There are 2 independent parts, one for each index of `groups`. The reference program is written for one: setup_inputs(seed, part) draws one part's arguments, and reference() takes and returns one part's arrays. A program takes and returns all parts, laid end to end along the dimension named above; an argument that names none is the same for every part. Nothing has to cross between parts.
All inputs are finite; a program needn't handle non-finite values. No bound on the sum of `masks` on one device may be relied on, other than what follows from the above.
Results may differ from the reference program's by a relative error of at most 0.012.
Values may be sent and summed in bfloat16 or wider, within the bound.
No kernel may reach another device: no remote copies, remote signals or barrier semaphores. Data moves between devices by JAX's collectives and lax.ppermute only.
A program may use at most 128 MiB of HBM per device.

```python
import jax
import jax.numpy as jnp
from jax import lax

D = 512
HEADS = 8
P_SIZE = 128
BY = 6
BZ = 1
NBX = 16


def bias_normal(key):
    values = jax.random.normal(jax.random.fold_in(key, 1701), (D,), jnp.float32)
    return jnp.clip(values, -6.0, 6.0)


def draw_shift_bias(key, part):
    return 0.5 * bias_normal(key)


def draw_w_qkv(key, part):
    spread = D ** (-0.5)
    noise = jax.random.normal(jax.random.fold_in(key, 1702), (D, 3 * D), jnp.float32) * spread
    noise = jnp.clip(noise, -6.0 * spread, 6.0 * spread)
    return noise.astype(jnp.bfloat16)


def plant(drawn, stream_key, least, top_value):
    shape = drawn.shape
    index_at = [jax.random.randint(jax.random.fold_in(stream_key, axis), (), 0, shape[axis]) for axis in range(len(shape))]
    drawn = drawn.at[tuple(index_at)].set(least)
    longest = shape.index(max(shape))
    index_at[longest] = (index_at[longest] + 1) % shape[longest]
    return drawn.at[tuple(index_at)].set(top_value)


def steps_of(own_key, dims, pieces, low, top_value):
    level, own = 1.0, jax.random.fold_in(own_key, 6)
    for position, parts in pieces:
        heights = jnp.exp(jax.random.uniform(jax.random.fold_in(own, position), (parts,), jnp.float32, low / len(pieces), top_value / len(pieces)))
        level = level * jnp.repeat(heights, dims[position] // parts).reshape([-1 if axis == position else 1 for axis in range(len(dims))])
    return level


def centred(key, extent, deviation, bound, split=(), kind=jnp.bfloat16):
    level = steps_of(key, extent, split, -0.22, 0.18) if split else 1.0
    array = jax.random.normal(key, extent, jnp.float32) * deviation * level
    return jnp.minimum(jnp.maximum(array, -bound), bound).astype(kind)


def setup_inputs(seed: int = 0, part: int = 0) -> dict:
    keys = jax.random.split(jax.random.key(seed), 9)
    part_splits = jax.random.split(jax.random.fold_in(keys[8], part), 9)
    points = centred(part_splits[0], (NBX, BY, BZ, P_SIZE, D), 1.0, 6.0, ((0, 16),))
    order = jax.vmap(lambda own: jax.random.permutation(own, P_SIZE))(jax.random.split(part_splits[1], NBX * BY * BZ)).reshape((NBX, BY, BZ, P_SIZE)).astype(jnp.int32)
    masks = plant((jax.random.randint(part_splits[2], (NBX, BY, BZ, 26), 0, 2) < 1).astype(jnp.int32), jax.random.fold_in(part_splits[2], 1), 0, 1)
    counts = plant(jax.random.randint(part_splits[3], (NBX, BY, BZ), 1, P_SIZE + 1), jax.random.fold_in(part_splits[3], 1), 1, P_SIZE).astype(jnp.int32)
    gain = jnp.clip(1.0 + 0.1 * jax.random.normal(keys[4], (D,), jnp.float32), 0.5, 1.5)
    shift_bias = draw_shift_bias(jax.random.fold_in(keys[8], 71), part)
    w_qkv = draw_w_qkv(jax.random.fold_in(keys[8], 71), part)
    w_out = centred(keys[7], (D, D), D ** -0.5, 0.25)
    return dict(points=points, order=order, masks=masks, counts=counts, gain=gain, shift_bias=shift_bias, w_qkv=w_qkv, w_out=w_out)


neighbour_offsets = [(a, b, c) for a in (-1, 0, 1) for b in (-1, 0, 1) for c in (-1, 0, 1)]

def column_of(a, b, c):
    index = 9 * (a + 1) + 3 * (b + 1) + (c + 1)
    return index if index < 13 else index - 1

def layer_norm(tiled, gain, shift_bias):
    values = tiled.astype(jnp.float32)
    mean = lax.optimization_barrier(jnp.mean(values, axis=-1, keepdims=True))
    var = lax.optimization_barrier(jnp.mean((values - mean) ** 2, axis=-1, keepdims=True))
    return ((values - mean) * lax.rsqrt(var + 1e-05) * gain + shift_bias).astype(jnp.bfloat16)

def attend_slab(queries, slabs, counts_pad, masks, heads):
    by, bz, p, width = queries.shape
    hd = width // heads
    scale = 1.0 / hd ** 0.5
    positions = jnp.arange(p, dtype=jnp.int32)
    blocks = []
    valids = []
    for a, b, c in neighbour_offsets:
        block = slabs[a + 1][1 + b:1 + b + by, 1 + c:1 + c + bz]
        near = counts_pad[a + 1, 1 + b:1 + b + by, 1 + c:1 + c + bz]
        valid = positions[None, None, :] < near[:, :, None]
        if (a, b, c) != (0, 0, 0):
            valid = valid & (masks[:, :, column_of(a, b, c)][:, :, None] == 1)
        blocks.append(block)
        valids.append(valid)
    keyvals = jnp.concatenate(blocks, axis=2).reshape(by * bz, -1, 2 * width)
    valid = jnp.concatenate(valids, axis=2).reshape(by * bz, -1)
    flat_queries = queries.reshape(by * bz, p, width)

    def one_block(operands):
        query, keyval, mask = operands
        qh = query.reshape(p, heads, hd).astype(jnp.float32)
        kh = keyval[:, :width].reshape(-1, heads, hd).astype(jnp.float32)
        vh = keyval[:, width:].reshape(-1, heads, hd).astype(jnp.float32)
        scores = jnp.einsum('qhd,khd->hqk', qh, kh) * scale
        scores = jnp.where(mask[None, None, :], scores, -1e+30)
        top = lax.optimization_barrier(jnp.max(scores, axis=-1, keepdims=True))
        probs = jnp.where(mask[None, None, :], jnp.exp(scores - top), 0.0)
        total = lax.optimization_barrier(jnp.sum(probs, axis=-1))
        rounded = probs.astype(jnp.bfloat16).astype(jnp.float32)
        accum = jnp.einsum('hqk,khd->qhd', rounded, vh)
        return (accum / jnp.transpose(total)[..., None]).reshape(p, width)
    attn = lax.map(one_block, (flat_queries, keyvals, valid))
    return attn.reshape(by, bz, p, width).astype(jnp.bfloat16)

def reference(points, order, masks, counts, gain, shift_bias, w_qkv, w_out):
    nbx, by, bz, p, width = points.shape
    tiled = jnp.take_along_axis(points, order[..., None], axis=3)
    normed = layer_norm(tiled, gain, shift_bias)
    qkv = jnp.dot(normed.reshape(-1, width), w_qkv, preferred_element_type=jnp.float32).astype(jnp.bfloat16)
    qkv = qkv.reshape(nbx, by, bz, p, 3 * width)
    queries = qkv[..., :width]
    keyvals = jnp.pad(qkv[..., width:], ((1, 1), (1, 1), (1, 1), (0, 0), (0, 0)))
    counts_pad = jnp.pad(counts, 1)

    def one_slab(index):
        index = index.astype(jnp.int32)
        slab = lax.dynamic_slice_in_dim(keyvals, index, 3, 0)
        near = lax.dynamic_slice_in_dim(counts_pad, index, 3, 0)
        query = lax.dynamic_index_in_dim(queries, index, 0, keepdims=False)
        mask = lax.dynamic_index_in_dim(masks, index, 0, keepdims=False)
        return attend_slab(query, (slab[0], slab[1], slab[2]), near, mask, HEADS)
    attn = lax.map(one_slab, jnp.arange(nbx, dtype=jnp.int32))
    mixed = jnp.dot(attn.reshape(-1, width), w_out, preferred_element_type=jnp.float32).reshape(nbx, by, bz, p, width)
    mixed = tiled.astype(jnp.float32) + mixed
    live = jnp.arange(p, dtype=jnp.int32)[None, None, None, :] < counts[..., None]
    return jnp.where(live[..., None], mixed, 0.0).astype(jnp.bfloat16)
```

```python
import functools

import jax
import jax.numpy as jnp
from jax import lax
from jax.experimental import pallas as pl
from jax.experimental.pallas import tpu as pltpu
from jax.sharding import PartitionSpec as P

HEADS = 8
NEG = -1e30
ONES = 16
LIMIT = 24 * 1024 * 1024


def nt(a, b):
    return lax.dot_general(a, b, (((1,), (1,)), ((), ())), preferred_element_type=jnp.float32)


def tn(a, b):
    return lax.dot_general(a, b, (((0,), (0,)), ((), ())), preferred_element_type=jnp.float32)


def nn(a, b):
    return jnp.dot(a, b, preferred_element_type=jnp.float32)


def normalise(tiled, gain, shift):
    values = tiled.astype(jnp.float32)
    mean = jnp.mean(values, axis=-1, keepdims=True)
    var = jnp.mean((values - mean) ** 2, axis=-1, keepdims=True)
    return ((values - mean) * lax.rsqrt(var + 1e-05) * gain + shift).astype(jnp.bfloat16)


def gather_kernel(points, order, counts, tiled, first, second):
    _, by, _, p, width = points.shape
    me = lax.axis_index("gx")
    slot = lax.broadcasted_iota(jnp.int32, (p, p), 0)
    place = lax.broadcasted_iota(jnp.int32, (1, p), 1)
    half = by // 2
    for j in range(by):
        row = order[0, j]
        row = jnp.where(place < counts[me, j, 0], row, row[:, :1])
        pick = (slot == row).astype(jnp.float32).astype(jnp.bfloat16)
        got = tn(pick, points[0, j, 0]).astype(jnp.bfloat16)
        tiled[j] = got
        if j < half:
            first[j] = got
        else:
            second[j - half] = got


def list_items(items, masks, by, n, a, j0, j1):
    me = lax.axis_index("gx")
    there = (me + a >= 0) & (me + a < n)

    def step(t, found):
        i, b = t // 3, t % 3 - 1
        j = i + b
        index = 9 * (a + 1) + 3 * (b + 1) + 1
        column = jnp.where(index > 13, index - 1, index)
        itself = (a == 0) & (b == 0)
        on = (j >= j0) & (j < j1) & there & (itself | (masks[0, i, 0, column] == 1))

        @pl.when(on)
        def _():
            items[0, found] = i
            items[1, found] = j - j0

        return found + on.astype(jnp.int32)

    found = lax.fori_loop(0, 3 * by, step, jnp.int32(0))
    items[0, found] = by
    items[1, found] = 0
    return (found + 1) // 2


def attend(items, pairs, keys, vals, qt, top, acc):
    groups = qt.shape[1]
    depth, lanes = qt.shape[2:]
    hd, p = depth // 2, lanes // 2

    def step(t, carry):
        work = []
        for u in range(2):
            i, j = items[0, 2 * t + u], items[1, 2 * t + u]
            for g in range(groups):
                key = keys[j, :, g * depth : (g + 1) * depth]
                work.append((i, j, g, nn(key, qt[i, g])))
        for i, j, g, s in work:
            cols = slice(g * lanes, (g + 1) * lanes)
            old = top[i, :, cols]
            new = jnp.maximum(old, jnp.max(s, axis=0, keepdims=True))
            probs = jnp.exp(s - new).astype(jnp.bfloat16)
            fade = jnp.exp(old - new)
            out = nn(vals[j, g], probs)
            both = jnp.concatenate([out[:hd, :p], out[hd:depth, p:]], axis=1)
            top[i, :, cols] = new
            acc[i, :hd, cols] = acc[i, :hd, cols] * fade + both
            acc[i, hd:, cols] = acc[i, hd:, cols] * fade + out[depth : depth + 8]
        return carry

    lax.fori_loop(0, pairs, step, 0)


def make_values(vals, j, vt, live, groups):
    depth = vt.shape[0] // groups
    vt = jnp.where(live, vt, 0.0).astype(jnp.bfloat16)
    for g in range(groups):
        vals[j, g, :depth] = vt[g * depth : (g + 1) * depth]
        vals[j, g, depth:] = jnp.broadcast_to(
            live.astype(jnp.float32).astype(jnp.bfloat16), (ONES, live.shape[1])
        )


def own_kernel(
    n, tiled, masks, counts, gain, shift, w_qkv, qt, top, acc, w_vt, nrm, keys, vals, w_qt, items
):
    by, p, width = tiled.shape
    groups, depth = qt.shape[1:3]
    hd = depth // 2
    me = lax.axis_index("gx")
    place = lax.broadcasted_iota(jnp.int32, (1, p), 1)
    w_qt[...] = w_qkv[:, :width].T
    w_vt[...] = w_qkv[:, 2 * width :].T
    for j in range(by):
        nrm[j * p : (j + 1) * p] = normalise(tiled[j], gain[...], shift[...])
    zeros = jnp.zeros((hd, p), jnp.bfloat16)
    for c in range(0, by, 2):
        rows = slice(c * p, (c + 2) * p)
        x = nrm[rows]
        made = nn(x, w_qkv[:, width : 2 * width]).astype(jnp.bfloat16)
        keys[c] = made[:p]
        keys[c + 1] = made[p:]
        q = nt(w_qt[...], x).astype(jnp.bfloat16) * jnp.bfloat16(1.0 / hd**0.5)
        v = nt(w_vt[...], x)
        for u in range(2):
            i, cols = c + u, slice(u * p, (u + 1) * p)
            make_values(vals, i, v[:, cols], place < counts[me, i, 0], groups)
            for g in range(groups):
                mid = g * depth + hd
                qt[i, g, :hd, :p] = q[g * depth : mid, cols]
                qt[i, g, :hd, p:] = zeros
                qt[i, g, hd:, :p] = zeros
                qt[i, g, hd:, p:] = q[mid : mid + hd, cols]
    top[...] = jnp.full_like(top, NEG)
    acc[...] = jnp.zeros_like(acc)
    pairs = list_items(items, masks, by, n, 0, 0, by)
    attend(items, pairs, keys, vals, qt, top, acc)


def rim_offset(which):
    toward = 1 - 2 * (lax.axis_index("gx") % 2)
    return toward if which == "near" else -toward


def rim_work(
    n, which, j0, by, rim, masks, counts, gain, shift, w_qkv, w_vt, qt, top, acc, nrm, keys, vals, items
):
    blocks, p, width = rim.shape
    groups = qt.shape[1]
    me = lax.axis_index("gx")
    a = rim_offset(which)
    slab = jnp.clip(me + a, 0, n - 1)
    place = lax.broadcasted_iota(jnp.int32, (1, p), 1)
    for j in range(blocks):
        nrm[j * p : (j + 1) * p] = normalise(rim[j], gain[...], shift[...])
    made = nn(nrm[...], w_qkv[:, width : 2 * width]).astype(jnp.bfloat16)
    v = nt(w_vt[...], nrm[...])
    for j in range(blocks):
        keys[j] = made[j * p : (j + 1) * p]
        live = place < counts[slab, j0 + j, 0]
        make_values(vals, j, v[:, j * p : (j + 1) * p], live, groups)
    pairs = list_items(items, masks, by, n, a, j0, j0 + blocks)
    attend(items, pairs, keys, vals, qt, top, acc)


def rim_kernel(
    n, which, j0, by, rim, masks, counts, gain, shift, w_qkv, w_vt, qt, top_in, acc_in, top, acc, *scratch
):
    rim_work(n, which, j0, by, rim, masks, counts, gain, shift, w_qkv, w_vt, qt, top, acc, *scratch)


def last_kernel(
    n, which, j0, by, rim, masks, counts, gain, shift, w_qkv, w_vt, qt, top_in, acc_in, tiled, w_out,
    result, top, acc, *scratch
):
    rim_work(n, which, j0, by, rim, masks, counts, gain, shift, w_qkv, w_vt, qt, top, acc, *scratch)
    groups, depth, lanes = qt.shape[1:]
    hd, p = depth // 2, lanes // 2
    me = lax.axis_index("gx")
    place = lax.broadcasted_iota(jnp.int32, (p, 1), 0)
    for i in range(by):
        total = acc[i, hd : hd + 1]
        attn = acc[i, :hd] / total
        attn = jnp.concatenate(
            [attn[:, h * p : (h + 1) * p] for h in range(2 * groups)], axis=0
        ).astype(jnp.bfloat16)
        mixed = tiled[i].astype(jnp.float32) + tn(attn, w_out[...])
        live = place < counts[me, i, 0]
        result[0, i, 0] = jnp.where(live, mixed, 0.0).astype(jnp.bfloat16)


def vmem(x):
    return pltpu.with_memory_space_constraint(x, pltpu.VMEM)


def shards(n, points, order, masks, counts, gain, shift_bias, w_qkv, w_out):
    _, by, _, p, width = points.shape
    hd = width // HEADS
    groups, depth, lanes = HEADS // 2, 2 * hd, 2 * p
    half = by // 2
    whole = pl.BlockSpec(memory_space=pltpu.VMEM)
    smem = pl.BlockSpec(memory_space=pltpu.SMEM)
    params = pltpu.CompilerParams(vmem_limit_bytes=LIMIT)
    bf16, f32 = jnp.bfloat16, jnp.float32

    def struct(shape, kind):
        return jax.ShapeDtypeStruct(shape, kind)

    gain, shift = gain[None], shift_bias[None]
    tiled, first, second = pl.pallas_call(
        gather_kernel,
        out_shape=(
            struct((by, p, width), bf16),
            struct((half, p, width), bf16),
            struct((by - half, p, width), bf16),
        ),
        in_specs=[whole, whole, smem],
        out_specs=(whole,) * 3,
        compiler_params=params,
        name="gather",
    )(points, order, counts)
    near_pairs = [(i, i ^ 1) for i in range(n) if i ^ 1 < n]
    far_pairs = [(i, i + 1) for i in range(1, n - 1, 2)] + [(i + 1, i) for i in range(1, n - 1, 2)]
    far0 = lax.ppermute(first, "gx", far_pairs)
    far1 = lax.ppermute(second, "gx", far_pairs)
    near = lax.ppermute(tiled, "gx", near_pairs)

    def scratch(blocks):
        return [
            pltpu.VMEM((blocks * p, width), bf16),
            pltpu.VMEM((blocks, p, width), bf16),
            pltpu.VMEM((blocks, groups, depth + ONES, p), bf16),
        ]

    items = pltpu.SMEM((2, 3 * by + 2), jnp.int32)
    state = (
        pltpu.VMEM((by + 1, 1, groups * lanes), f32),
        pltpu.VMEM((by + 1, hd + 8, groups * lanes), f32),
    )
    qt, top, acc, w_vt = pl.pallas_call(
        functools.partial(own_kernel, n),
        out_shape=(
            pltpu.VMEM((by + 1, groups, depth, lanes), bf16),
            *state,
            pltpu.VMEM((width, width), bf16),
        ),
        in_specs=[whole, smem, smem, whole, whole, whole],
        out_specs=(whole,) * 4,
        scratch_shapes=[*scratch(by), pltpu.VMEM((width, width), bf16), items],
        compiler_params=params,
        name="own",
    )(tiled, masks, counts, gain, shift, w_qkv)

    def rim(which, j0, block, top, acc):
        return pl.pallas_call(
            functools.partial(rim_kernel, n, which, j0, by),
            out_shape=state,
            in_specs=[whole, smem, smem, *(whole,) * 7],
            out_specs=(whole,) * 2,
            scratch_shapes=[*scratch(block.shape[0]), items],
            input_output_aliases={8: 0, 9: 1},
            compiler_params=params,
            name=f"{which}{j0}",
        )(block, masks, counts, gain, shift, w_qkv, vmem(w_vt), vmem(qt), vmem(top), vmem(acc))

    top, acc = rim("near", 0, near, top, acc)
    top, acc = rim("far", 0, far0, top, acc)
    result, _, _ = pl.pallas_call(
        functools.partial(last_kernel, n, "far", half, by),
        out_shape=(struct((1, by, 1, p, width), bf16), *state),
        in_specs=[whole, smem, smem, *(whole,) * 9],
        out_specs=(whole,) * 3,
        scratch_shapes=[*scratch(by - half), items],
        input_output_aliases={8: 1, 9: 2},
        compiler_params=params,
        name="last",
    )(far1, masks, counts, gain, shift, w_qkv, vmem(w_vt), vmem(qt), vmem(top), vmem(acc), tiled, w_out)
    return result


def solution(mesh):
    placed = (
        P(("groups", "gx"), None, None, None, None),
        P(("groups", "gx"), None, None, None),
        P(("groups", "gx"), None, None, None),
        P("groups", None, None),
        P(),
        P(),
        P(),
        P(),
    )
    return jax.shard_map(
        functools.partial(shards, mesh.shape["gx"]),
        mesh=mesh,
        in_specs=placed,
        out_specs=P(("groups", "gx"), None, None, None, None),
        check_vma=False,
    )
```

```python
import functools

import jax
import jax.numpy as jnp
from jax import lax
from jax.experimental import pallas as pl
from jax.experimental.pallas import tpu as pltpu
from jax.sharding import PartitionSpec as P

HEADS = 8
NEG = -1e30
ONES = 16
LIMIT = 24 * 1024 * 1024
BF16, F32 = jnp.bfloat16, jnp.float32


def tn(a, b):
    return lax.dot_general(a, b, (((0,), (0,)), ((), ())), preferred_element_type=F32)


def nn(a, b):
    return jnp.dot(a, b, preferred_element_type=F32)


def normalise(tiled, gain, shift):
    values = tiled.astype(F32)
    mean = jnp.mean(values, axis=-1, keepdims=True)
    var = jnp.mean((values - mean) ** 2, axis=-1, keepdims=True)
    return ((values - mean) * lax.rsqrt(var + 1e-05) * gain + shift).astype(BF16)


def gather_kernel(
    split, points, order, counts, gain, shift, tiled, first, second, norm, raw, rows, live, sems
):
    _, by, _, p, width = points.shape
    me = lax.axis_index("gx")
    small = [
        pltpu.make_async_copy(order, rows, sems.at[by]),
        pltpu.make_async_copy(counts, live, sems.at[by + 1]),
        pltpu.make_async_copy(gain, norm.at[0:1], sems.at[by + 2]),
        pltpu.make_async_copy(shift, norm.at[1:2], sems.at[by + 3]),
    ]
    large = [pltpu.make_async_copy(points.at[0, j, 0], raw.at[j], sems.at[j]) for j in range(by)]
    for copy in (*small, *large):
        copy.start()
    slot = lax.broadcasted_iota(jnp.int32, (p, p), 0)
    place = lax.broadcasted_iota(jnp.int32, (1, p), 1)
    small[0].wait()
    small[1].wait()
    picks = []
    for j in range(by):
        row = rows[0, j]
        row = jnp.where(place < live[j, 0, me], row, row[:, :1])
        picks.append((slot == row).astype(F32).astype(BF16))
    for j in range(by):
        large[j].wait()
        got = tn(picks[j], raw[j]).astype(BF16)
        tiled[j] = got
        if j < split:
            first[j] = got
        else:
            second[j - split] = got
    small[2].wait()
    small[3].wait()


def toward_near():
    return 1 - 2 * (lax.axis_index("gx") & 1)


def column(side, b):
    index = 9 * (side + 1) + 3 * (b + 1) + 1
    if isinstance(index, int):
        return index if index < 13 else index - 1
    return jnp.where(index > 13, index - 1, index)


def list_pairs(items, masks, by, sides):
    spare = sum(j1 - j0 for _, _, j0, j1, _, _ in sides)
    pairs, ends = jnp.int32(0), []
    for i in range(by):
        start, found, last = pairs, jnp.int32(0), jnp.int32(0)
        most = 0
        for side, exists, j0, j1, tile0, own in sides:
            for b in (0, -1, 1):
                j = i + b
                if not j0 <= j < j1:
                    continue
                tile = tile0 + j - j0
                items[1, 2 * start + found] = tile
                items[2, 2 * start + found] = tile
                most += 1
                if own and b == 0:
                    found = found + 1
                    last = jnp.int32(tile)
                    continue
                on = masks[0, i, 0, column(side, b)] == 1
                on = on if exists is None else on & exists
                found = found + on.astype(jnp.int32)
                last = jnp.where(on, tile, last)
        items[1, 2 * start + found] = last
        items[2, 2 * start + found] = spare
        for u in range((most + 1) // 2):
            items[0, start + u] = i
        pairs = start + ((found + 1) >> 1)
        ends.append(pairs)
    return pairs, ends


def attend(items, low, high, keys, vals, qt, top, acc):
    groups, depth, lanes = qt.shape[1:]
    hd, p = depth // 2, lanes // 2

    def step(t, carry):
        i = items[0, t]
        k0, k1 = items[1, 2 * t], items[1, 2 * t + 1]
        v0, v1 = items[2, 2 * t], items[2, 2 * t + 1]
        for g in range(groups):
            rows = slice(g * depth, (g + 1) * depth)
            cols = slice(g * lanes, (g + 1) * lanes)
            s0 = nn(keys[k0, :, rows], qt[i, g])
            s1 = nn(keys[k1, :, rows], qt[i, g])
            old = top[i, :, cols]
            new = jnp.maximum(old, jnp.max(jnp.maximum(s0, s1), axis=0, keepdims=True))
            probs = jnp.concatenate(
                [jnp.exp(s0 - new).astype(BF16), jnp.exp(s1 - new).astype(BF16)], axis=0
            )
            fade = jnp.exp(old - new)
            out = nn(jnp.concatenate([vals[v0, g], vals[v1, g]], axis=1), probs)
            both = jnp.concatenate([out[:hd, :p], out[hd:depth, p:]], axis=1)
            top[i, :, cols] = new
            acc[i, :hd, cols] = acc[i, :hd, cols] * fade + both
            acc[i, hd:, cols] = acc[i, hd:, cols] * fade + out[depth : depth + 8]
        return carry

    lax.fori_loop(low, high, step, 0)


def put_values(vals, tile, v, live):
    groups, _, p = vals.shape[1:]
    depth = v.shape[1] // groups
    flag = jnp.broadcast_to(live.astype(F32).astype(BF16), (ONES, p))
    vt = jnp.where(live, v.T, 0.0).astype(BF16)
    for g in range(groups):
        vals[tile, g, :depth] = vt[g * depth : (g + 1) * depth]
        vals[tile, g, depth:] = flag


def finish(i, tiled, acc, w_out, alive):
    hd = acc.shape[1] - 8
    p = tiled.shape[1]
    heads = acc.shape[2] // p
    attn = acc[i, :hd] * (1.0 / acc[i, hd : hd + 1])
    attn = jnp.concatenate([attn[:, h * p : (h + 1) * p] for h in range(heads)], axis=0).astype(BF16)
    mixed = tiled[i].astype(F32) + tn(attn, w_out[...])
    place = lax.broadcasted_iota(jnp.int32, (p, 1), 0)
    return jnp.where(place < alive, mixed, 0.0).astype(BF16)


def main_kernel(
    n, tiled, near, norm, masks, counts, w_qkv, w_out, qt, top, acc, w_all, w_last, keys, vals, flags, live,
    items, sems
):
    by, p, width = tiled.shape
    groups, depth = qt.shape[1:3]
    hd = depth // 2
    copies = [
        pltpu.make_async_copy(masks, flags, sems.at[0]),
        pltpu.make_async_copy(counts, live, sems.at[1]),
        pltpu.make_async_copy(w_qkv, w_all, sems.at[2]),
        pltpu.make_async_copy(w_out, w_last, sems.at[3]),
    ]
    for copy in copies:
        copy.start()
    me = lax.axis_index("gx")
    side = toward_near()
    partner = me + side
    exists = (partner >= 0) & (partner < n)
    slab = jnp.clip(partner, 0, n - 1)
    place = lax.broadcasted_iota(jnp.int32, (1, p), 1)
    gain, shift = norm[0:1], norm[1:2]
    top[...] = jnp.full_like(top, NEG)
    acc[...] = jnp.zeros_like(acc)
    vals[2 * by] = jnp.zeros(vals.shape[1:], BF16)
    copies[0].wait()
    copies[1].wait()
    pairs, _ = list_pairs(
        items, flags, by, [(0, None, 0, by, 0, True), (side, exists, 0, by, by, False)]
    )
    zeros = jnp.zeros((hd, p), BF16)
    copies[2].wait()
    for c in range(0, by, 2):
        span = range(c, min(c + 2, by))
        x = jnp.concatenate([normalise(tiled[j], gain, shift) for j in span], axis=0)
        q = (nn(x, w_all[:, :width]).astype(BF16) * BF16(1.0 / hd**0.5)).astype(F32)
        k = nn(x, w_all[:, width : 2 * width]).astype(BF16)
        v = nn(x, w_all[:, 2 * width :])
        for u, i in enumerate(span):
            rows = slice(u * p, (u + 1) * p)
            keys[i] = k[rows]
            put_values(vals, i, v[rows], place < live[i, 0, me])
            t = q[rows].T.astype(BF16)
            for g in range(groups):
                mid = g * depth + hd
                qt[i, g, :hd, :p] = t[g * depth : mid]
                qt[i, g, :hd, p:] = zeros
                qt[i, g, hd:, :p] = zeros
                qt[i, g, hd:, p:] = t[mid : mid + hd]
        x = jnp.concatenate([normalise(near[j], gain, shift) for j in span], axis=0)
        k = nn(x, w_all[:, width : 2 * width]).astype(BF16)
        v = nn(x, w_all[:, 2 * width :])
        for u, i in enumerate(span):
            rows = slice(u * p, (u + 1) * p)
            keys[by + i] = k[rows]
            put_values(vals, by + i, v[rows], place < live[i, 0, slab])
    attend(items, 0, pairs, keys, vals, qt, top, acc)
    copies[3].wait()


def far_work(n, j0, by, rim, norm, masks, counts, w_all, qt, top, acc, keys, vals, flags, live, items, sems):
    blocks, p, width = rim.shape
    copies = [
        pltpu.make_async_copy(masks, flags, sems.at[0]),
        pltpu.make_async_copy(counts, live, sems.at[1]),
    ]
    for copy in copies:
        copy.start()
    side = -toward_near()
    other = lax.axis_index("gx") + side
    exists = (other >= 0) & (other < n)
    slab = jnp.clip(other, 0, n - 1)
    place = lax.broadcasted_iota(jnp.int32, (1, p), 1)
    gain, shift = norm[0:1], norm[1:2]
    vals[blocks] = jnp.zeros(vals.shape[1:], BF16)
    copies[0].wait()
    copies[1].wait()
    pairs, _ = list_pairs(items, flags, by, [(side, exists, j0, j0 + blocks, 0, False)])
    for c in range(0, blocks, 2):
        span = range(c, min(c + 2, blocks))
        x = jnp.concatenate([normalise(rim[j], gain, shift) for j in span], axis=0)
        k = nn(x, w_all[:, width : 2 * width]).astype(BF16)
        v = nn(x, w_all[:, 2 * width :])
        for u, j in enumerate(span):
            rows = slice(u * p, (u + 1) * p)
            keys[j] = k[rows]
            put_values(vals, j, v[rows], place < live[j0 + j, 0, slab])
    attend(items, 0, pairs, keys, vals, qt, top, acc)


def hand_out(blocks, tiled, acc, w_out, live, result, out, sems):
    me = lax.axis_index("gx")
    copies = []
    for u, i in enumerate(blocks):
        out[u] = finish(i, tiled, acc, w_out, live[i, 0, me])
        copies.append(pltpu.make_async_copy(out.at[u], result.at[0, i, 0], sems.at[2 + u]))
        copies[-1].start()
    for copy in copies:
        copy.wait()


def far_kernel(
    n, j0, done, rim, norm, masks, counts, w_all, qt, top_in, acc_in, tiled, w_out, top, acc, result, keys, vals,
    flags, live, items, out, sems
):
    by = tiled.shape[0]
    far_work(n, j0, by, rim, norm, masks, counts, w_all, qt, top, acc, keys, vals, flags, live, items, sems)
    hand_out(done, tiled, acc, w_out, live, result, out, sems)


def last_kernel(
    n, j0, done, rim, norm, masks, counts, w_all, qt, top_in, acc_in, tiled, w_out, result_in, top, acc, result,
    keys, vals, flags, live, items, out, sems
):
    by = tiled.shape[0]
    far_work(n, j0, by, rim, norm, masks, counts, w_all, qt, top, acc, keys, vals, flags, live, items, sems)
    hand_out(done, tiled, acc, w_out, live, result, out, sems)


def vmem(x):
    return pltpu.with_memory_space_constraint(x, pltpu.VMEM)


def hbm(x):
    return pltpu.with_memory_space_constraint(x, pltpu.HBM)


def shards(n, points, order, masks, counts, gain, shift_bias, w_qkv, w_out):
    _, by, bz, p, width = points.shape
    hd = width // HEADS
    groups, depth, lanes = HEADS // 2, 2 * hd, 2 * p
    split = max(by - 2, 1)
    early = max(split - 1, 0)
    whole = pl.BlockSpec(memory_space=pltpu.VMEM)
    apart = pl.BlockSpec(memory_space=pltpu.HBM)
    params = pltpu.CompilerParams(vmem_limit_bytes=LIMIT)
    points, order, masks, w_qkv, w_out = map(hbm, (points, order, masks, w_qkv, w_out))
    counts = hbm(jnp.transpose(counts, (1, 2, 0)))
    live = pltpu.SMEM(counts.shape, jnp.int32)
    flags = pltpu.SMEM(masks.shape, jnp.int32)

    tiled, first, second, norm = pl.pallas_call(
        functools.partial(gather_kernel, split),
        out_shape=(
            pltpu.VMEM((by, p, width), BF16),
            pltpu.VMEM((split, p, width), BF16),
            pltpu.VMEM((by - split, p, width), BF16),
            pltpu.VMEM((2, width), F32),
        ),
        in_specs=[apart] * 5,
        out_specs=(whole,) * 4,
        scratch_shapes=[
            pltpu.VMEM((by, p, width), BF16),
            pltpu.VMEM(order.shape, jnp.int32),
            live,
            pltpu.SemaphoreType.DMA((by + 4,)),
        ],
        compiler_params=params,
        name="gather",
    )(points, order, counts, hbm(gain[None]), hbm(shift_bias[None]))
    near_pairs = [(i, i ^ 1) for i in range(n) if i ^ 1 < n]
    far_pairs = [(i, i + 1) for i in range(1, n - 1, 2)] + [(i + 1, i) for i in range(1, n - 1, 2)]
    far0 = lax.ppermute(first, "gx", far_pairs)
    far1 = lax.ppermute(second, "gx", far_pairs)
    near = lax.ppermute(tiled, "gx", near_pairs)

    state = (
        pltpu.VMEM((by, 1, groups * lanes), F32),
        pltpu.VMEM((by, hd + 8, groups * lanes), F32),
    )

    def scratch(tiles):
        return [
            pltpu.VMEM((tiles, p, width), BF16),
            pltpu.VMEM((tiles + 1, groups, depth + ONES, p), BF16),
            flags,
            live,
            pltpu.SMEM((3, 8 * by), jnp.int32),
        ]

    qt, top, acc, w_all, w_last = pl.pallas_call(
        functools.partial(main_kernel, n),
        out_shape=(
            pltpu.VMEM((by, groups, depth, lanes), BF16),
            *state,
            pltpu.VMEM(w_qkv.shape, BF16),
            pltpu.VMEM(w_out.shape, BF16),
        ),
        in_specs=[whole, whole, whole, apart, apart, apart, apart],
        out_specs=(whole,) * 5,
        scratch_shapes=[*scratch(2 * by), pltpu.SemaphoreType.DMA((4,))],
        compiler_params=params,
        name="main",
    )(vmem(tiled), vmem(near), vmem(norm), masks, counts, w_qkv, w_out)

    def far(kernel, name, j0, done, block, top, acc, result):
        ins = [block, norm, masks, counts, w_all, qt, top, acc, tiled, w_last, *result]
        spaces = [whole, whole, apart, apart, *(whole,) * 6, *(apart,) * len(result)]
        ins = [vmem(x) if s is whole else x for x, s in zip(ins, spaces)]
        return pl.pallas_call(
            functools.partial(kernel, n, j0, done),
            out_shape=(*state, pltpu.HBM((1, by, bz, p, width), BF16)),
            in_specs=spaces,
            out_specs=(whole, whole, apart),
            scratch_shapes=[
                *scratch(block.shape[0]),
                pltpu.VMEM((max(len(done), 1), p, width), BF16),
                pltpu.SemaphoreType.DMA((2 + by,)),
            ],
            input_output_aliases={6: 0, 7: 1, **({10: 2} if result else {})},
            compiler_params=params,
            name=name,
        )(*ins)

    top, acc, result = far(far_kernel, "far", 0, range(early), far0, top, acc, ())
    _, _, result = far(last_kernel, "last", split, range(early, by), far1, top, acc, (result,))
    return result


def solution(mesh):
    placed = (
        P(("groups", "gx"), None, None, None, None),
        P(("groups", "gx"), None, None, None),
        P(("groups", "gx"), None, None, None),
        P("groups", None, None),
        P(),
        P(),
        P(),
        P(),
    )
    return jax.shard_map(
        functools.partial(shards, mesh.shape["gx"]),
        mesh=mesh,
        in_specs=placed,
        out_specs=P(("groups", "gx"), None, None, None, None),
        check_vma=False,
    )
```

```python
import functools

import jax
import jax.numpy as jnp
from jax import lax
from jax.experimental import pallas as pl
from jax.experimental.pallas import tpu as pltpu
from jax.sharding import PartitionSpec as P

HEADS = 8
NEG = -1e30
ONES = 16
LIMIT = 24 * 1024 * 1024
BF16, F32 = jnp.bfloat16, jnp.float32


def tn(a, b):
    return lax.dot_general(a, b, (((0,), (0,)), ((), ())), preferred_element_type=F32)


def nn(a, b):
    return jnp.dot(a, b, preferred_element_type=F32)


def normalise(tiled, gain, shift):
    values = tiled.astype(F32)
    mean = jnp.mean(values, axis=-1, keepdims=True)
    var = jnp.mean((values - mean) ** 2, axis=-1, keepdims=True)
    return ((values - mean) * lax.rsqrt(var + 1e-05) * gain + shift).astype(BF16)


def gather_kernel(
    split, points, order, counts, gain, shift, tiled, first, second, norm, raw, rows, live, sems
):
    _, by, _, p, width = points.shape
    me = lax.axis_index("gx")
    small = [
        pltpu.make_async_copy(order, rows, sems.at[by]),
        pltpu.make_async_copy(counts, live, sems.at[by + 1]),
        pltpu.make_async_copy(gain, norm.at[0:1], sems.at[by + 2]),
        pltpu.make_async_copy(shift, norm.at[1:2], sems.at[by + 3]),
    ]
    large = [pltpu.make_async_copy(points.at[0, j, 0], raw.at[j], sems.at[j]) for j in range(by)]
    for copy in (*small, *large):
        copy.start()
    slot = lax.broadcasted_iota(jnp.int32, (p, p), 0)
    place = lax.broadcasted_iota(jnp.int32, (1, p), 1)
    small[0].wait()
    small[1].wait()
    picks = []
    for j in range(by):
        row = rows[0, j]
        row = jnp.where(place < live[j, 0, me], row, row[:, :1])
        picks.append((slot == row).astype(F32).astype(BF16))
    for j in range(by):
        large[j].wait()
        got = tn(picks[j], raw[j]).astype(BF16)
        tiled[j] = got
        if j < split:
            first[j] = got
        else:
            second[j - split] = got
    small[2].wait()
    small[3].wait()


def toward_near():
    return 1 - 2 * (lax.axis_index("gx") & 1)


def column(side, b):
    index = 9 * (side + 1) + 3 * (b + 1) + 1
    if isinstance(index, int):
        return index if index < 13 else index - 1
    return jnp.where(index > 13, index - 1, index)


def list_pairs(items, masks, by, sides):
    spare = sum(j1 - j0 for _, _, j0, j1, _, _ in sides)
    pairs, ends = jnp.int32(0), []
    for i in range(by):
        start, found, last = pairs, jnp.int32(0), jnp.int32(0)
        most = 0
        for side, exists, j0, j1, tile0, own in sides:
            for b in (0, -1, 1):
                j = i + b
                if not j0 <= j < j1:
                    continue
                tile = tile0 + j - j0
                items[1, 2 * start + found] = tile
                items[2, 2 * start + found] = tile
                most += 1
                if own and b == 0:
                    found = found + 1
                    last = jnp.int32(tile)
                    continue
                on = masks[0, i, 0, column(side, b)] == 1
                on = on if exists is None else on & exists
                found = found + on.astype(jnp.int32)
                last = jnp.where(on, tile, last)
        items[1, 2 * start + found] = last
        items[2, 2 * start + found] = spare
        for u in range((most + 1) // 2):
            items[0, start + u] = i
        pairs = start + ((found + 1) >> 1)
        ends.append(pairs)
    items[0, pairs] = 0
    for u in range(2):
        items[1, 2 * pairs + u] = 0
    return pairs, ends


def attend(items, high, keys, vals, qt, top, acc, scores, peaks):
    groups, depth, lanes = qt.shape[1:]
    hd, p = depth // 2, lanes // 2

    def score(t, g):
        i, k0, k1 = items[0, t], items[1, 2 * t], items[1, 2 * t + 1]
        rows = slice(g * depth, (g + 1) * depth)
        cols = slice(g * lanes, (g + 1) * lanes)
        s0 = nn(keys[k0, :, rows], qt[i, g])
        s1 = nn(keys[k1, :, rows], qt[i, g])
        scores[:p, cols] = s0
        scores[p:, cols] = s1
        peaks[:, cols] = jnp.max(jnp.maximum(s0, s1), axis=0, keepdims=True)

    def weigh(t, g):
        i, v0, v1 = items[0, t], items[2, 2 * t], items[2, 2 * t + 1]
        cols = slice(g * lanes, (g + 1) * lanes)
        old = top[i, :, cols]
        new = jnp.maximum(old, peaks[:, cols])
        probs = jnp.exp(scores[:, cols] - new).astype(BF16)
        fade = jnp.exp(old - new)
        out = nn(jnp.concatenate([vals[v0, g], vals[v1, g]], axis=1), probs)
        both = jnp.concatenate([out[:hd, :p], out[hd:depth, p:]], axis=1)
        top[i, :, cols] = new
        acc[i, :hd, cols] = acc[i, :hd, cols] * fade + both
        acc[i, hd:, cols] = acc[i, hd:, cols] * fade + out[depth : depth + 8]

    def step(t, carry):
        for g in range(groups):
            weigh(t, g)
            score(t + 1, g)
        return carry

    for g in range(groups):
        score(0, g)
    lax.fori_loop(0, high, step, 0)


def put_values(vals, tile, v, live):
    groups, _, p = vals.shape[1:]
    depth = v.shape[1] // groups
    flag = jnp.broadcast_to(live.astype(F32).astype(BF16), (ONES, p))
    vt = jnp.where(live, v.T, 0.0).astype(BF16)
    for g in range(groups):
        vals[tile, g, :depth] = vt[g * depth : (g + 1) * depth]
        vals[tile, g, depth:] = flag


def finish(i, tiled, acc, w_out, alive):
    hd = acc.shape[1] - 8
    p = tiled.shape[1]
    heads = acc.shape[2] // p
    attn = acc[i, :hd] * (1.0 / acc[i, hd : hd + 1])
    attn = jnp.concatenate([attn[:, h * p : (h + 1) * p] for h in range(heads)], axis=0).astype(BF16)
    mixed = tiled[i].astype(F32) + tn(attn, w_out[...])
    place = lax.broadcasted_iota(jnp.int32, (p, 1), 0)
    return jnp.where(place < alive, mixed, 0.0).astype(BF16)


def main_kernel(
    n, tiled, near, norm, masks, counts, w_qkv, w_out, qt, top, acc, w_all, w_last, keys, vals, flags, live,
    items, scores, peaks, sems
):
    by, p, width = tiled.shape
    groups, depth = qt.shape[1:3]
    hd = depth // 2
    copies = [
        pltpu.make_async_copy(masks, flags, sems.at[0]),
        pltpu.make_async_copy(counts, live, sems.at[1]),
        pltpu.make_async_copy(w_qkv, w_all, sems.at[2]),
        pltpu.make_async_copy(w_out, w_last, sems.at[3]),
    ]
    for copy in copies:
        copy.start()
    me = lax.axis_index("gx")
    side = toward_near()
    partner = me + side
    exists = (partner >= 0) & (partner < n)
    slab = jnp.clip(partner, 0, n - 1)
    place = lax.broadcasted_iota(jnp.int32, (1, p), 1)
    gain, shift = norm[0:1], norm[1:2]
    top[...] = jnp.full_like(top, NEG)
    acc[...] = jnp.zeros_like(acc)
    vals[2 * by] = jnp.zeros(vals.shape[1:], BF16)
    copies[0].wait()
    copies[1].wait()
    pairs, _ = list_pairs(
        items, flags, by, [(0, None, 0, by, 0, True), (side, exists, 0, by, by, False)]
    )
    zeros = jnp.zeros((hd, p), BF16)
    copies[2].wait()
    for c in range(0, by, 2):
        span = range(c, min(c + 2, by))
        x = jnp.concatenate([normalise(tiled[j], gain, shift) for j in span], axis=0)
        q = (nn(x, w_all[:, :width]).astype(BF16) * BF16(1.0 / hd**0.5)).astype(F32)
        k = nn(x, w_all[:, width : 2 * width]).astype(BF16)
        v = nn(x, w_all[:, 2 * width :])
        for u, i in enumerate(span):
            rows = slice(u * p, (u + 1) * p)
            keys[i] = k[rows]
            put_values(vals, i, v[rows], place < live[i, 0, me])
            t = q[rows].T.astype(BF16)
            for g in range(groups):
                mid = g * depth + hd
                qt[i, g, :hd, :p] = t[g * depth : mid]
                qt[i, g, :hd, p:] = zeros
                qt[i, g, hd:, :p] = zeros
                qt[i, g, hd:, p:] = t[mid : mid + hd]
        x = jnp.concatenate([normalise(near[j], gain, shift) for j in span], axis=0)
        k = nn(x, w_all[:, width : 2 * width]).astype(BF16)
        v = nn(x, w_all[:, 2 * width :])
        for u, i in enumerate(span):
            rows = slice(u * p, (u + 1) * p)
            keys[by + i] = k[rows]
            put_values(vals, by + i, v[rows], place < live[i, 0, slab])
    attend(items, pairs, keys, vals, qt, top, acc, scores, peaks)
    copies[3].wait()


def far_work(n, j0, by, rim, norm, masks, counts, w_all, qt, top, acc, keys, vals, flags, live, items, scores, peaks, sems):
    blocks, p, width = rim.shape
    copies = [
        pltpu.make_async_copy(masks, flags, sems.at[0]),
        pltpu.make_async_copy(counts, live, sems.at[1]),
    ]
    for copy in copies:
        copy.start()
    side = -toward_near()
    other = lax.axis_index("gx") + side
    exists = (other >= 0) & (other < n)
    slab = jnp.clip(other, 0, n - 1)
    place = lax.broadcasted_iota(jnp.int32, (1, p), 1)
    gain, shift = norm[0:1], norm[1:2]
    vals[blocks] = jnp.zeros(vals.shape[1:], BF16)
    copies[0].wait()
    copies[1].wait()
    pairs, _ = list_pairs(items, flags, by, [(side, exists, j0, j0 + blocks, 0, False)])
    for c in range(0, blocks, 2):
        span = range(c, min(c + 2, blocks))
        x = jnp.concatenate([normalise(rim[j], gain, shift) for j in span], axis=0)
        k = nn(x, w_all[:, width : 2 * width]).astype(BF16)
        v = nn(x, w_all[:, 2 * width :])
        for u, j in enumerate(span):
            rows = slice(u * p, (u + 1) * p)
            keys[j] = k[rows]
            put_values(vals, j, v[rows], place < live[j0 + j, 0, slab])
    attend(items, pairs, keys, vals, qt, top, acc, scores, peaks)


def hand_out(blocks, tiled, acc, w_out, live, result, out, sems):
    me = lax.axis_index("gx")
    copies = []
    for u, i in enumerate(blocks):
        out[u] = finish(i, tiled, acc, w_out, live[i, 0, me])
        copies.append(pltpu.make_async_copy(out.at[u], result.at[0, i, 0], sems.at[2 + u]))
        copies[-1].start()
    for copy in copies:
        copy.wait()


def far_kernel(
    n, j0, done, rim, norm, masks, counts, w_all, qt, top_in, acc_in, tiled, w_out, top, acc, result, keys, vals,
    flags, live, items, scores, peaks, out, sems
):
    by = tiled.shape[0]
    far_work(n, j0, by, rim, norm, masks, counts, w_all, qt, top, acc, keys, vals, flags, live, items, scores, peaks, sems)
    hand_out(done, tiled, acc, w_out, live, result, out, sems)


def last_kernel(
    n, j0, done, rim, norm, masks, counts, w_all, qt, top_in, acc_in, tiled, w_out, result_in, top, acc, result,
    keys, vals, flags, live, items, scores, peaks, out, sems
):
    by = tiled.shape[0]
    far_work(n, j0, by, rim, norm, masks, counts, w_all, qt, top, acc, keys, vals, flags, live, items, scores, peaks, sems)
    hand_out(done, tiled, acc, w_out, live, result, out, sems)


def vmem(x):
    return pltpu.with_memory_space_constraint(x, pltpu.VMEM)


def hbm(x):
    return pltpu.with_memory_space_constraint(x, pltpu.HBM)


def shards(n, points, order, masks, counts, gain, shift_bias, w_qkv, w_out):
    _, by, bz, p, width = points.shape
    hd = width // HEADS
    groups, depth, lanes = HEADS // 2, 2 * hd, 2 * p
    split = max(by - 2, 1)
    early = max(split - 1, 0)
    whole = pl.BlockSpec(memory_space=pltpu.VMEM)
    apart = pl.BlockSpec(memory_space=pltpu.HBM)
    params = pltpu.CompilerParams(vmem_limit_bytes=LIMIT)
    points, order, masks, w_qkv, w_out = map(hbm, (points, order, masks, w_qkv, w_out))
    counts = hbm(jnp.transpose(counts, (1, 2, 0)))
    live = pltpu.SMEM(counts.shape, jnp.int32)
    flags = pltpu.SMEM(masks.shape, jnp.int32)

    tiled, first, second, norm = pl.pallas_call(
        functools.partial(gather_kernel, split),
        out_shape=(
            pltpu.VMEM((by, p, width), BF16),
            pltpu.VMEM((split, p, width), BF16),
            pltpu.VMEM((by - split, p, width), BF16),
            pltpu.VMEM((2, width), F32),
        ),
        in_specs=[apart] * 5,
        out_specs=(whole,) * 4,
        scratch_shapes=[
            pltpu.VMEM((by, p, width), BF16),
            pltpu.VMEM(order.shape, jnp.int32),
            live,
            pltpu.SemaphoreType.DMA((by + 4,)),
        ],
        compiler_params=params,
        name="gather",
    )(points, order, counts, hbm(gain[None]), hbm(shift_bias[None]))
    near_pairs = [(i, i ^ 1) for i in range(n) if i ^ 1 < n]
    far_pairs = [(i, i + 1) for i in range(1, n - 1, 2)] + [(i + 1, i) for i in range(1, n - 1, 2)]
    far0 = lax.ppermute(first, "gx", far_pairs)
    far1 = lax.ppermute(second, "gx", far_pairs)
    near = lax.ppermute(tiled, "gx", near_pairs)

    state = (
        pltpu.VMEM((by, 1, groups * lanes), F32),
        pltpu.VMEM((by, hd + 8, groups * lanes), F32),
    )

    def scratch(tiles):
        return [
            pltpu.VMEM((tiles, p, width), BF16),
            pltpu.VMEM((tiles + 1, groups, depth + ONES, p), BF16),
            flags,
            live,
            pltpu.SMEM((3, 8 * by), jnp.int32),
            pltpu.VMEM((2 * p, groups * lanes), F32),
            pltpu.VMEM((1, groups * lanes), F32),
        ]

    qt, top, acc, w_all, w_last = pl.pallas_call(
        functools.partial(main_kernel, n),
        out_shape=(
            pltpu.VMEM((by, groups, depth, lanes), BF16),
            *state,
            pltpu.VMEM(w_qkv.shape, BF16),
            pltpu.VMEM(w_out.shape, BF16),
        ),
        in_specs=[whole, whole, whole, apart, apart, apart, apart],
        out_specs=(whole,) * 5,
        scratch_shapes=[*scratch(2 * by), pltpu.SemaphoreType.DMA((4,))],
        compiler_params=params,
        name="main",
    )(vmem(tiled), vmem(near), vmem(norm), masks, counts, w_qkv, w_out)

    def far(kernel, name, j0, done, block, top, acc, result):
        ins = [block, norm, masks, counts, w_all, qt, top, acc, tiled, w_last, *result]
        spaces = [whole, whole, apart, apart, *(whole,) * 6, *(apart,) * len(result)]
        ins = [vmem(x) if s is whole else x for x, s in zip(ins, spaces)]
        return pl.pallas_call(
            functools.partial(kernel, n, j0, done),
            out_shape=(*state, pltpu.HBM((1, by, bz, p, width), BF16)),
            in_specs=spaces,
            out_specs=(whole, whole, apart),
            scratch_shapes=[
                *scratch(block.shape[0]),
                pltpu.VMEM((max(len(done), 1), p, width), BF16),
                pltpu.SemaphoreType.DMA((2 + by,)),
            ],
            input_output_aliases={6: 0, 7: 1, **({10: 2} if result else {})},
            compiler_params=params,
            name=name,
        )(*ins)

    top, acc, result = far(far_kernel, "far", 0, range(early), far0, top, acc, ())
    _, _, result = far(last_kernel, "last", split, range(early, by), far1, top, acc, (result,))
    return result


def solution(mesh):
    placed = (
        P(("groups", "gx"), None, None, None, None),
        P(("groups", "gx"), None, None, None),
        P(("groups", "gx"), None, None, None),
        P("groups", None, None),
        P(),
        P(),
        P(),
        P(),
    )
    return jax.shard_map(
        functools.partial(shards, mesh.shape["gx"]),
        mesh=mesh,
        in_specs=placed,
        out_specs=P(("groups", "gx"), None, None, None, None),
        check_vma=False,
    )
```

```python
import functools

import jax
import jax.numpy as jnp
from jax import lax
from jax.experimental import pallas as pl
from jax.experimental.pallas import tpu as pltpu
from jax.sharding import PartitionSpec as P


HEADS = 8
NEG = -1e30
ONES = 16
LIMIT = 24 * 1024 * 1024
BF16, F32 = jnp.bfloat16, jnp.float32


def tn(a, b):
    return lax.dot_general(a, b, (((0,), (0,)), ((), ())), preferred_element_type=F32)


def nn(a, b):
    return jnp.dot(a, b, preferred_element_type=F32)


def normalise(tiled, gain, shift):
    values = tiled.astype(F32)
    mean = jnp.mean(values, axis=-1, keepdims=True)
    var = jnp.mean((values - mean) ** 2, axis=-1, keepdims=True)
    return ((values - mean) * lax.rsqrt(var + 1e-05) * gain + shift).astype(BF16)


def gather_kernel(
    split, points, order, counts, gain, shift, tiled, first, second, norm, raw, rows, live, sems
):
    _, by, _, p, _ = points.shape
    me = lax.axis_index("gx")
    small = [
        pltpu.make_async_copy(order, rows, sems.at[by]),
        pltpu.make_async_copy(counts, live, sems.at[by + 1]),
        pltpu.make_async_copy(gain, norm.at[0:1], sems.at[by + 2]),
        pltpu.make_async_copy(shift, norm.at[1:2], sems.at[by + 3]),
    ]
    large = [pltpu.make_async_copy(points.at[0, j, 0], raw.at[j], sems.at[j]) for j in range(by)]
    for copy in (*small, *large):
        copy.start()
    slot = lax.broadcasted_iota(jnp.int32, (p, p), 0)
    place = lax.broadcasted_iota(jnp.int32, (1, p), 1)
    small[0].wait()
    small[1].wait()
    picks = []
    for j in range(by):
        row = rows[0, j]
        row = jnp.where(place < live[j, 0, me], row, row[:, :1])
        picks.append((slot == row).astype(F32).astype(BF16))
    for j in range(by):
        large[j].wait()
        got = tn(picks[j], raw[j]).astype(BF16)
        tiled[j] = got
        if j < split:
            first[j] = got
        else:
            second[j - split] = got
    small[2].wait()
    small[3].wait()


def toward_near():
    return 1 - 2 * (lax.axis_index("gx") & 1)


def column(side, b):
    index = 9 * (side + 1) + 3 * (b + 1) + 1
    if isinstance(index, int):
        return index if index < 13 else index - 1
    return jnp.where(index > 13, index - 1, index)


def list_pairs(items, masks, by, sides):
    spare = sum(j1 - j0 for _, _, j0, j1, _, _ in sides)
    pairs, ends = jnp.int32(0), []
    for i in range(by):
        start, found, last = pairs, jnp.int32(0), jnp.int32(0)
        most = 0
        for side, exists, j0, j1, tile0, own in sides:
            for b in (0, -1, 1):
                j = i + b
                if not j0 <= j < j1:
                    continue
                tile = tile0 + j - j0
                items[1, 2 * start + found] = tile
                items[2, 2 * start + found] = tile
                most += 1
                if own and b == 0:
                    found = found + 1
                    last = jnp.int32(tile)
                    continue
                on = masks[0, i, 0, column(side, b)] == 1
                on = on if exists is None else on & exists
                found = found + on.astype(jnp.int32)
                last = jnp.where(on, tile, last)
        items[1, 2 * start + found] = last
        items[2, 2 * start + found] = spare
        for u in range((most + 1) // 2):
            items[0, start + u] = i
        pairs = start + ((found + 1) >> 1)
        ends.append(pairs)
    items[0, pairs] = 0
    for u in range(2):
        items[1, 2 * pairs + u] = 0
    return pairs, ends


def attend(items, high, keys, vals, qt, top, acc, scores, peaks):
    groups, depth, lanes = qt.shape[1:]
    hd, p = depth // 2, lanes // 2

    def score(t, g):
        i, k0, k1 = items[0, t], items[1, 2 * t], items[1, 2 * t + 1]
        rows = slice(g * depth, (g + 1) * depth)
        cols = slice(g * lanes, (g + 1) * lanes)
        s0 = nn(keys[k0, :, rows], qt[i, g])
        s1 = nn(keys[k1, :, rows], qt[i, g])
        scores[:p, cols] = s0
        scores[p:, cols] = s1
        peaks[:, cols] = jnp.max(jnp.maximum(s0, s1), axis=0, keepdims=True)

    def weigh(t, g):
        i, v0, v1 = items[0, t], items[2, 2 * t], items[2, 2 * t + 1]
        cols = slice(g * lanes, (g + 1) * lanes)
        old = top[i, :, cols]
        new = jnp.maximum(old, peaks[:, cols])
        probs = jnp.exp(scores[:, cols] - new).astype(BF16)
        fade = jnp.exp(old - new)
        out = nn(jnp.concatenate([vals[v0, g], vals[v1, g]], axis=1), probs)
        both = jnp.concatenate([out[:hd, :p], out[hd:depth, p:]], axis=1)
        top[i, :, cols] = new
        acc[i, :hd, cols] = acc[i, :hd, cols] * fade + both
        acc[i, hd:, cols] = acc[i, hd:, cols] * fade + out[depth : depth + 8]

    def step(t, carry):
        for g in range(groups):
            weigh(t, g)
            score(t + 1, g)
        return carry

    for g in range(groups):
        score(0, g)
    lax.fori_loop(0, high, step, 0)


def put_values(vals, tile, v, live):
    groups, _, p = vals.shape[1:]
    depth = v.shape[1] // groups
    flag = jnp.broadcast_to(live.astype(F32).astype(BF16), (ONES, p))
    vt = jnp.where(live, v.T, 0.0).astype(BF16)
    for g in range(groups):
        vals[tile, g, :depth] = vt[g * depth : (g + 1) * depth]
        vals[tile, g, depth:] = flag


def finish(i, tiled, acc, w_out, alive):
    hd = acc.shape[1] - 8
    p = tiled.shape[1]
    heads = acc.shape[2] // p
    attn = acc[i, :hd] * (1.0 / acc[i, hd : hd + 1])
    attn = jnp.concatenate([attn[:, h * p : (h + 1) * p] for h in range(heads)], axis=0).astype(BF16)
    mixed = tiled[i].astype(F32) + tn(attn, w_out[...])
    place = lax.broadcasted_iota(jnp.int32, (p, 1), 0)
    return jnp.where(place < alive, mixed, 0.0).astype(BF16)


def main_kernel(
    n, split, tiled, near, norm, masks, counts, w_qkv, w_out, qt, top, acc, w_all, w_last, plan0, plan1, keys, vals,
    items, flags, live, scores, peaks, sems
):
    by, p, width = tiled.shape
    groups, depth = qt.shape[1:3]
    hd = depth // 2
    copies = [
        pltpu.make_async_copy(masks, flags, sems.at[0]),
        pltpu.make_async_copy(counts, live, sems.at[1]),
        pltpu.make_async_copy(w_qkv, w_all, sems.at[2]),
        pltpu.make_async_copy(w_out, w_last, sems.at[3]),
    ]
    for copy in copies:
        copy.start()
    me = lax.axis_index("gx")
    side = toward_near()
    partner = me + side
    exists = (partner >= 0) & (partner < n)
    slab = jnp.clip(partner, 0, n - 1)
    place = lax.broadcasted_iota(jnp.int32, (1, p), 1)
    gain, shift = norm[0:1], norm[1:2]
    top[...] = jnp.full_like(top, NEG)
    acc[...] = jnp.zeros_like(acc)
    vals[2 * by] = jnp.zeros(vals.shape[1:], BF16)
    copies[0].wait()
    copies[1].wait()
    pairs, _ = list_pairs(
        items, flags, by, [(0, None, 0, by, 0, True), (side, exists, 0, by, by, False)]
    )
    other = me - side
    there = (other >= 0) & (other < n)
    beyond = jnp.clip(other, 0, n - 1)
    for plan, j0, j1 in ((plan0, 0, split), (plan1, split, by)):
        plan[3, 0], _ = list_pairs(plan, flags, by, [(-side, there, j0, j1, 0, False)])
        for i in range(by):
            plan[3, 1 + i] = live[i, 0, me]
        for j in range(j0, j1):
            plan[3, 1 + by + j - j0] = live[j, 0, beyond]
    zeros = jnp.zeros((hd, p), BF16)
    copies[2].wait()
    for c in range(0, by, 2):
        span = range(c, min(c + 2, by))
        x = jnp.concatenate([normalise(tiled[j], gain, shift) for j in span], axis=0)
        q = (nn(x, w_all[:, :width]).astype(BF16) * BF16(1.0 / hd**0.5)).astype(F32)
        k = nn(x, w_all[:, width : 2 * width]).astype(BF16)
        v = nn(x, w_all[:, 2 * width :])
        for u, i in enumerate(span):
            rows = slice(u * p, (u + 1) * p)
            keys[i] = k[rows]
            put_values(vals, i, v[rows], place < live[i, 0, me])
            t = q[rows].T.astype(BF16)
            for g in range(groups):
                mid = g * depth + hd
                qt[i, g, :hd, :p] = t[g * depth : mid]
                qt[i, g, :hd, p:] = zeros
                qt[i, g, hd:, :p] = zeros
                qt[i, g, hd:, p:] = t[mid : mid + hd]
        x = jnp.concatenate([normalise(near[j], gain, shift) for j in span], axis=0)
        k = nn(x, w_all[:, width : 2 * width]).astype(BF16)
        v = nn(x, w_all[:, 2 * width :])
        for u, i in enumerate(span):
            rows = slice(u * p, (u + 1) * p)
            keys[by + i] = k[rows]
            put_values(vals, by + i, v[rows], place < live[i, 0, slab])
    attend(items, pairs, keys, vals, qt, top, acc, scores, peaks)
    copies[3].wait()


def far_work(rim, norm, w_all, qt, plan, top, acc, keys, vals, scores, peaks):
    by = qt.shape[0]
    blocks, p, width = rim.shape
    place = lax.broadcasted_iota(jnp.int32, (1, p), 1)
    gain, shift = norm[0:1], norm[1:2]
    vals[blocks] = jnp.zeros(vals.shape[1:], BF16)
    for c in range(0, blocks, 2):
        span = range(c, min(c + 2, blocks))
        x = jnp.concatenate([normalise(rim[j], gain, shift) for j in span], axis=0)
        k = nn(x, w_all[:, width : 2 * width]).astype(BF16)
        v = nn(x, w_all[:, 2 * width :])
        for u, j in enumerate(span):
            rows = slice(u * p, (u + 1) * p)
            keys[j] = k[rows]
            put_values(vals, j, v[rows], place < plan[3, 1 + by + j])
    attend(plan, plan[3, 0], keys, vals, qt, top, acc, scores, peaks)


def hand_out(blocks, tiled, acc, w_out, plan, result, out, sems):
    copies = []
    for u, i in enumerate(blocks):
        out[u] = finish(i, tiled, acc, w_out, plan[3, 1 + i])
        copies.append(pltpu.make_async_copy(out.at[u], result.at[0, i, 0], sems.at[u]))
        copies[-1].start()
    for copy in copies:
        copy.wait()


def far_kernel(
    done, rim, norm, w_all, qt, top_in, acc_in, tiled, w_out, plan, top, acc, result, keys, vals, scores, peaks, out,
    sems
):
    far_work(rim, norm, w_all, qt, plan, top, acc, keys, vals, scores, peaks)
    hand_out(done, tiled, acc, w_out, plan, result, out, sems)


def last_kernel(
    done, rim, norm, w_all, qt, top_in, acc_in, tiled, w_out, plan, result_in, top, acc, result, keys, vals, scores,
    peaks, out, sems
):
    far_work(rim, norm, w_all, qt, plan, top, acc, keys, vals, scores, peaks)
    hand_out(done, tiled, acc, w_out, plan, result, out, sems)


def vmem(x):
    return pltpu.with_memory_space_constraint(x, pltpu.VMEM)


def smem(x):
    return pltpu.with_memory_space_constraint(x, pltpu.SMEM)


def hbm(x):
    return pltpu.with_memory_space_constraint(x, pltpu.HBM)


def shards(n, points, order, masks, counts, gain, shift_bias, w_qkv, w_out):
    _, by, bz, p, width = points.shape
    hd = width // HEADS
    groups, depth, lanes = HEADS // 2, 2 * hd, 2 * p
    split = max(by - 2, 1)
    early = max(split - 1, 0)
    whole = pl.BlockSpec(memory_space=pltpu.VMEM)
    apart = pl.BlockSpec(memory_space=pltpu.HBM)
    words = pl.BlockSpec(memory_space=pltpu.SMEM)
    plan = pltpu.SMEM((4, 8 * by), jnp.int32)
    params = pltpu.CompilerParams(vmem_limit_bytes=LIMIT)
    points, order, masks, w_qkv, w_out = map(hbm, (points, order, masks, w_qkv, w_out))
    counts = hbm(jnp.transpose(counts, (1, 2, 0)))
    live = pltpu.SMEM(counts.shape, jnp.int32)
    flags = pltpu.SMEM(masks.shape, jnp.int32)

    tiled, first, second, norm = pl.pallas_call(
        functools.partial(gather_kernel, split),
        out_shape=(
            pltpu.VMEM((by, p, width), BF16),
            pltpu.VMEM((split, p, width), BF16),
            pltpu.VMEM((by - split, p, width), BF16),
            pltpu.VMEM((2, width), F32),
        ),
        in_specs=[apart] * 5,
        out_specs=(whole,) * 4,
        scratch_shapes=[
            pltpu.VMEM((by, p, width), BF16),
            pltpu.VMEM(order.shape, jnp.int32),
            live,
            pltpu.SemaphoreType.DMA((by + 4,)),
        ],
        compiler_params=params,
        name="gather",
    )(points, order, counts, hbm(gain[None]), hbm(shift_bias[None]))
    near_pairs = [(i, i ^ 1) for i in range(n) if i ^ 1 < n]
    far_pairs = [(i, i + 1) for i in range(1, n - 1, 2)] + [(i + 1, i) for i in range(1, n - 1, 2)]

    def moved(value, pairs):
        return lax.ppermute(value, "gx", pairs)

    far0 = moved(first, far_pairs)
    near = moved(tiled, near_pairs)
    far1 = moved(second, far_pairs)

    state = (
        pltpu.VMEM((by, 1, groups * lanes), F32),
        pltpu.VMEM((by, hd + 8, groups * lanes), F32),
    )

    def scratch(tiles):
        return [
            pltpu.VMEM((tiles, p, width), BF16),
            pltpu.VMEM((tiles + 1, groups, depth + ONES, p), BF16),
        ]

    ahead = [
        pltpu.VMEM((2 * p, groups * lanes), F32),
        pltpu.VMEM((1, groups * lanes), F32),
    ]
    qt, top, acc, w_all, w_last, plan0, plan1 = pl.pallas_call(
        functools.partial(main_kernel, n, split),
        out_shape=(
            pltpu.VMEM((by, groups, depth, lanes), BF16),
            *state,
            pltpu.VMEM(w_qkv.shape, BF16),
            pltpu.VMEM(w_out.shape, BF16),
            plan,
            plan,
        ),
        in_specs=[whole, whole, whole, apart, apart, apart, apart],
        out_specs=(whole,) * 5 + (words,) * 2,
        scratch_shapes=[*scratch(2 * by), plan, flags, live, *ahead, pltpu.SemaphoreType.DMA((4,))],
        compiler_params=params,
        name="main",
    )(vmem(tiled), vmem(near), vmem(norm), masks, counts, w_qkv, w_out)

    def far(kernel, done, block, plan, top, acc, result):
        ins = [block, norm, w_all, qt, top, acc, tiled, w_last]
        return pl.pallas_call(
            functools.partial(kernel, done),
            out_shape=(*state, pltpu.HBM((1, by, bz, p, width), BF16)),
            in_specs=[*(whole,) * len(ins), words, *(apart,) * len(result)],
            out_specs=(whole, whole, apart),
            scratch_shapes=[
                *scratch(block.shape[0]),
                *ahead,
                pltpu.VMEM((max(len(done), 1), p, width), BF16),
                pltpu.SemaphoreType.DMA((by,)),
            ],
            input_output_aliases={4: 0, 5: 1, **({9: 2} if result else {})},
            compiler_params=params,
        )(*map(vmem, ins), smem(plan), *result)

    top, acc, result = far(far_kernel, range(early), far0, plan0, top, acc, ())
    _, _, result = far(last_kernel, range(early, by), far1, plan1, top, acc, (result,))
    return result


def solution(mesh):
    placed = (
        P(("groups", "gx"), None, None, None, None),
        P(("groups", "gx"), None, None, None),
        P(("groups", "gx"), None, None, None),
        P("groups", None, None),
        P(),
        P(),
        P(),
        P(),
    )
    return jax.shard_map(
        functools.partial(shards, mesh.shape["gx"]),
        mesh=mesh,
        in_specs=placed,
        out_specs=P(("groups", "gx"), None, None, None, None),
        check_vma=False,
    )
```

```python
import functools

import jax
import jax.numpy as jnp
from jax import lax
from jax.experimental import pallas as pl
from jax.experimental.pallas import tpu as pltpu
from jax.sharding import PartitionSpec as P


HEADS = 8
NEG = -1e30
ONES = 16
LIMIT = 24 * 1024 * 1024
BF16, F32 = jnp.bfloat16, jnp.float32


def tn(a, b):
    return lax.dot_general(a, b, (((0,), (0,)), ((), ())), preferred_element_type=F32)


def nn(a, b):
    return jnp.dot(a, b, preferred_element_type=F32)


def normalise(tiled, gain, shift):
    values = tiled.astype(F32)
    mean = jnp.mean(values, axis=-1, keepdims=True)
    var = jnp.mean((values - mean) ** 2, axis=-1, keepdims=True)
    return ((values - mean) * lax.rsqrt(var + 1e-05) * gain + shift).astype(BF16)


def gather_kernel(
    split, points, order, counts, gain, shift, tiled, first, second, norm, raw, rows, live, sems
):
    _, by, _, p, _ = points.shape
    me = lax.axis_index("gx")
    small = [
        pltpu.make_async_copy(order, rows, sems.at[by]),
        pltpu.make_async_copy(counts, live, sems.at[by + 1]),
        pltpu.make_async_copy(gain, norm.at[0:1], sems.at[by + 2]),
        pltpu.make_async_copy(shift, norm.at[1:2], sems.at[by + 3]),
    ]
    large = [pltpu.make_async_copy(points.at[0, j, 0], raw.at[j], sems.at[j]) for j in range(by)]
    for copy in (*small, *large):
        copy.start()
    slot = lax.broadcasted_iota(jnp.int32, (p, p), 0)
    place = lax.broadcasted_iota(jnp.int32, (1, p), 1)
    small[0].wait()
    small[1].wait()
    picks = []
    for j in range(by):
        row = rows[0, j]
        row = jnp.where(place < live[j, 0, me], row, row[:, :1])
        picks.append((slot == row).astype(F32).astype(BF16))
    for j in range(by):
        large[j].wait()
        got = tn(picks[j], raw[j]).astype(BF16)
        tiled[j] = got
        if j < split:
            first[j] = got
        else:
            second[j - split] = got
    small[2].wait()
    small[3].wait()


def toward_near():
    return 1 - 2 * (lax.axis_index("gx") & 1)


def column(side, b):
    index = 9 * (side + 1) + 3 * (b + 1) + 1
    if isinstance(index, int):
        return index if index < 13 else index - 1
    return jnp.where(index > 13, index - 1, index)


def list_pairs(items, masks, by, sides):
    spare = sum(j1 - j0 for _, _, j0, j1, _, _ in sides)
    pairs, ends = jnp.int32(0), []
    for i in range(by):
        start, found, last = pairs, jnp.int32(0), jnp.int32(0)
        most = 0
        for side, exists, j0, j1, tile0, own in sides:
            for b in (0, -1, 1):
                j = i + b
                if not j0 <= j < j1:
                    continue
                tile = tile0 + j - j0
                items[1, 2 * start + found] = tile
                items[2, 2 * start + found] = tile
                most += 1
                if own and b == 0:
                    found = found + 1
                    last = jnp.int32(tile)
                    continue
                on = masks[0, i, 0, column(side, b)] == 1
                on = on if exists is None else on & exists
                found = found + on.astype(jnp.int32)
                last = jnp.where(on, tile, last)
        items[1, 2 * start + found] = last
        items[2, 2 * start + found] = spare
        for u in range((most + 1) // 2):
            items[0, start + u] = i
        pairs = start + ((found + 1) >> 1)
        ends.append(pairs)
    items[0, pairs] = 0
    for u in range(2):
        items[1, 2 * pairs + u] = 0
    return pairs, ends


def attend(items, high, keys, vals, qt, top, acc, scores, peaks):
    groups, depth, lanes = qt.shape[1:]
    hd, p = depth // 2, lanes // 2

    def score(t, g):
        i, k0, k1 = items[0, t], items[1, 2 * t], items[1, 2 * t + 1]
        rows = slice(g * depth, (g + 1) * depth)
        cols = slice(g * lanes, (g + 1) * lanes)
        s0 = nn(keys[k0, :, rows], qt[i, g])
        s1 = nn(keys[k1, :, rows], qt[i, g])
        scores[:p, cols] = s0
        scores[p:, cols] = s1
        peaks[:, cols] = jnp.max(jnp.maximum(s0, s1), axis=0, keepdims=True)

    def weigh(t, g):
        i, v0, v1 = items[0, t], items[2, 2 * t], items[2, 2 * t + 1]
        cols = slice(g * lanes, (g + 1) * lanes)
        old = top[i, :, cols]
        new = jnp.maximum(old, peaks[:, cols])
        probs = jnp.exp(scores[:, cols] - new).astype(BF16)
        fade = jnp.exp(old - new)
        out = nn(jnp.concatenate([vals[v0, g], vals[v1, g]], axis=1), probs)
        both = jnp.concatenate([out[:hd, :p], out[hd:depth, p:]], axis=1)
        top[i, :, cols] = new
        acc[i, :hd, cols] = acc[i, :hd, cols] * fade + both
        acc[i, hd:, cols] = acc[i, hd:, cols] * fade + out[depth : depth + 8]

    def step(t, carry):
        for g in range(groups):
            weigh(t, g)
            score(t + 1, g)
        return carry

    for g in range(groups):
        score(0, g)
    lax.fori_loop(0, high, step, 0)


def put_values(vals, tile, v, live):
    groups, _, p = vals.shape[1:]
    depth = v.shape[1] // groups
    flag = jnp.broadcast_to(live.astype(F32).astype(BF16), (ONES, p))
    vt = jnp.where(live, v.T, 0.0).astype(BF16)
    for g in range(groups):
        vals[tile, g, :depth] = vt[g * depth : (g + 1) * depth]
        vals[tile, g, depth:] = flag


def finish(i, tiled, acc, w_out, alive):
    hd = acc.shape[1] - 8
    p = tiled.shape[1]
    heads = acc.shape[2] // p
    attn = acc[i, :hd] * (1.0 / acc[i, hd : hd + 1])
    attn = jnp.concatenate([attn[:, h * p : (h + 1) * p] for h in range(heads)], axis=0).astype(BF16)
    mixed = tiled[i].astype(F32) + tn(attn, w_out[...])
    place = lax.broadcasted_iota(jnp.int32, (p, 1), 0)
    return jnp.where(place < alive, mixed, 0.0).astype(BF16)


def main_kernel(
    n, split, tiled, near, norm, masks, counts, w_qkv, w_out, qt, top, acc, w_all, w_last, plan0, plan1, keys, vals,
    items, flags, live, scores, peaks, sems
):
    by, p, width = tiled.shape
    groups, depth = qt.shape[1:3]
    hd = depth // 2
    copies = [
        pltpu.make_async_copy(masks, flags, sems.at[0]),
        pltpu.make_async_copy(counts, live, sems.at[1]),
        pltpu.make_async_copy(w_qkv, w_all, sems.at[2]),
        pltpu.make_async_copy(w_out, w_last, sems.at[3]),
    ]
    for copy in copies:
        copy.start()
    me = lax.axis_index("gx")
    side = toward_near()
    partner = me + side
    exists = (partner >= 0) & (partner < n)
    slab = jnp.clip(partner, 0, n - 1)
    place = lax.broadcasted_iota(jnp.int32, (1, p), 1)
    gain, shift = norm[0:1], norm[1:2]
    top[...] = jnp.full_like(top, NEG)
    acc[...] = jnp.zeros_like(acc)
    vals[2 * by] = jnp.zeros(vals.shape[1:], BF16)
    copies[0].wait()
    copies[1].wait()
    pairs, _ = list_pairs(
        items, flags, by, [(0, None, 0, by, 0, True), (side, exists, 0, by, by, False)]
    )
    other = me - side
    there = (other >= 0) & (other < n)
    beyond = jnp.clip(other, 0, n - 1)
    for plan, j0, j1 in ((plan0, 0, split), (plan1, split, by)):
        plan[3, 0], _ = list_pairs(plan, flags, by, [(-side, there, j0, j1, 0, False)])
        for i in range(by):
            plan[3, 1 + i] = live[i, 0, me]
        for j in range(j0, j1):
            plan[3, 1 + by + j - j0] = live[j, 0, beyond]
    zeros = jnp.zeros((hd, p), BF16)
    copies[2].wait()
    for c in range(0, by, 2):
        span = range(c, min(c + 2, by))
        x = jnp.concatenate([normalise(tiled[j], gain, shift) for j in span], axis=0)
        q = (nn(x, w_all[:, :width]).astype(BF16) * BF16(1.0 / hd**0.5)).astype(F32)
        k = nn(x, w_all[:, width : 2 * width]).astype(BF16)
        v = nn(x, w_all[:, 2 * width :])
        for u, i in enumerate(span):
            rows = slice(u * p, (u + 1) * p)
            keys[i] = k[rows]
            put_values(vals, i, v[rows], place < live[i, 0, me])
            t = q[rows].T.astype(BF16)
            for g in range(groups):
                mid = g * depth + hd
                qt[i, g, :hd, :p] = t[g * depth : mid]
                qt[i, g, :hd, p:] = zeros
                qt[i, g, hd:, :p] = zeros
                qt[i, g, hd:, p:] = t[mid : mid + hd]
        x = jnp.concatenate([normalise(near[j], gain, shift) for j in span], axis=0)
        k = nn(x, w_all[:, width : 2 * width]).astype(BF16)
        v = nn(x, w_all[:, 2 * width :])
        for u, i in enumerate(span):
            rows = slice(u * p, (u + 1) * p)
            keys[by + i] = k[rows]
            put_values(vals, by + i, v[rows], place < live[i, 0, slab])
    attend(items, pairs, keys, vals, qt, top, acc, scores, peaks)
    copies[3].wait()


def far_work(rim, norm, w_all, qt, plan, top, acc, keys, vals, scores, peaks):
    by = qt.shape[0]
    blocks, p, width = rim.shape
    place = lax.broadcasted_iota(jnp.int32, (1, p), 1)
    gain, shift = norm[0:1], norm[1:2]
    vals[blocks] = jnp.zeros(vals.shape[1:], BF16)
    for c in range(0, blocks, 2):
        span = range(c, min(c + 2, blocks))
        x = jnp.concatenate([normalise(rim[j], gain, shift) for j in span], axis=0)
        k = nn(x, w_all[:, width : 2 * width]).astype(BF16)
        v = nn(x, w_all[:, 2 * width :])
        for u, j in enumerate(span):
            rows = slice(u * p, (u + 1) * p)
            keys[j] = k[rows]
            put_values(vals, j, v[rows], place < plan[3, 1 + by + j])
    attend(plan, plan[3, 0], keys, vals, qt, top, acc, scores, peaks)


def hand_out(blocks, tiled, acc, w_out, plan, result, out, sems):
    copies = []
    for u, i in enumerate(blocks):
        out[u] = finish(i, tiled, acc, w_out, plan[3, 1 + i])
        copies.append(pltpu.make_async_copy(out.at[u], result.at[0, i, 0], sems.at[u]))
        copies[-1].start()
    for copy in copies:
        copy.wait()


def far_kernel(
    done, rim, norm, w_all, qt, top_in, acc_in, tiled, w_out, plan, top, acc, result, keys, vals, scores, peaks, out,
    sems
):
    far_work(rim, norm, w_all, qt, plan, top, acc, keys, vals, scores, peaks)
    hand_out(done, tiled, acc, w_out, plan, result, out, sems)


def last_kernel(
    done, rim, norm, w_all, qt, top_in, acc_in, tiled, w_out, plan, result_in, top, acc, result, keys, vals, scores,
    peaks, out, sems
):
    far_work(rim, norm, w_all, qt, plan, top, acc, keys, vals, scores, peaks)
    hand_out(done, tiled, acc, w_out, plan, result, out, sems)


def vmem(x):
    return pltpu.with_memory_space_constraint(x, pltpu.VMEM)


def smem(x):
    return pltpu.with_memory_space_constraint(x, pltpu.SMEM)


def hbm(x):
    return pltpu.with_memory_space_constraint(x, pltpu.HBM)


def shards(n, points, order, masks, counts, gain, shift_bias, w_qkv, w_out):
    _, by, bz, p, width = points.shape
    hd = width // HEADS
    groups, depth, lanes = HEADS // 2, 2 * hd, 2 * p
    split = max(by - 2, 1)
    early = max(split - 1, 0)
    whole = pl.BlockSpec(memory_space=pltpu.VMEM)
    apart = pl.BlockSpec(memory_space=pltpu.HBM)
    words = pl.BlockSpec(memory_space=pltpu.SMEM)
    plan = pltpu.SMEM((4, 8 * by), jnp.int32)
    params = pltpu.CompilerParams(vmem_limit_bytes=LIMIT)
    points, order, masks, w_qkv, w_out = map(hbm, (points, order, masks, w_qkv, w_out))
    counts = hbm(jnp.transpose(counts, (1, 2, 0)))
    live = pltpu.SMEM(counts.shape, jnp.int32)
    flags = pltpu.SMEM(masks.shape, jnp.int32)

    tiled, first, second, norm = pl.pallas_call(
        functools.partial(gather_kernel, split),
        out_shape=(
            pltpu.VMEM((by, p, width), BF16),
            pltpu.VMEM((split, p, width), BF16),
            pltpu.VMEM((by - split, p, width), BF16),
            pltpu.VMEM((2, width), F32),
        ),
        in_specs=[apart] * 5,
        out_specs=(whole,) * 4,
        scratch_shapes=[
            pltpu.VMEM((by, p, width), BF16),
            pltpu.VMEM(order.shape, jnp.int32),
            live,
            pltpu.SemaphoreType.DMA((by + 4,)),
        ],
        compiler_params=params,
        name="gather",
    )(points, order, counts, hbm(gain[None]), hbm(shift_bias[None]))
    near_pairs = [(i, i ^ 1) for i in range(n) if i ^ 1 < n]
    far_pairs = [(i, i + 1) for i in range(1, n - 1, 2)] + [(i + 1, i) for i in range(1, n - 1, 2)]

    def moved(value, pairs):
        return lax.ppermute(value, "gx", pairs)

    far0 = moved(first, far_pairs)
    near = moved(tiled, near_pairs)
    far1 = moved(second, far_pairs)

    state = (
        pltpu.VMEM((by, 1, groups * lanes), F32),
        pltpu.VMEM((by, hd + 8, groups * lanes), F32),
    )

    def scratch(tiles):
        return [
            pltpu.VMEM((tiles, p, width), BF16),
            pltpu.VMEM((tiles + 1, groups, depth + ONES, p), BF16),
        ]

    ahead = [
        pltpu.VMEM((2 * p, groups * lanes), F32),
        pltpu.VMEM((1, groups * lanes), F32),
    ]
    main = pl.pallas_call(
        functools.partial(main_kernel, n, split),
        out_shape=(
            pltpu.VMEM((by, groups, depth, lanes), BF16),
            *state,
            pltpu.VMEM(w_qkv.shape, BF16),
            pltpu.VMEM(w_out.shape, BF16),
            plan,
            plan,
        ),
        in_specs=[whole, whole, whole, apart, apart, apart, apart],
        out_specs=(whole,) * 5 + (words,) * 2,
        scratch_shapes=[*scratch(2 * by), plan, flags, live, *ahead, pltpu.SemaphoreType.DMA((4,))],
        compiler_params=params,
        name="main",
    )
    qt, top, acc, w_all, w_last, plan0, plan1 = main(vmem(tiled), vmem(near), vmem(norm), masks, counts, w_qkv, w_out)

    def far(kernel, done, block, plan, top, acc, result):
        ins = [block, norm, w_all, qt, top, acc, tiled, w_last]
        return pl.pallas_call(
            functools.partial(kernel, done),
            out_shape=(*state, pltpu.HBM((1, by, bz, p, width), BF16)),
            in_specs=[*(whole,) * len(ins), words, *(apart,) * len(result)],
            out_specs=(whole, whole, apart),
            scratch_shapes=[
                *scratch(block.shape[0]),
                *ahead,
                pltpu.VMEM((max(len(done), 1), p, width), BF16),
                pltpu.SemaphoreType.DMA((by,)),
            ],
            input_output_aliases={4: 0, 5: 1, **({9: 2} if result else {})},
            compiler_params=params,
        )(*map(vmem, ins), smem(plan), *result)

    top, acc, result = far(far_kernel, range(early), far0, plan0, top, acc, ())
    _, _, result = far(last_kernel, range(early, by), far1, plan1, top, acc, (result,))
    return result


def solution(mesh):
    placed = (
        P(("groups", "gx"), None, None, None, None),
        P(("groups", "gx"), None, None, None),
        P(("groups", "gx"), None, None, None),
        P("groups", None, None),
        P(),
        P(),
        P(),
        P(),
    )
    return jax.shard_map(
        functools.partial(shards, mesh.shape["gx"]),
        mesh=mesh,
        in_specs=placed,
        out_specs=P(("groups", "gx"), None, None, None, None),
        check_vma=False,
    )
```

```python
import functools

import jax
import jax.numpy as jnp
from jax import lax
from jax.experimental import pallas as pl
from jax.experimental.pallas import tpu as pltpu
from jax.sharding import PartitionSpec as P


HEADS = 8
NEG = -1e30
ONES = 16
LIMIT = 24 * 1024 * 1024
BF16, F32 = jnp.bfloat16, jnp.float32


def tn(a, b):
    return lax.dot_general(a, b, (((0,), (0,)), ((), ())), preferred_element_type=F32)


def nn(a, b):
    return jnp.dot(a, b, preferred_element_type=F32)


def normalise(tiled, gain, shift):
    values = tiled.astype(F32)
    mean = jnp.mean(values, axis=-1, keepdims=True)
    var = jnp.mean((values - mean) ** 2, axis=-1, keepdims=True)
    return ((values - mean) * lax.rsqrt(var + 1e-05) * gain + shift).astype(BF16)


def select(row, raw):
    p = raw.shape[0]
    slot = lax.broadcasted_iota(jnp.int32, (p, p), 0)
    return tn((slot == row).astype(F32).astype(BF16), raw).astype(BF16)


def gather_kernel(points, order, counts, gain, shift, first, rest, places, norm, raw, rows, live, sems):
    _, by, _, p, _ = points.shape
    split = first.shape[0]
    me = lax.axis_index("gx")
    small = [
        pltpu.make_async_copy(order, rows, sems.at[by]),
        pltpu.make_async_copy(counts, live, sems.at[by + 1]),
        pltpu.make_async_copy(gain, norm.at[0:1], sems.at[by + 2]),
        pltpu.make_async_copy(shift, norm.at[1:2], sems.at[by + 3]),
    ]
    large = [
        pltpu.make_async_copy(
            points.at[0, j, 0], raw.at[j] if j < split else rest.at[j - split], sems.at[j]
        )
        for j in range(by)
    ]
    for copy in (*small[:2], *large, *small[2:]):
        copy.start()
    place = lax.broadcasted_iota(jnp.int32, (1, p), 1)
    small[0].wait()
    small[1].wait()
    picks = []
    for j in range(by):
        row = rows[0, j]
        picks.append(jnp.where(place < live[j, 0, me], row, row[:, :1]))
        if j >= split:
            places[j - split] = picks[j]
    for j in range(split):
        large[j].wait()
    for j in range(split):
        first[j] = select(picks[j], raw[j])
    for copy in (*large[split:], *small[2:]):
        copy.wait()


def rest_kernel(first, rest, places, tiled, second):
    split = first.shape[0]
    for j in range(split):
        tiled[j] = first[j]
    for j in range(rest.shape[0]):
        got = select(places[j], rest[j])
        second[j] = got
        tiled[split + j] = got


def toward_near():
    return 1 - 2 * (lax.axis_index("gx") & 1)


def column(side, b):
    index = 9 * (side + 1) + 3 * (b + 1) + 1
    if isinstance(index, int):
        return index if index < 13 else index - 1
    return jnp.where(index > 13, index - 1, index)


def list_pairs(items, masks, by, sides):
    spare = sum(j1 - j0 for _, _, j0, j1, _, _ in sides)
    pairs, ends = jnp.int32(0), []
    for i in range(by):
        start, found, last = pairs, jnp.int32(0), jnp.int32(0)
        most = 0
        for side, exists, j0, j1, tile0, own in sides:
            for b in (0, -1, 1):
                j = i + b
                if not j0 <= j < j1:
                    continue
                tile = tile0 + j - j0
                items[1, 2 * start + found] = tile
                items[2, 2 * start + found] = tile
                most += 1
                if own and b == 0:
                    found = found + 1
                    last = jnp.int32(tile)
                    continue
                on = masks[0, i, 0, column(side, b)] == 1
                on = on if exists is None else on & exists
                found = found + on.astype(jnp.int32)
                last = jnp.where(on, tile, last)
        items[1, 2 * start + found] = last
        items[2, 2 * start + found] = spare
        for u in range((most + 1) // 2):
            items[0, start + u] = i
        pairs = start + ((found + 1) >> 1)
        ends.append(pairs)
    items[0, pairs] = 0
    for u in range(2):
        items[1, 2 * pairs + u] = 0
    return pairs, ends


def attend(items, high, keys, vals, qt, top, acc, scores, peaks):
    groups, depth, lanes = qt.shape[1:]
    hd, p = depth // 2, lanes // 2

    def score(t, g):
        i, k0, k1 = items[0, t], items[1, 2 * t], items[1, 2 * t + 1]
        rows = slice(g * depth, (g + 1) * depth)
        cols = slice(g * lanes, (g + 1) * lanes)
        s0 = nn(keys[k0, :, rows], qt[i, g])
        s1 = nn(keys[k1, :, rows], qt[i, g])
        scores[:p, cols] = s0
        scores[p:, cols] = s1
        peaks[:, cols] = jnp.max(jnp.maximum(s0, s1), axis=0, keepdims=True)

    def weigh(t, g):
        i, v0, v1 = items[0, t], items[2, 2 * t], items[2, 2 * t + 1]
        cols = slice(g * lanes, (g + 1) * lanes)
        old = top[i, :, cols]
        new = jnp.maximum(old, peaks[:, cols])
        probs = jnp.exp(scores[:, cols] - new).astype(BF16)
        fade = jnp.exp(old - new)
        both, sums = [], []
        for h in range(2):
            rows = slice(h * (hd + ONES), (h + 1) * (hd + ONES))
            val = jnp.concatenate([vals[v0, g, rows], vals[v1, g, rows]], axis=1)
            out = nn(val, probs[:, h * p : (h + 1) * p])
            both.append(out[:hd])
            sums.append(out[hd : hd + 8])
        return cols, new, fade, jnp.concatenate(both, axis=1), jnp.concatenate(sums, axis=1)

    lead = groups // 2

    def step(t, carry):
        made = []
        for g in range(0, groups, lead):
            for u in range(g, g + lead):
                score(t + (u + lead) // groups, (u + lead) % groups)
            for u in range(g, g + lead):
                made.append(weigh(t, u))
        i = items[0, t]
        for cols, new, fade, both, sums in made:
            top[i, :, cols] = new
            acc[i, :hd, cols] = acc[i, :hd, cols] * fade + both
            acc[i, hd:, cols] = acc[i, hd:, cols] * fade + sums
        return carry

    for g in range(lead):
        score(0, g)
    lax.fori_loop(0, high, step, 0)


def put_values(vals, tile, g0, v, live):
    p = vals.shape[3]
    hd = vals.shape[2] // 2 - ONES
    flag = jnp.broadcast_to(live.astype(F32).astype(BF16), (ONES, p))
    vt = jnp.where(live, v.T, 0.0).astype(BF16)
    for h in range(v.shape[1] // hd):
        g, r = g0 + h // 2, h % 2 * (hd + ONES)
        vals[tile, g, r : r + hd] = vt[h * hd : (h + 1) * hd]
        vals[tile, g, r + hd : r + hd + ONES] = flag


def put_blocks(tile0, x, w_all, keys, vals, lives):
    p, width = keys.shape[1:]
    wide = min(256, width)
    groups = vals.shape[1]
    for c in range(0, width, wide):
        k = nn(x, w_all[:, width + c : width + c + wide]).astype(BF16)
        v = nn(x, w_all[:, 2 * width + c : 2 * width + c + wide])
        for u, live in enumerate(lives):
            rows = slice(u * p, (u + 1) * p)
            keys[tile0 + u, :, c : c + wide] = k[rows]
            put_values(vals, tile0 + u, c * groups // width, v[rows], live)


def finish(i, tiled, acc, w_out, alive):
    hd = acc.shape[1] - 8
    p = tiled.shape[1]
    heads = acc.shape[2] // p
    attn = acc[i, :hd] * (1.0 / acc[i, hd : hd + 1])
    attn = jnp.concatenate([attn[:, h * p : (h + 1) * p] for h in range(heads)], axis=0).astype(BF16)
    mixed = tiled[i].astype(F32) + tn(attn, w_out[...])
    place = lax.broadcasted_iota(jnp.int32, (p, 1), 0)
    return jnp.where(place < alive, mixed, 0.0).astype(BF16)


def main_kernel(
    n, split, tiled, near, norm, masks, counts, w_qkv, w_out, qt, top, acc, w_all, w_last, plan0, plan1, keys, vals, nrm,
    items, flags, live, scores, peaks, sems
):
    by, p, width = tiled.shape
    _, depth = qt.shape[1:3]
    hd = depth // 2
    copies = [
        pltpu.make_async_copy(masks, flags, sems.at[0]),
        pltpu.make_async_copy(counts, live, sems.at[1]),
        pltpu.make_async_copy(w_qkv, w_all, sems.at[2]),
        pltpu.make_async_copy(w_out, w_last, sems.at[3]),
    ]
    for copy in copies:
        copy.start()
    me = lax.axis_index("gx")
    side = toward_near()
    partner = me + side
    exists = (partner >= 0) & (partner < n)
    slab = jnp.clip(partner, 0, n - 1)
    place = lax.broadcasted_iota(jnp.int32, (1, p), 1)
    gain, shift = norm[0:1], norm[1:2]
    top[...] = jnp.full_like(top, NEG)
    acc[...] = jnp.zeros_like(acc)
    vals[2 * by] = jnp.zeros(vals.shape[1:], BF16)
    copies[0].wait()
    copies[1].wait()
    pairs, _ = list_pairs(
        items, flags, by, [(0, None, 0, by, 0, True), (side, exists, 0, by, by, False)]
    )
    other = me - side
    there = (other >= 0) & (other < n)
    beyond = jnp.clip(other, 0, n - 1)
    for plan, j0, j1 in ((plan0, 0, split), (plan1, split, by)):
        plan[3, 0], _ = list_pairs(plan, flags, by, [(-side, there, j0, j1, 0, False)])
        for i in range(by):
            plan[3, 1 + i] = live[i, 0, me]
        for j in range(j0, j1):
            plan[3, 1 + by + j - j0] = live[j, 0, beyond]
    zeros = jnp.zeros((hd, p), BF16)
    for j in range(by):
        nrm[j * p : (j + 1) * p] = normalise(tiled[j], gain, shift)
    copies[2].wait()
    wide = min(256, width)
    for c in range(0, width, wide):
        q = (nn(nrm[: by * p], w_all[:, c : c + wide]).astype(BF16) * BF16(1.0 / hd**0.5)).astype(F32)
        for i in range(by):
            t = q[i * p : (i + 1) * p].T.astype(BF16)
            for u in range(wide // depth):
                g, mid = c // depth + u, u * depth + hd
                qt[i, g, :hd, :p] = t[mid - hd : mid]
                qt[i, g, :hd, p:] = zeros
                qt[i, g, hd:, :p] = zeros
                qt[i, g, hd:, p:] = t[mid : mid + hd]
    for j in range(by):
        nrm[(by + j) * p : (by + j + 1) * p] = normalise(near[j], gain, shift)
    put_blocks(0, nrm[: by * p], w_all, keys, vals, [place < live[i, 0, me] for i in range(by)])
    put_blocks(by, nrm[by * p :], w_all, keys, vals, [place < live[i, 0, slab] for i in range(by)])
    attend(items, pairs, keys, vals, qt, top, acc, scores, peaks)
    copies[3].wait()


def far_work(rim, norm, w_all, qt, plan, top, acc, keys, vals, nrm, scores, peaks):
    by = qt.shape[0]
    blocks, p, _ = rim.shape
    place = lax.broadcasted_iota(jnp.int32, (1, p), 1)
    vals[blocks] = jnp.zeros(vals.shape[1:], BF16)
    for j in range(blocks):
        nrm[j * p : (j + 1) * p] = normalise(rim[j], norm[0:1], norm[1:2])
    put_blocks(0, nrm[...], w_all, keys, vals, [place < plan[3, 1 + by + j] for j in range(blocks)])
    attend(plan, plan[3, 0], keys, vals, qt, top, acc, scores, peaks)


def far_kernel(
    rim, norm, w_all, qt, top_in, acc_in, tiled, w_out, plan, top, acc, held, keys, vals, nrm, scores, peaks
):
    far_work(rim, norm, w_all, qt, plan, top, acc, keys, vals, nrm, scores, peaks)
    for i in range(held.shape[0]):
        held[i] = finish(i, tiled, acc, w_out, plan[3, 1 + i])


def last_kernel(
    rim, norm, w_all, qt, top_in, acc_in, tiled, w_out, held, plan, top, acc, result, keys, vals, nrm, scores, peaks,
    out, sems
):
    by, early = tiled.shape[0], held.shape[0]
    copies = [pltpu.make_async_copy(held.at[i], result.at[0, i, 0], sems.at[i]) for i in range(early)]
    for copy in copies:
        copy.start()
    far_work(rim, norm, w_all, qt, plan, top, acc, keys, vals, nrm, scores, peaks)
    for i in range(early, by):
        out[i - early] = finish(i, tiled, acc, w_out, plan[3, 1 + i])
        copies.append(pltpu.make_async_copy(out.at[i - early], result.at[0, i, 0], sems.at[i]))
        copies[-1].start()
    for copy in copies:
        copy.wait()


def vmem(x):
    return pltpu.with_memory_space_constraint(x, pltpu.VMEM)


def smem(x):
    return pltpu.with_memory_space_constraint(x, pltpu.SMEM)


def hbm(x):
    return pltpu.with_memory_space_constraint(x, pltpu.HBM)


def shards(n, points, order, masks, counts, gain, shift_bias, w_qkv, w_out):
    _, by, bz, p, width = points.shape
    hd = width // HEADS
    groups, depth, lanes = HEADS // 2, 2 * hd, 2 * p
    split = max(by // 2, 1)
    early = max(split - 1, 1)
    whole = pl.BlockSpec(memory_space=pltpu.VMEM)
    apart = pl.BlockSpec(memory_space=pltpu.HBM)
    words = pl.BlockSpec(memory_space=pltpu.SMEM)
    plan = pltpu.SMEM((4, 8 * by), jnp.int32)
    params = pltpu.CompilerParams(vmem_limit_bytes=LIMIT)
    points, order, masks, w_qkv, w_out = map(hbm, (points, order, masks, w_qkv, w_out))
    counts = hbm(jnp.transpose(counts, (1, 2, 0)))
    live = pltpu.SMEM(counts.shape, jnp.int32)
    flags = pltpu.SMEM(masks.shape, jnp.int32)

    first, rest, places, norm = pl.pallas_call(
        gather_kernel,
        out_shape=(
            pltpu.VMEM((split, p, width), BF16),
            pltpu.VMEM((by - split, p, width), BF16),
            pltpu.VMEM((by - split, 1, p), jnp.int32),
            pltpu.VMEM((2, width), F32),
        ),
        in_specs=[apart] * 5,
        out_specs=(whole,) * 4,
        scratch_shapes=[
            pltpu.VMEM((split, p, width), BF16),
            pltpu.VMEM(order.shape, jnp.int32),
            live,
            pltpu.SemaphoreType.DMA((by + 4,)),
        ],
        compiler_params=params,
        name="gather",
    )(points, order, counts, hbm(gain[None]), hbm(shift_bias[None]))
    tile_rest = pl.pallas_call(
        rest_kernel,
        out_shape=(pltpu.VMEM((by, p, width), BF16), pltpu.VMEM((by - split, p, width), BF16)),
        in_specs=[whole] * 3,
        out_specs=(whole,) * 2,
        compiler_params=params,
        name="rest",
    )
    tiled, second = tile_rest(vmem(first), vmem(rest), vmem(places))
    near_pairs = [(i, i ^ 1) for i in range(n) if i ^ 1 < n]
    far_pairs = [(i, i + 1) for i in range(1, n - 1, 2)] + [(i + 1, i) for i in range(1, n - 1, 2)]

    def moved(value, pairs):
        return lax.ppermute(value, "gx", pairs)

    far0 = moved(first, far_pairs)
    near = moved(tiled, near_pairs)
    far1 = moved(second, far_pairs)

    state = (
        pltpu.VMEM((by, 1, groups * lanes), F32),
        pltpu.VMEM((by, hd + 8, groups * lanes), F32),
    )

    def scratch(tiles):
        return [
            pltpu.VMEM((tiles, p, width), BF16),
            pltpu.VMEM((tiles + 1, groups, depth + 2 * ONES, p), BF16),
            pltpu.VMEM((tiles * p, width), BF16),
        ]

    ahead = [
        pltpu.VMEM((2 * p, groups * lanes), F32),
        pltpu.VMEM((1, groups * lanes), F32),
    ]
    qt, top, acc, w_all, w_last, plan0, plan1 = pl.pallas_call(
        functools.partial(main_kernel, n, split),
        out_shape=(
            pltpu.VMEM((by, groups, depth, lanes), BF16),
            *state,
            pltpu.VMEM(w_qkv.shape, BF16),
            pltpu.VMEM(w_out.shape, BF16),
            plan,
            plan,
        ),
        in_specs=[whole, whole, whole, apart, apart, apart, apart],
        out_specs=(whole,) * 5 + (words,) * 2,
        scratch_shapes=[*scratch(2 * by), plan, flags, live, *ahead, pltpu.SemaphoreType.DMA((4,))],
        compiler_params=params,
        name="main",
    )(vmem(tiled), vmem(near), vmem(norm), masks, counts, w_qkv, w_out)

    ins = [far0, norm, w_all, qt, top, acc, tiled, w_last]
    top, acc, held = pl.pallas_call(
        far_kernel,
        out_shape=(*state, pltpu.VMEM((early, p, width), BF16)),
        in_specs=[*(whole,) * len(ins), words],
        out_specs=(whole,) * 3,
        scratch_shapes=[*scratch(split), *ahead],
        input_output_aliases={4: 0, 5: 1},
        compiler_params=params,
        name="far",
    )(*map(vmem, ins), smem(plan0))
    ins = [far1, norm, w_all, qt, top, acc, tiled, w_last, held]
    _, _, result = pl.pallas_call(
        last_kernel,
        out_shape=(*state, pltpu.HBM((1, by, bz, p, width), BF16)),
        in_specs=[*(whole,) * len(ins), words],
        out_specs=(whole, whole, apart),
        scratch_shapes=[
            *scratch(by - split),
            *ahead,
            pltpu.VMEM((by - early, p, width), BF16),
            pltpu.SemaphoreType.DMA((by,)),
        ],
        input_output_aliases={4: 0, 5: 1},
        compiler_params=params,
        name="last",
    )(*map(vmem, ins), smem(plan1))
    return result


def solution(mesh):
    placed = (
        P(("groups", "gx"), None, None, None, None),
        P(("groups", "gx"), None, None, None),
        P(("groups", "gx"), None, None, None),
        P("groups", None, None),
        P(),
        P(),
        P(),
        P(),
    )
    return jax.shard_map(
        functools.partial(shards, mesh.shape["gx"]),
        mesh=mesh,
        in_specs=placed,
        out_specs=P(("groups", "gx"), None, None, None, None),
        check_vma=False,
    )
```

```python
import functools

import jax
import jax.numpy as jnp
from jax import lax
from jax.experimental import pallas as pl
from jax.experimental.pallas import tpu as pltpu
from jax.sharding import PartitionSpec as P


HEADS = 8
NEG = -1e30
ONES = 16
LIMIT = 24 * 1024 * 1024
BF16, F32 = jnp.bfloat16, jnp.float32


def tn(a, b):
    return lax.dot_general(a, b, (((0,), (0,)), ((), ())), preferred_element_type=F32)


def nn(a, b):
    return jnp.dot(a, b, preferred_element_type=F32)


def normalise(tiled, gain, shift):
    values = tiled.astype(F32)
    mean = jnp.mean(values, axis=-1, keepdims=True)
    var = jnp.mean((values - mean) ** 2, axis=-1, keepdims=True)
    return ((values - mean) * lax.rsqrt(var + 1e-05) * gain + shift).astype(BF16)


def select(row, raw):
    p = raw.shape[0]
    slot = lax.broadcasted_iota(jnp.int32, (p, p), 0)
    return tn((slot == row).astype(F32).astype(BF16), raw).astype(BF16)


def gather_kernel(points, order, counts, gain, shift, first, rest, places, norm, raw, rows, live, sems):
    _, by, _, p, _ = points.shape
    split = first.shape[0]
    me = lax.axis_index("gx")
    small = [
        pltpu.make_async_copy(order, rows, sems.at[by]),
        pltpu.make_async_copy(counts, live, sems.at[by + 1]),
        pltpu.make_async_copy(gain, norm.at[0:1], sems.at[by + 2]),
        pltpu.make_async_copy(shift, norm.at[1:2], sems.at[by + 3]),
    ]
    large = [
        pltpu.make_async_copy(
            points.at[0, j, 0], raw.at[j] if j < split else rest.at[j - split], sems.at[j]
        )
        for j in range(by)
    ]
    for copy in (*small[:2], *large, *small[2:]):
        copy.start()
    place = lax.broadcasted_iota(jnp.int32, (1, p), 1)
    small[0].wait()
    small[1].wait()
    picks = []
    for j in range(by):
        row = rows[0, j]
        picks.append(jnp.where(place < live[j, 0, me], row, row[:, :1]))
        if j >= split:
            places[j - split] = picks[j]
    for j in range(split):
        large[j].wait()
    for j in range(split):
        first[j] = select(picks[j], raw[j])
    for copy in (*large[split:], *small[2:]):
        copy.wait()


def rest_kernel(first, rest, places, norm, tiled, normed, second):
    split = first.shape[0]
    gain, shift = norm[0:1], norm[1:2]
    for j in range(rest.shape[0]):
        got = select(places[j], rest[j])
        tiled[split + j] = got
        got = normalise(got, gain, shift)
        second[j] = got
        normed[split + j] = got
    for j in range(split):
        got = first[j]
        tiled[j] = got
        normed[j] = normalise(got, gain, shift)


def toward_near():
    return 1 - 2 * (lax.axis_index("gx") & 1)


def column(side, b):
    index = 9 * (side + 1) + 3 * (b + 1) + 1
    if isinstance(index, int):
        return index if index < 13 else index - 1
    return jnp.where(index > 13, index - 1, index)


def list_pairs(items, masks, by, sides):
    spare = sum(j1 - j0 for _, _, j0, j1, _, _ in sides)
    pairs, ends = jnp.int32(0), []
    for i in range(by):
        start, found, last = pairs, jnp.int32(0), jnp.int32(0)
        most = 0
        for side, exists, j0, j1, tile0, own in sides:
            for b in (0, -1, 1):
                j = i + b
                if not j0 <= j < j1:
                    continue
                tile = tile0 + j - j0
                items[1, 2 * start + found] = tile
                items[2, 2 * start + found] = tile
                most += 1
                if own and b == 0:
                    found = found + 1
                    last = jnp.int32(tile)
                    continue
                on = masks[0, i, 0, column(side, b)] == 1
                on = on if exists is None else on & exists
                found = found + on.astype(jnp.int32)
                last = jnp.where(on, tile, last)
        items[1, 2 * start + found] = last
        items[2, 2 * start + found] = spare
        for u in range((most + 1) // 2):
            items[0, start + u] = i
        pairs = start + ((found + 1) >> 1)
        ends.append(pairs)
    items[0, pairs] = 0
    for u in range(2):
        items[1, 2 * pairs + u] = 0
    return pairs, ends


def attend(items, high, keys, vals, qt, top, acc, scores, peaks):
    groups, depth, lanes = qt.shape[1:]
    hd, p = depth // 2, lanes // 2

    def score(t, g):
        i, k0, k1 = items[0, t], items[1, 2 * t], items[1, 2 * t + 1]
        rows = slice(g * depth, (g + 1) * depth)
        cols = slice(g * lanes, (g + 1) * lanes)
        s0 = nn(keys[k0, :, rows], qt[i, g])
        s1 = nn(keys[k1, :, rows], qt[i, g])
        scores[:p, cols] = s0
        scores[p:, cols] = s1
        peaks[:, cols] = jnp.max(jnp.maximum(s0, s1), axis=0, keepdims=True)

    def weigh(t, g):
        i, v0, v1 = items[0, t], items[2, 2 * t], items[2, 2 * t + 1]
        cols = slice(g * lanes, (g + 1) * lanes)
        old = top[i, :, cols]
        new = jnp.maximum(old, peaks[:, cols])
        probs = jnp.exp(scores[:, cols] - new).astype(BF16)
        fade = jnp.exp(old - new)
        both, sums = [], []
        for h in range(2):
            rows = slice(h * (hd + ONES), (h + 1) * (hd + ONES))
            val = jnp.concatenate([vals[v0, g, rows], vals[v1, g, rows]], axis=1)
            out = nn(val, probs[:, h * p : (h + 1) * p])
            both.append(out[:hd])
            sums.append(out[hd : hd + 8])
        return cols, new, fade, jnp.concatenate(both, axis=1), jnp.concatenate(sums, axis=1)

    lead = groups // 2

    def step(t, carry):
        made = []
        for g in range(0, groups, lead):
            for u in range(g, g + lead):
                score(t + (u + lead) // groups, (u + lead) % groups)
            for u in range(g, g + lead):
                made.append(weigh(t, u))
        i = items[0, t]
        for cols, new, fade, both, sums in made:
            top[i, :, cols] = new
            acc[i, :hd, cols] = acc[i, :hd, cols] * fade + both
            acc[i, hd:, cols] = acc[i, hd:, cols] * fade + sums
        return carry

    for g in range(lead):
        score(0, g)
    lax.fori_loop(0, high, step, 0)


def put_values(vals, tile, g0, v, live):
    p = vals.shape[3]
    hd = vals.shape[2] // 2 - ONES
    flag = jnp.broadcast_to(live.astype(F32).astype(BF16), (ONES, p))
    vt = jnp.where(live, v.T, 0.0).astype(BF16)
    for h in range(v.shape[1] // hd):
        g, r = g0 + h // 2, h % 2 * (hd + ONES)
        vals[tile, g, r : r + hd] = vt[h * hd : (h + 1) * hd]
        vals[tile, g, r + hd : r + hd + ONES] = flag


def put_blocks(tile0, x, w_all, keys, vals, lives):
    p, width = keys.shape[1:]
    wide = min(256, width)
    groups = vals.shape[1]
    for c in range(0, width, wide):
        k = nn(x, w_all[:, width + c : width + c + wide]).astype(BF16)
        v = nn(x, w_all[:, 2 * width + c : 2 * width + c + wide])
        for u, live in enumerate(lives):
            rows = slice(u * p, (u + 1) * p)
            keys[tile0 + u, :, c : c + wide] = k[rows]
            put_values(vals, tile0 + u, c * groups // width, v[rows], live)


def finish(i, tiled, acc, w_out, alive):
    hd = acc.shape[1] - 8
    p = tiled.shape[1]
    heads = acc.shape[2] // p
    attn = acc[i, :hd] * (1.0 / acc[i, hd : hd + 1])
    attn = jnp.concatenate([attn[:, h * p : (h + 1) * p] for h in range(heads)], axis=0).astype(BF16)
    mixed = tiled[i].astype(F32) + tn(attn, w_out[...])
    place = lax.broadcasted_iota(jnp.int32, (p, 1), 0)
    return jnp.where(place < alive, mixed, 0.0).astype(BF16)


def main_kernel(
    n, split, own, near, masks, counts, w_qkv, w_out, qt, top, acc, w_all, w_last, plan0, plan1, keys, vals,
    items, flags, live, scores, peaks, sems
):
    by, p, width = own.shape
    _, depth = qt.shape[1:3]
    hd = depth // 2
    copies = [
        pltpu.make_async_copy(masks, flags, sems.at[0]),
        pltpu.make_async_copy(counts, live, sems.at[1]),
        pltpu.make_async_copy(w_qkv, w_all, sems.at[2]),
        pltpu.make_async_copy(w_out, w_last, sems.at[3]),
    ]
    for copy in copies:
        copy.start()
    me = lax.axis_index("gx")
    side = toward_near()
    partner = me + side
    exists = (partner >= 0) & (partner < n)
    slab = jnp.clip(partner, 0, n - 1)
    place = lax.broadcasted_iota(jnp.int32, (1, p), 1)
    top[...] = jnp.full_like(top, NEG)
    acc[...] = jnp.zeros_like(acc)
    vals[2 * by] = jnp.zeros(vals.shape[1:], BF16)
    copies[0].wait()
    copies[1].wait()
    pairs, _ = list_pairs(
        items, flags, by, [(0, None, 0, by, 0, True), (side, exists, 0, by, by, False)]
    )
    other = me - side
    there = (other >= 0) & (other < n)
    beyond = jnp.clip(other, 0, n - 1)
    for plan, j0, j1 in ((plan0, 0, split), (plan1, split, by)):
        plan[3, 0], _ = list_pairs(plan, flags, by, [(-side, there, j0, j1, 0, False)])
        for i in range(by):
            plan[3, 1 + i] = live[i, 0, me]
        for j in range(j0, j1):
            plan[3, 1 + by + j - j0] = live[j, 0, beyond]
    zeros = jnp.zeros((hd, p), BF16)
    copies[2].wait()
    mine, theirs = own[...].reshape(by * p, width), near[...].reshape(by * p, width)
    wide = min(256, width)
    for c in range(0, width, wide):
        q = (nn(mine, w_all[:, c : c + wide]).astype(BF16) * BF16(1.0 / hd**0.5)).astype(F32)
        for i in range(by):
            t = q[i * p : (i + 1) * p].T.astype(BF16)
            for u in range(wide // depth):
                g, mid = c // depth + u, u * depth + hd
                qt[i, g, :hd, :p] = t[mid - hd : mid]
                qt[i, g, :hd, p:] = zeros
                qt[i, g, hd:, :p] = zeros
                qt[i, g, hd:, p:] = t[mid : mid + hd]
    put_blocks(0, mine, w_all, keys, vals, [place < live[i, 0, me] for i in range(by)])
    put_blocks(by, theirs, w_all, keys, vals, [place < live[i, 0, slab] for i in range(by)])
    attend(items, pairs, keys, vals, qt, top, acc, scores, peaks)
    copies[3].wait()


def far_work(rim, w_all, qt, plan, top, acc, keys, vals, scores, peaks):
    by = qt.shape[0]
    blocks, p, width = rim.shape
    place = lax.broadcasted_iota(jnp.int32, (1, p), 1)
    vals[blocks] = jnp.zeros(vals.shape[1:], BF16)
    put_blocks(0, rim[...].reshape(blocks * p, width), w_all, keys, vals, [place < plan[3, 1 + by + j] for j in range(blocks)])
    attend(plan, plan[3, 0], keys, vals, qt, top, acc, scores, peaks)


def far_kernel(
    rim, norm, w_all, qt, top_in, acc_in, tiled, w_out, plan, top, acc, held, keys, vals, scores, peaks, nrm
):
    for j in range(rim.shape[0]):
        nrm[j] = normalise(rim[j], norm[0:1], norm[1:2])
    far_work(nrm, w_all, qt, plan, top, acc, keys, vals, scores, peaks)
    for i in range(held.shape[0]):
        held[i] = finish(i, tiled, acc, w_out, plan[3, 1 + i])


def last_kernel(
    rim, w_all, qt, top_in, acc_in, tiled, w_out, held, plan, top, acc, result, keys, vals, scores, peaks, out,
    sems
):
    by, early = tiled.shape[0], held.shape[0]
    copies = [pltpu.make_async_copy(held.at[i], result.at[0, i, 0], sems.at[i]) for i in range(early)]
    for copy in copies:
        copy.start()
    far_work(rim, w_all, qt, plan, top, acc, keys, vals, scores, peaks)
    for i in range(early, by):
        out[i - early] = finish(i, tiled, acc, w_out, plan[3, 1 + i])
        copies.append(pltpu.make_async_copy(out.at[i - early], result.at[0, i, 0], sems.at[i]))
        copies[-1].start()
    for copy in copies:
        copy.wait()


def vmem(x):
    return pltpu.with_memory_space_constraint(x, pltpu.VMEM)


def smem(x):
    return pltpu.with_memory_space_constraint(x, pltpu.SMEM)


def hbm(x):
    return pltpu.with_memory_space_constraint(x, pltpu.HBM)


def shards(n, points, order, masks, counts, gain, shift_bias, w_qkv, w_out):
    _, by, bz, p, width = points.shape
    hd = width // HEADS
    groups, depth, lanes = HEADS // 2, 2 * hd, 2 * p
    split = max(by // 2, 1)
    early = max(split - 1, 1)
    whole = pl.BlockSpec(memory_space=pltpu.VMEM)
    apart = pl.BlockSpec(memory_space=pltpu.HBM)
    words = pl.BlockSpec(memory_space=pltpu.SMEM)
    plan = pltpu.SMEM((4, 8 * by), jnp.int32)
    params = pltpu.CompilerParams(vmem_limit_bytes=LIMIT)
    points, order, masks, w_qkv, w_out = map(hbm, (points, order, masks, w_qkv, w_out))
    counts = hbm(jnp.transpose(counts, (1, 2, 0)))
    live = pltpu.SMEM(counts.shape, jnp.int32)
    flags = pltpu.SMEM(masks.shape, jnp.int32)

    first, rest, places, norm = pl.pallas_call(
        gather_kernel,
        out_shape=(
            pltpu.VMEM((split, p, width), BF16),
            pltpu.VMEM((by - split, p, width), BF16),
            pltpu.VMEM((by - split, 1, p), jnp.int32),
            pltpu.VMEM((2, width), F32),
        ),
        in_specs=[apart] * 5,
        out_specs=(whole,) * 4,
        scratch_shapes=[
            pltpu.VMEM((split, p, width), BF16),
            pltpu.VMEM(order.shape, jnp.int32),
            live,
            pltpu.SemaphoreType.DMA((by + 4,)),
        ],
        compiler_params=params,
        name="gather",
    )(points, order, counts, hbm(gain[None]), hbm(shift_bias[None]))
    tile_rest = pl.pallas_call(
        rest_kernel,
        out_shape=(
            pltpu.VMEM((by, p, width), BF16),
            pltpu.VMEM((by, p, width), BF16),
            pltpu.VMEM((by - split, p, width), BF16),
        ),
        in_specs=[whole] * 4,
        out_specs=(whole,) * 3,
        compiler_params=params,
        name="rest",
    )
    tiled, normed, second = tile_rest(vmem(first), vmem(rest), vmem(places), vmem(norm))
    near_pairs = [(i, i ^ 1) for i in range(n) if i ^ 1 < n]
    far_pairs = [(i, i + 1) for i in range(1, n - 1, 2)] + [(i + 1, i) for i in range(1, n - 1, 2)]

    def moved(value, pairs):
        return lax.ppermute(value, "gx", pairs)

    far0 = moved(first, far_pairs)
    near = moved(normed, near_pairs)
    far1 = moved(second, far_pairs)

    state = (
        pltpu.VMEM((by, 1, groups * lanes), F32),
        pltpu.VMEM((by, hd + 8, groups * lanes), F32),
    )

    def scratch(tiles):
        return [
            pltpu.VMEM((tiles, p, width), BF16),
            pltpu.VMEM((tiles + 1, groups, depth + 2 * ONES, p), BF16),
        ]

    ahead = [
        pltpu.VMEM((2 * p, groups * lanes), F32),
        pltpu.VMEM((1, groups * lanes), F32),
    ]
    qt, top, acc, w_all, w_last, plan0, plan1 = pl.pallas_call(
        functools.partial(main_kernel, n, split),
        out_shape=(
            pltpu.VMEM((by, groups, depth, lanes), BF16),
            *state,
            pltpu.VMEM(w_qkv.shape, BF16),
            pltpu.VMEM(w_out.shape, BF16),
            plan,
            plan,
        ),
        in_specs=[whole, whole, apart, apart, apart, apart],
        out_specs=(whole,) * 5 + (words,) * 2,
        scratch_shapes=[*scratch(2 * by), plan, flags, live, *ahead, pltpu.SemaphoreType.DMA((4,))],
        compiler_params=params,
        name="main",
    )(vmem(normed), vmem(near), masks, counts, w_qkv, w_out)

    ins = [far0, norm, w_all, qt, top, acc, tiled, w_last]
    top, acc, held = pl.pallas_call(
        far_kernel,
        out_shape=(*state, pltpu.VMEM((early, p, width), BF16)),
        in_specs=[*(whole,) * len(ins), words],
        out_specs=(whole,) * 3,
        scratch_shapes=[*scratch(split), *ahead, pltpu.VMEM((split, p, width), BF16)],
        input_output_aliases={4: 0, 5: 1},
        compiler_params=params,
        name="far",
    )(*map(vmem, ins), smem(plan0))
    ins = [far1, w_all, qt, top, acc, tiled, w_last, held]
    _, _, result = pl.pallas_call(
        last_kernel,
        out_shape=(*state, pltpu.HBM((1, by, bz, p, width), BF16)),
        in_specs=[*(whole,) * len(ins), words],
        out_specs=(whole, whole, apart),
        scratch_shapes=[
            *scratch(by - split),
            *ahead,
            pltpu.VMEM((by - early, p, width), BF16),
            pltpu.SemaphoreType.DMA((by,)),
        ],
        input_output_aliases={3: 0, 4: 1},
        compiler_params=params,
        name="last",
    )(*map(vmem, ins), smem(plan1))
    return result


def solution(mesh):
    placed = (
        P(("groups", "gx"), None, None, None, None),
        P(("groups", "gx"), None, None, None),
        P(("groups", "gx"), None, None, None),
        P("groups", None, None),
        P(),
        P(),
        P(),
        P(),
    )
    return jax.shard_map(
        functools.partial(shards, mesh.shape["gx"]),
        mesh=mesh,
        in_specs=placed,
        out_specs=P(("groups", "gx"), None, None, None, None),
        check_vma=False,
    )
```

```python
import functools

import jax
import jax.numpy as jnp
from jax import lax
from jax.experimental import pallas as pl
from jax.experimental.pallas import tpu as pltpu
from jax.sharding import PartitionSpec as P


HEADS = 8
NEG = -1e30
ONES = 16
LIMIT = 24 * 1024 * 1024
BF16, F32 = jnp.bfloat16, jnp.float32


def tn(a, b):
    return lax.dot_general(a, b, (((0,), (0,)), ((), ())), preferred_element_type=F32)


def nn(a, b):
    return jnp.dot(a, b, preferred_element_type=F32)


def normalise(tiled, gain, shift):
    values = tiled.astype(F32)
    mean = jnp.mean(values, axis=-1, keepdims=True)
    var = jnp.mean((values - mean) ** 2, axis=-1, keepdims=True)
    return ((values - mean) * lax.rsqrt(var + 1e-05) * gain + shift).astype(BF16)


def select(row, raw):
    p = raw.shape[0]
    slot = lax.broadcasted_iota(jnp.int32, (p, p), 0)
    return tn((slot == row).astype(F32).astype(BF16), raw).astype(BF16)


def gather_kernel(points, order, counts, gain, shift, first, rest, places, norm, raw, rows, live, sems):
    _, by, _, p, _ = points.shape
    split = first.shape[0]
    me = lax.axis_index("gx")
    small = [
        pltpu.make_async_copy(order, rows, sems.at[by]),
        pltpu.make_async_copy(counts, live, sems.at[by + 1]),
        pltpu.make_async_copy(gain, norm.at[0:1], sems.at[by + 2]),
        pltpu.make_async_copy(shift, norm.at[1:2], sems.at[by + 3]),
    ]
    large = [
        pltpu.make_async_copy(
            points.at[0, j, 0], raw.at[j] if j < split else rest.at[j - split], sems.at[j]
        )
        for j in range(by)
    ]
    for copy in (*small[:2], *large, *small[2:]):
        copy.start()
    place = lax.broadcasted_iota(jnp.int32, (1, p), 1)
    small[0].wait()
    small[1].wait()
    picks = []
    for j in range(by):
        row = rows[0, j]
        picks.append(jnp.where(place < live[j, 0, me], row, row[:, :1]))
        if j >= split:
            places[j - split] = picks[j]
    for j in range(split):
        large[j].wait()
    for j in range(split):
        first[j] = select(picks[j], raw[j])
    for copy in (*large[split:], *small[2:]):
        copy.wait()


def rest_kernel(first, rest, places, norm, tiled, normed, second):
    split = first.shape[0]
    gain, shift = norm[0:1], norm[1:2]
    for j in range(rest.shape[0]):
        got = select(places[j], rest[j])
        tiled[split + j] = got
        got = normalise(got, gain, shift)
        second[j] = got
        normed[split + j] = got
    for j in range(split):
        got = first[j]
        tiled[j] = got
        normed[j] = normalise(got, gain, shift)


def toward_near():
    return 1 - 2 * (lax.axis_index("gx") & 1)


def column(side, b):
    index = 9 * (side + 1) + 3 * (b + 1) + 1
    if isinstance(index, int):
        return index if index < 13 else index - 1
    return jnp.where(index > 13, index - 1, index)


def list_pairs(items, masks, by, sides):
    spare = sum(j1 - j0 for _, _, j0, j1, _, _ in sides)
    pairs = jnp.int32(0)
    for i in range(by):
        start, found, last = pairs, jnp.int32(0), jnp.int32(0)
        most = 0
        for side, exists, j0, j1, tile0, own in sides:
            for b in (0, -1, 1):
                j = i + b
                if not j0 <= j < j1:
                    continue
                tile = tile0 + j - j0
                items[1, 2 * start + found] = tile
                items[2, 2 * start + found] = tile
                most += 1
                if own and b == 0:
                    found = found + 1
                    last = jnp.int32(tile)
                    continue
                on = masks[0, i, 0, column(side, b)] == 1
                on = on if exists is None else on & exists
                found = found + on.astype(jnp.int32)
                last = jnp.where(on, tile, last)
        items[1, 2 * start + found] = last
        items[2, 2 * start + found] = spare
        for u in range((most + 1) // 2):
            items[0, start + u] = i
        pairs = start + ((found + 1) >> 1)
    items[0, pairs] = 0
    for u in range(2):
        items[1, 2 * pairs + u] = 0
    return pairs


def attend(items, high, keys, vals, qt, top, acc, scores, peaks):
    groups, depth, lanes = qt.shape[1:]
    hd, p = depth // 2, lanes // 2

    def score(t, g):
        i, k0, k1 = items[0, t], items[1, 2 * t], items[1, 2 * t + 1]
        rows = slice(g * depth, (g + 1) * depth)
        cols = slice(g * lanes, (g + 1) * lanes)
        s0 = nn(keys[k0, :, rows], qt[i, g])
        s1 = nn(keys[k1, :, rows], qt[i, g])
        scores[:p, cols] = s0
        scores[p:, cols] = s1
        peaks[:, cols] = jnp.max(jnp.maximum(s0, s1), axis=0, keepdims=True)

    def weigh(t, g):
        i, v0, v1 = items[0, t], items[2, 2 * t], items[2, 2 * t + 1]
        cols = slice(g * lanes, (g + 1) * lanes)
        old = top[i, :, cols]
        new = jnp.maximum(old, peaks[:, cols])
        probs = jnp.exp(scores[:, cols] - new).astype(BF16)
        fade = jnp.exp(old - new)
        both, sums = [], []
        for h in range(2):
            rows = slice(h * (hd + ONES), (h + 1) * (hd + ONES))
            val = jnp.concatenate([vals[v0, g, rows], vals[v1, g, rows]], axis=1)
            out = nn(val, probs[:, h * p : (h + 1) * p])
            both.append(out[:hd])
            sums.append(out[hd : hd + 8])
        return cols, new, fade, jnp.concatenate(both, axis=1), jnp.concatenate(sums, axis=1)

    lead = groups // 2

    def step(t, carry):
        made = []
        for g in range(0, groups, lead):
            for u in range(g, g + lead):
                score(t + (u + lead) // groups, (u + lead) % groups)
            for u in range(g, g + lead):
                made.append(weigh(t, u))
        i = items[0, t]
        for cols, new, fade, both, sums in made:
            top[i, :, cols] = new
            acc[i, :hd, cols] = acc[i, :hd, cols] * fade + both
            acc[i, hd:, cols] = acc[i, hd:, cols] * fade + sums
        return carry

    for g in range(lead):
        score(0, g)
    lax.fori_loop(0, high, step, 0)


def put_values(vals, tile, g0, v, live):
    p = vals.shape[3]
    hd = vals.shape[2] // 2 - ONES
    flag = jnp.broadcast_to(live.astype(F32).astype(BF16), (ONES, p))
    vt = jnp.where(live, v.T, 0.0).astype(BF16)
    for h in range(v.shape[1] // hd):
        g, r = g0 + h // 2, h % 2 * (hd + ONES)
        vals[tile, g, r : r + hd] = vt[h * hd : (h + 1) * hd]
        vals[tile, g, r + hd : r + hd + ONES] = flag


def put_blocks(tile0, x, w_all, keys, vals, lives):
    p, width = keys.shape[1:]
    wide = min(256, width)
    groups = vals.shape[1]
    for c in range(0, width, wide):
        k = nn(x, w_all[:, width + c : width + c + wide]).astype(BF16)
        v = nn(x, w_all[:, 2 * width + c : 2 * width + c + wide])
        for u, live in enumerate(lives):
            rows = slice(u * p, (u + 1) * p)
            keys[tile0 + u, :, c : c + wide] = k[rows]
            put_values(vals, tile0 + u, c * groups // width, v[rows], live)


def finish(i, tiled, acc, w_out, alive):
    hd = acc.shape[1] - 8
    p = tiled.shape[1]
    heads = acc.shape[2] // p
    attn = acc[i, :hd] * (1.0 / acc[i, hd : hd + 1])
    attn = jnp.concatenate([attn[:, h * p : (h + 1) * p] for h in range(heads)], axis=0).astype(BF16)
    mixed = tiled[i].astype(F32) + tn(attn, w_out[...])
    place = lax.broadcasted_iota(jnp.int32, (p, 1), 0)
    return jnp.where(place < alive, mixed, 0.0).astype(BF16)


def own_kernel(
    n, split, own, masks, counts, w_qkv, w_out, qt, top, acc, w_all, w_last, plan_near, plan0, plan1, keys, vals,
    items, flags, live, scores, peaks, sems
):
    by, p, width = own.shape
    _, depth = qt.shape[1:3]
    hd = depth // 2
    copies = [
        pltpu.make_async_copy(masks, flags, sems.at[0]),
        pltpu.make_async_copy(counts, live, sems.at[1]),
        pltpu.make_async_copy(w_qkv, w_all, sems.at[2]),
        pltpu.make_async_copy(w_out, w_last, sems.at[3]),
    ]
    for copy in copies:
        copy.start()
    me = lax.axis_index("gx")
    side = toward_near()
    place = lax.broadcasted_iota(jnp.int32, (1, p), 1)
    top[...] = jnp.full_like(top, NEG)
    acc[...] = jnp.zeros_like(acc)
    vals[by] = jnp.zeros(vals.shape[1:], BF16)
    copies[0].wait()
    copies[1].wait()
    pairs = list_pairs(items, flags, by, [(0, None, 0, by, 0, True)])
    for plan, a, j0, j1 in ((plan_near, side, 0, by), (plan0, -side, 0, split), (plan1, -side, split, by)):
        there = (me + a >= 0) & (me + a < n)
        slab = jnp.clip(me + a, 0, n - 1)
        plan[3, 0] = list_pairs(plan, flags, by, [(a, there, j0, j1, 0, False)])
        for i in range(by):
            plan[3, 1 + i] = live[i, 0, me]
        for j in range(j0, j1):
            plan[3, 1 + by + j - j0] = live[j, 0, slab]
    zeros = jnp.zeros((hd, p), BF16)
    copies[2].wait()
    mine = own[...].reshape(by * p, width)
    wide = min(256, width)
    for c in range(0, width, wide):
        q = (nn(mine, w_all[:, c : c + wide]).astype(BF16) * BF16(1.0 / hd**0.5)).astype(F32)
        for i in range(by):
            t = q[i * p : (i + 1) * p].T.astype(BF16)
            for u in range(wide // depth):
                g, mid = c // depth + u, u * depth + hd
                qt[i, g, :hd, :p] = t[mid - hd : mid]
                qt[i, g, :hd, p:] = zeros
                qt[i, g, hd:, :p] = zeros
                qt[i, g, hd:, p:] = t[mid : mid + hd]
    put_blocks(0, mine, w_all, keys, vals, [place < live[i, 0, me] for i in range(by)])
    attend(items, pairs, keys, vals, qt, top, acc, scores, peaks)
    copies[3].wait()


def far_work(rim, w_all, qt, plan, top, acc, keys, vals, scores, peaks):
    by = qt.shape[0]
    blocks, p, width = rim.shape
    place = lax.broadcasted_iota(jnp.int32, (1, p), 1)
    vals[blocks] = jnp.zeros(vals.shape[1:], BF16)
    put_blocks(0, rim[...].reshape(blocks * p, width), w_all, keys, vals, [place < plan[3, 1 + by + j] for j in range(blocks)])
    attend(plan, plan[3, 0], keys, vals, qt, top, acc, scores, peaks)


def near_kernel(rim, w_all, qt, top_in, acc_in, plan, top, acc, keys, vals, scores, peaks):
    far_work(rim, w_all, qt, plan, top, acc, keys, vals, scores, peaks)


def far_kernel(
    rim, norm, w_all, qt, top_in, acc_in, tiled, w_out, plan, top, acc, held, keys, vals, scores, peaks, nrm
):
    for j in range(rim.shape[0]):
        nrm[j] = normalise(rim[j], norm[0:1], norm[1:2])
    far_work(nrm, w_all, qt, plan, top, acc, keys, vals, scores, peaks)
    for i in range(held.shape[0]):
        held[i] = finish(i, tiled, acc, w_out, plan[3, 1 + i])


def last_kernel(
    rim, w_all, qt, top_in, acc_in, tiled, w_out, held, plan, top, acc, result, keys, vals, scores, peaks, out,
    sems
):
    by, early = tiled.shape[0], held.shape[0]
    copies = [pltpu.make_async_copy(held.at[i], result.at[0, i, 0], sems.at[i]) for i in range(early)]
    for copy in copies:
        copy.start()
    far_work(rim, w_all, qt, plan, top, acc, keys, vals, scores, peaks)
    for i in range(early, by):
        out[i - early] = finish(i, tiled, acc, w_out, plan[3, 1 + i])
        copies.append(pltpu.make_async_copy(out.at[i - early], result.at[0, i, 0], sems.at[i]))
        copies[-1].start()
    for copy in copies:
        copy.wait()


def vmem(x):
    return pltpu.with_memory_space_constraint(x, pltpu.VMEM)


def smem(x):
    return pltpu.with_memory_space_constraint(x, pltpu.SMEM)


def hbm(x):
    return pltpu.with_memory_space_constraint(x, pltpu.HBM)


def shards(n, points, order, masks, counts, gain, shift_bias, w_qkv, w_out):
    _, by, bz, p, width = points.shape
    hd = width // HEADS
    groups, depth, lanes = HEADS // 2, 2 * hd, 2 * p
    split = max(by - 2, 1)
    early = max(split - 1, 1)
    whole = pl.BlockSpec(memory_space=pltpu.VMEM)
    apart = pl.BlockSpec(memory_space=pltpu.HBM)
    words = pl.BlockSpec(memory_space=pltpu.SMEM)
    plan = pltpu.SMEM((4, 8 * by), jnp.int32)
    params = pltpu.CompilerParams(vmem_limit_bytes=LIMIT)
    points, order, masks, w_qkv, w_out = map(hbm, (points, order, masks, w_qkv, w_out))
    counts = hbm(jnp.transpose(counts, (1, 2, 0)))
    live = pltpu.SMEM(counts.shape, jnp.int32)
    flags = pltpu.SMEM(masks.shape, jnp.int32)

    first, rest, places, norm = pl.pallas_call(
        gather_kernel,
        out_shape=(
            pltpu.VMEM((split, p, width), BF16),
            pltpu.VMEM((by - split, p, width), BF16),
            pltpu.VMEM((by - split, 1, p), jnp.int32),
            pltpu.VMEM((2, width), F32),
        ),
        in_specs=[apart] * 5,
        out_specs=(whole,) * 4,
        scratch_shapes=[
            pltpu.VMEM((split, p, width), BF16),
            pltpu.VMEM(order.shape, jnp.int32),
            live,
            pltpu.SemaphoreType.DMA((by + 4,)),
        ],
        compiler_params=params,
        name="gather",
    )(points, order, counts, hbm(gain[None]), hbm(shift_bias[None]))
    tile_rest = pl.pallas_call(
        rest_kernel,
        out_shape=(
            pltpu.VMEM((by, p, width), BF16),
            pltpu.VMEM((by, p, width), BF16),
            pltpu.VMEM((by - split, p, width), BF16),
        ),
        in_specs=[whole] * 4,
        out_specs=(whole,) * 3,
        compiler_params=params,
        name="rest",
    )
    tiled, normed, second = tile_rest(vmem(first), vmem(rest), vmem(places), vmem(norm))
    near_pairs = [(i, i ^ 1) for i in range(n) if i ^ 1 < n]
    far_pairs = [(i, i + 1) for i in range(1, n - 1, 2)] + [(i + 1, i) for i in range(1, n - 1, 2)]

    def moved(value, pairs):
        return lax.ppermute(value, "gx", pairs)

    far0 = moved(first, far_pairs)
    near = moved(normed, near_pairs)
    far1 = moved(second, far_pairs)

    state = (
        pltpu.VMEM((by, 1, groups * lanes), F32),
        pltpu.VMEM((by, hd + 8, groups * lanes), F32),
    )

    def scratch(tiles):
        return [
            pltpu.VMEM((tiles, p, width), BF16),
            pltpu.VMEM((tiles + 1, groups, depth + 2 * ONES, p), BF16),
        ]

    ahead = [
        pltpu.VMEM((2 * p, groups * lanes), F32),
        pltpu.VMEM((1, groups * lanes), F32),
    ]
    qt, top, acc, w_all, w_last, plan_near, plan0, plan1 = pl.pallas_call(
        functools.partial(own_kernel, n, split),
        out_shape=(
            pltpu.VMEM((by, groups, depth, lanes), BF16),
            *state,
            pltpu.VMEM(w_qkv.shape, BF16),
            pltpu.VMEM(w_out.shape, BF16),
            *(plan,) * 3,
        ),
        in_specs=[whole, apart, apart, apart, apart],
        out_specs=(whole,) * 5 + (words,) * 3,
        scratch_shapes=[*scratch(by), plan, flags, live, *ahead, pltpu.SemaphoreType.DMA((4,))],
        compiler_params=params,
        name="own",
    )(vmem(normed), masks, counts, w_qkv, w_out)
    near_work = pl.pallas_call(
        near_kernel,
        out_shape=state,
        in_specs=[*(whole,) * 5, words],
        out_specs=(whole,) * 2,
        scratch_shapes=[*scratch(by), *ahead],
        input_output_aliases={3: 0, 4: 1},
        compiler_params=params,
        name="near",
    )
    top, acc = near_work(*map(vmem, (near, w_all, qt, top, acc)), smem(plan_near))
    ins = [far0, norm, w_all, qt, top, acc, tiled, w_last]
    top, acc, held = pl.pallas_call(
        far_kernel,
        out_shape=(*state, pltpu.VMEM((early, p, width), BF16)),
        in_specs=[*(whole,) * len(ins), words],
        out_specs=(whole,) * 3,
        scratch_shapes=[*scratch(split), *ahead, pltpu.VMEM((split, p, width), BF16)],
        input_output_aliases={4: 0, 5: 1},
        compiler_params=params,
        name="far",
    )(*map(vmem, ins), smem(plan0))
    ins = [far1, w_all, qt, top, acc, tiled, w_last, held]
    _, _, result = pl.pallas_call(
        last_kernel,
        out_shape=(*state, pltpu.HBM((1, by, bz, p, width), BF16)),
        in_specs=[*(whole,) * len(ins), words],
        out_specs=(whole, whole, apart),
        scratch_shapes=[
            *scratch(by - split),
            *ahead,
            pltpu.VMEM((by - early, p, width), BF16),
            pltpu.SemaphoreType.DMA((by,)),
        ],
        input_output_aliases={3: 0, 4: 1},
        compiler_params=params,
        name="last",
    )(*map(vmem, ins), smem(plan1))
    return result


def solution(mesh):
    placed = (
        P(("groups", "gx"), None, None, None, None),
        P(("groups", "gx"), None, None, None),
        P(("groups", "gx"), None, None, None),
        P("groups", None, None),
        P(),
        P(),
        P(),
        P(),
    )
    return jax.shard_map(
        functools.partial(shards, mesh.shape["gx"]),
        mesh=mesh,
        in_specs=placed,
        out_specs=P(("groups", "gx"), None, None, None, None),
        check_vma=False,
    )
```

```python
import functools

import jax
import jax.numpy as jnp
from jax import lax
from jax.experimental import pallas as pl
from jax.experimental.pallas import tpu as pltpu
from jax.sharding import PartitionSpec as P


HEADS = 8
NEG = -1e30
ONES = 16
LIMIT = 24 * 1024 * 1024
BF16, F32 = jnp.bfloat16, jnp.float32


def tn(a, b):
    return lax.dot_general(a, b, (((0,), (0,)), ((), ())), preferred_element_type=F32)


def nn(a, b):
    return jnp.dot(a, b, preferred_element_type=F32)


def normalise(tiled, gain, shift):
    values = tiled.astype(F32)
    mean = jnp.mean(values, axis=-1, keepdims=True)
    var = jnp.mean((values - mean) ** 2, axis=-1, keepdims=True)
    return ((values - mean) * lax.rsqrt(var + 1e-05) * gain + shift).astype(BF16)


def select(row, raw):
    p = raw.shape[0]
    slot = lax.broadcasted_iota(jnp.int32, (p, p), 0)
    return tn((slot == row).astype(F32).astype(BF16), raw).astype(BF16)


def gather_kernel(points, order, counts, gain, shift, first, rest, places, norm, raw, rows, live, sems):
    _, by, _, p, _ = points.shape
    split = first.shape[0]
    me = lax.axis_index("gx")
    small = [
        pltpu.make_async_copy(order, rows, sems.at[by]),
        pltpu.make_async_copy(counts, live, sems.at[by + 1]),
        pltpu.make_async_copy(gain, norm.at[0:1], sems.at[by + 2]),
        pltpu.make_async_copy(shift, norm.at[1:2], sems.at[by + 3]),
    ]
    large = [
        pltpu.make_async_copy(
            points.at[0, j, 0], raw.at[j] if j < split else rest.at[j - split], sems.at[j]
        )
        for j in range(by)
    ]
    for copy in (*small[:2], *large, *small[2:]):
        copy.start()
    place = lax.broadcasted_iota(jnp.int32, (1, p), 1)
    small[0].wait()
    small[1].wait()
    picks = []
    for j in range(by):
        row = rows[0, j]
        picks.append(jnp.where(place < live[j, 0, me], row, row[:, :1]))
        if j >= split:
            places[j - split] = picks[j]
    for j in range(split):
        large[j].wait()
    for j in range(split):
        first[j] = select(picks[j], raw[j])
    for copy in (*large[split:], *small[2:]):
        copy.wait()


def rest_kernel(first, rest, places, norm, tiled, normed, second):
    split = first.shape[0]
    gain, shift = norm[0:1], norm[1:2]
    for j in range(rest.shape[0]):
        got = select(places[j], rest[j])
        tiled[split + j] = got
        got = normalise(got, gain, shift)
        second[j] = got
        normed[split + j] = got
    for j in range(split):
        got = first[j]
        tiled[j] = got
        normed[j] = normalise(got, gain, shift)


def toward_near():
    return 1 - 2 * (lax.axis_index("gx") & 1)


def in_first_class(me):
    return ((me + 1) >> 1) & 1 == 1


def column(side, b):
    index = 9 * (side + 1) + 3 * (b + 1) + 1
    if isinstance(index, int):
        return index if index < 13 else index - 1
    return jnp.where(index > 13, index - 1, index)


def list_pairs(items, masks, by, sides):
    spare = sum(j1 - j0 for _, _, j0, j1, _, _ in sides)
    pairs, ends = jnp.int32(0), []
    for i in range(by):
        start, found, last = pairs, jnp.int32(0), jnp.int32(0)
        most = 0
        for side, exists, j0, j1, tile0, own in sides:
            for b in (0, -1, 1):
                j = i + b
                if not j0 <= j < j1:
                    continue
                tile = tile0 + j - j0
                items[1, 2 * start + found] = tile
                items[2, 2 * start + found] = tile
                most += 1
                if own and b == 0:
                    found = found + 1
                    last = jnp.int32(tile)
                    continue
                on = masks[0, i, 0, column(side, b)] == 1
                on = on if exists is None else on & exists
                found = found + on.astype(jnp.int32)
                last = jnp.where(on, tile, last)
        items[1, 2 * start + found] = last
        items[2, 2 * start + found] = spare
        for u in range((most + 1) // 2):
            items[0, start + u] = i
        pairs = start + ((found + 1) >> 1)
        ends.append(pairs)
    items[0, pairs] = 0
    for u in range(2):
        items[1, 2 * pairs + u] = 0
    return pairs, ends


def attend(items, high, keys, vals, qt, top, acc, scores, peaks):
    groups, depth, lanes = qt.shape[1:]
    hd, p = depth // 2, lanes // 2

    def score(t, g):
        i, k0, k1 = items[0, t], items[1, 2 * t], items[1, 2 * t + 1]
        rows = slice(g * depth, (g + 1) * depth)
        cols = slice(g * lanes, (g + 1) * lanes)
        s0 = nn(keys[k0, :, rows], qt[i, g])
        s1 = nn(keys[k1, :, rows], qt[i, g])
        scores[:p, cols] = s0
        scores[p:, cols] = s1
        peaks[:, cols] = jnp.max(jnp.maximum(s0, s1), axis=0, keepdims=True)

    def weigh(t, g):
        i, v0, v1 = items[0, t], items[2, 2 * t], items[2, 2 * t + 1]
        cols = slice(g * lanes, (g + 1) * lanes)
        old = top[i, :, cols]
        new = jnp.maximum(old, peaks[:, cols])
        probs = jnp.exp(scores[:, cols] - new).astype(BF16)
        fade = jnp.exp(old - new)
        both, sums = [], []
        for h in range(2):
            rows = slice(h * (hd + ONES), (h + 1) * (hd + ONES))
            val = jnp.concatenate([vals[v0, g, rows], vals[v1, g, rows]], axis=1)
            out = nn(val, probs[:, h * p : (h + 1) * p])
            both.append(out[:hd])
            sums.append(out[hd : hd + 8])
        return cols, new, fade, jnp.concatenate(both, axis=1), jnp.concatenate(sums, axis=1)

    lead = groups // 2

    def step(t, carry):
        made = []
        for g in range(0, groups, lead):
            for u in range(g, g + lead):
                score(t + (u + lead) // groups, (u + lead) % groups)
            for u in range(g, g + lead):
                made.append(weigh(t, u))
        i = items[0, t]
        for cols, new, fade, both, sums in made:
            top[i, :, cols] = new
            acc[i, :hd, cols] = acc[i, :hd, cols] * fade + both
            acc[i, hd:, cols] = acc[i, hd:, cols] * fade + sums
        return carry

    for g in range(lead):
        score(0, g)
    lax.fori_loop(0, high, step, 0)


def put_values(vals, tile, g0, v, live):
    p = vals.shape[3]
    hd = vals.shape[2] // 2 - ONES
    flag = jnp.broadcast_to(live.astype(F32).astype(BF16), (ONES, p))
    vt = jnp.where(live, v.T, 0.0).astype(BF16)
    for h in range(v.shape[1] // hd):
        g, r = g0 + h // 2, h % 2 * (hd + ONES)
        vals[tile, g, r : r + hd] = vt[h * hd : (h + 1) * hd]
        vals[tile, g, r + hd : r + hd + ONES] = flag


def put_blocks(tile0, x, w_all, keys, vals, lives):
    p, width = keys.shape[1:]
    wide = min(256, width)
    groups = vals.shape[1]
    for c in range(0, width, wide):
        k = nn(x, w_all[:, width + c : width + c + wide]).astype(BF16)
        v = nn(x, w_all[:, 2 * width + c : 2 * width + c + wide])
        for u, live in enumerate(lives):
            rows = slice(u * p, (u + 1) * p)
            keys[tile0 + u, :, c : c + wide] = k[rows]
            put_values(vals, tile0 + u, c * groups // width, v[rows], live)


def finish(i, tiled, acc, w_out, alive):
    hd = acc.shape[1] - 8
    p = tiled.shape[1]
    heads = acc.shape[2] // p
    attn = acc[i, :hd] * (1.0 / acc[i, hd : hd + 1])
    attn = jnp.concatenate([attn[:, h * p : (h + 1) * p] for h in range(heads)], axis=0).astype(BF16)
    mixed = tiled[i].astype(F32) + tn(attn, w_out[...])
    place = lax.broadcasted_iota(jnp.int32, (p, 1), 0)
    return jnp.where(place < alive, mixed, 0.0).astype(BF16)


def main_kernel(
    n, split, own, near, masks, counts, w_qkv, w_out, qt, top, acc, w_all, w_last, plan0, plan1, keys, vals,
    items, flags, live, scores, peaks, sems
):
    by, p, width = own.shape
    _, depth = qt.shape[1:3]
    hd = depth // 2
    copies = [
        pltpu.make_async_copy(masks, flags, sems.at[0]),
        pltpu.make_async_copy(counts, live, sems.at[1]),
        pltpu.make_async_copy(w_qkv, w_all, sems.at[2]),
        pltpu.make_async_copy(w_out, w_last, sems.at[3]),
    ]
    for copy in copies:
        copy.start()
    me = lax.axis_index("gx")
    side = toward_near()
    partner = me + side
    exists = (partner >= 0) & (partner < n)
    slab = jnp.clip(partner, 0, n - 1)
    place = lax.broadcasted_iota(jnp.int32, (1, p), 1)
    top[...] = jnp.full_like(top, NEG)
    acc[...] = jnp.zeros_like(acc)
    vals[2 * by] = jnp.zeros(vals.shape[1:], BF16)
    copies[0].wait()
    copies[1].wait()
    pairs, _ = list_pairs(
        items, flags, by, [(0, None, 0, by, 0, True), (side, exists, 0, by, by, False)]
    )
    other = me - side
    there = (other >= 0) & (other < n)
    beyond = jnp.clip(other, 0, n - 1)
    for plan, j0, j1 in ((plan0, 0, split), (plan1, split, by)):
        plan[3, 0], _ = list_pairs(plan, flags, by, [(-side, there, j0, j1, 0, False)])
        for i in range(by):
            plan[3, 1 + i] = live[i, 0, me]
        for j in range(j0, j1):
            plan[3, 1 + by + j - j0] = live[j, 0, beyond]
    zeros = jnp.zeros((hd, p), BF16)
    copies[2].wait()
    mine, theirs = own[...].reshape(by * p, width), near[...].reshape(by * p, width)
    wide = min(256, width)
    for c in range(0, width, wide):
        q = (nn(mine, w_all[:, c : c + wide]).astype(BF16) * BF16(1.0 / hd**0.5)).astype(F32)
        for i in range(by):
            t = q[i * p : (i + 1) * p].T.astype(BF16)
            for u in range(wide // depth):
                g, mid = c // depth + u, u * depth + hd
                qt[i, g, :hd, :p] = t[mid - hd : mid]
                qt[i, g, :hd, p:] = zeros
                qt[i, g, hd:, :p] = zeros
                qt[i, g, hd:, p:] = t[mid : mid + hd]
    put_blocks(0, mine, w_all, keys, vals, [place < live[i, 0, me] for i in range(by)])
    put_blocks(by, theirs, w_all, keys, vals, [place < live[i, 0, slab] for i in range(by)])
    attend(items, pairs, keys, vals, qt, top, acc, scores, peaks)
    copies[3].wait()


def far_work(rim, w_all, qt, plan, top, acc, keys, vals, scores, peaks):
    by = qt.shape[0]
    blocks, p, width = rim.shape
    place = lax.broadcasted_iota(jnp.int32, (1, p), 1)
    vals[blocks] = jnp.zeros(vals.shape[1:], BF16)
    put_blocks(0, rim[...].reshape(blocks * p, width), w_all, keys, vals, [place < plan[3, 1 + by + j] for j in range(blocks)])
    attend(plan, plan[3, 0], keys, vals, qt, top, acc, scores, peaks)


def far_kernel(
    rim, norm, w_all, qt, top_in, acc_in, tiled, w_out, plan, top, acc, held, keys, vals, scores, peaks, nrm
):
    for j in range(rim.shape[0]):
        nrm[j] = normalise(rim[j], norm[0:1], norm[1:2])
    far_work(nrm, w_all, qt, plan, top, acc, keys, vals, scores, peaks)
    for i in range(held.shape[0]):
        held[i] = finish(i, tiled, acc, w_out, plan[3, 1 + i])


def last_kernel(
    rim_a, rim_b, w_all, qt, top_in, acc_in, tiled, w_out, held, plan, top, acc, result, keys, vals, scores, peaks, out,
    rim, sems
):
    by, early = tiled.shape[0], held.shape[0]
    copies = [pltpu.make_async_copy(held.at[i], result.at[0, i, 0], sems.at[i]) for i in range(early)]
    for copy in copies:
        copy.start()
    rim[...] = jnp.where(in_first_class(lax.axis_index("gx")), rim_a[...], rim_b[...])
    far_work(rim, w_all, qt, plan, top, acc, keys, vals, scores, peaks)
    for i in range(early, by):
        out[i - early] = finish(i, tiled, acc, w_out, plan[3, 1 + i])
        copies.append(pltpu.make_async_copy(out.at[i - early], result.at[0, i, 0], sems.at[i]))
        copies[-1].start()
    for copy in copies:
        copy.wait()


def vmem(x):
    return pltpu.with_memory_space_constraint(x, pltpu.VMEM)


def smem(x):
    return pltpu.with_memory_space_constraint(x, pltpu.SMEM)


def hbm(x):
    return pltpu.with_memory_space_constraint(x, pltpu.HBM)


def shards(n, points, order, masks, counts, gain, shift_bias, w_qkv, w_out):
    _, by, bz, p, width = points.shape
    hd = width // HEADS
    groups, depth, lanes = HEADS // 2, 2 * hd, 2 * p
    split = max(by - 2, 1)
    early = max(split - 1, 1)
    whole = pl.BlockSpec(memory_space=pltpu.VMEM)
    apart = pl.BlockSpec(memory_space=pltpu.HBM)
    words = pl.BlockSpec(memory_space=pltpu.SMEM)
    plan = pltpu.SMEM((4, 8 * by), jnp.int32)
    params = pltpu.CompilerParams(vmem_limit_bytes=LIMIT)
    points, order, masks, w_qkv, w_out = map(hbm, (points, order, masks, w_qkv, w_out))
    counts = hbm(jnp.transpose(counts, (1, 2, 0)))
    live = pltpu.SMEM(counts.shape, jnp.int32)
    flags = pltpu.SMEM(masks.shape, jnp.int32)

    first, rest, places, norm = pl.pallas_call(
        gather_kernel,
        out_shape=(
            pltpu.VMEM((split, p, width), BF16),
            pltpu.VMEM((by - split, p, width), BF16),
            pltpu.VMEM((by - split, 1, p), jnp.int32),
            pltpu.VMEM((2, width), F32),
        ),
        in_specs=[apart] * 5,
        out_specs=(whole,) * 4,
        scratch_shapes=[
            pltpu.VMEM((split, p, width), BF16),
            pltpu.VMEM(order.shape, jnp.int32),
            live,
            pltpu.SemaphoreType.DMA((by + 4,)),
        ],
        compiler_params=params,
        name="gather",
    )(points, order, counts, hbm(gain[None]), hbm(shift_bias[None]))
    tile_rest = pl.pallas_call(
        rest_kernel,
        out_shape=(
            pltpu.VMEM((by, p, width), BF16),
            pltpu.VMEM((by, p, width), BF16),
            pltpu.VMEM((by - split, p, width), BF16),
        ),
        in_specs=[whole] * 4,
        out_specs=(whole,) * 3,
        compiler_params=params,
        name="rest",
    )
    tiled, normed, second = tile_rest(vmem(first), vmem(rest), vmem(places), vmem(norm))
    near_pairs = [(i, i ^ 1) for i in range(n) if i ^ 1 < n]
    far_pairs = [(i, i + 1) for i in range(1, n - 1, 2)] + [(i + 1, i) for i in range(1, n - 1, 2)]

    def moved(value, pairs):
        return lax.ppermute(value, "gx", pairs)

    far0 = moved(first, far_pairs)
    near = moved(normed, near_pairs)
    far_a = moved(second, [pair for pair in far_pairs if in_first_class(pair[0])])
    far_b = moved(second, [pair for pair in far_pairs if not in_first_class(pair[0])])

    state = (
        pltpu.VMEM((by, 1, groups * lanes), F32),
        pltpu.VMEM((by, hd + 8, groups * lanes), F32),
    )

    def scratch(tiles):
        return [
            pltpu.VMEM((tiles, p, width), BF16),
            pltpu.VMEM((tiles + 1, groups, depth + 2 * ONES, p), BF16),
        ]

    ahead = [
        pltpu.VMEM((2 * p, groups * lanes), F32),
        pltpu.VMEM((1, groups * lanes), F32),
    ]
    main = pl.pallas_call(
        functools.partial(main_kernel, n, split),
        out_shape=(
            pltpu.VMEM((by, groups, depth, lanes), BF16),
            *state,
            pltpu.VMEM(w_qkv.shape, BF16),
            pltpu.VMEM(w_out.shape, BF16),
            plan,
            plan,
        ),
        in_specs=[whole, whole, apart, apart, apart, apart],
        out_specs=(whole,) * 5 + (words,) * 2,
        scratch_shapes=[*scratch(2 * by), plan, flags, live, *ahead, pltpu.SemaphoreType.DMA((4,))],
        compiler_params=params,
        name="main",
    )
    qt, top, acc, w_all, w_last, plan0, plan1 = main(
        vmem(normed), vmem(near), masks, counts, w_qkv, w_out
    )

    ins = [far0, norm, w_all, qt, top, acc, tiled, w_last]
    top, acc, held = pl.pallas_call(
        far_kernel,
        out_shape=(*state, pltpu.VMEM((early, p, width), BF16)),
        in_specs=[*(whole,) * len(ins), words],
        out_specs=(whole,) * 3,
        scratch_shapes=[*scratch(split), *ahead, pltpu.VMEM((split, p, width), BF16)],
        input_output_aliases={4: 0, 5: 1},
        compiler_params=params,
        name="far",
    )(*map(vmem, ins), smem(plan0))
    ins = [far_a, far_b, w_all, qt, top, acc, tiled, w_last, held]
    _, _, result = pl.pallas_call(
        last_kernel,
        out_shape=(*state, pltpu.HBM((1, by, bz, p, width), BF16)),
        in_specs=[*(whole,) * len(ins), words],
        out_specs=(whole, whole, apart),
        scratch_shapes=[
            *scratch(by - split),
            *ahead,
            pltpu.VMEM((by - early, p, width), BF16),
            pltpu.VMEM((by - split, p, width), BF16),
            pltpu.SemaphoreType.DMA((by,)),
        ],
        input_output_aliases={4: 0, 5: 1},
        compiler_params=params,
        name="last",
    )(*map(vmem, ins), smem(plan1))
    return result


def solution(mesh):
    placed = (
        P(("groups", "gx"), None, None, None, None),
        P(("groups", "gx"), None, None, None),
        P(("groups", "gx"), None, None, None),
        P("groups", None, None),
        P(),
        P(),
        P(),
        P(),
    )
    return jax.shard_map(
        functools.partial(shards, mesh.shape["gx"]),
        mesh=mesh,
        in_specs=placed,
        out_specs=P(("groups", "gx"), None, None, None, None),
        check_vma=False,
    )
```

```python
import functools

import jax
import jax.numpy as jnp
from jax import lax
from jax.experimental import pallas as pl
from jax.experimental.pallas import tpu as pltpu
from jax.sharding import PartitionSpec as P


HEADS = 8
NEG = -1e30
ONES = 16
LIMIT = 24 * 1024 * 1024
BF16, F32 = jnp.bfloat16, jnp.float32


def tn(a, b):
    return lax.dot_general(a, b, (((0,), (0,)), ((), ())), preferred_element_type=F32)


def nn(a, b):
    return jnp.dot(a, b, preferred_element_type=F32)


def normalise(tiled, gain, shift):
    values = tiled.astype(F32)
    mean = jnp.mean(values, axis=-1, keepdims=True)
    var = jnp.mean((values - mean) ** 2, axis=-1, keepdims=True)
    return ((values - mean) * lax.rsqrt(var + 1e-05) * gain + shift).astype(BF16)


def select(row, raw):
    p = raw.shape[0]
    slot = lax.broadcasted_iota(jnp.int32, (p, p), 0)
    return tn((slot == row).astype(F32).astype(BF16), raw).astype(BF16)


def gather_kernel(points, order, counts, gain, shift, first, rest, places, norm, raw, rows, live, sems):
    _, by, _, p, _ = points.shape
    split = first.shape[0]
    me = lax.axis_index("gx")
    small = [
        pltpu.make_async_copy(order, rows, sems.at[by]),
        pltpu.make_async_copy(counts, live, sems.at[by + 1]),
        pltpu.make_async_copy(gain, norm.at[0:1], sems.at[by + 2]),
        pltpu.make_async_copy(shift, norm.at[1:2], sems.at[by + 3]),
    ]
    large = [
        pltpu.make_async_copy(
            points.at[0, j, 0], raw.at[j] if j < split else rest.at[j - split], sems.at[j]
        )
        for j in range(by)
    ]
    for copy in (*small[:2], *large, *small[2:]):
        copy.start()
    place = lax.broadcasted_iota(jnp.int32, (1, p), 1)
    small[0].wait()
    small[1].wait()
    picks = []
    for j in range(by):
        row = rows[0, j]
        picks.append(jnp.where(place < live[j, 0, me], row, row[:, :1]))
        if j >= split:
            places[j - split] = picks[j]
    for j in range(split):
        large[j].wait()
    for j in range(split):
        first[j] = select(picks[j], raw[j])
    for copy in (*large[split:], *small[2:]):
        copy.wait()


def rest_kernel(first, rest, places, norm, tiled, normed, second):
    split = first.shape[0]
    gain, shift = norm[0:1], norm[1:2]
    for j in range(rest.shape[0]):
        got = select(places[j], rest[j])
        tiled[split + j] = got
        got = normalise(got, gain, shift)
        second[j] = got
        normed[split + j] = got
    for j in range(split):
        got = first[j]
        tiled[j] = got
        normed[j] = normalise(got, gain, shift)


def toward_near():
    return 1 - 2 * (lax.axis_index("gx") & 1)


def in_first_class(me):
    return ((me + 1) >> 1) & 1 == 1


def column(side, b):
    index = 9 * (side + 1) + 3 * (b + 1) + 1
    if isinstance(index, int):
        return index if index < 13 else index - 1
    return jnp.where(index > 13, index - 1, index)


def list_pairs(items, masks, by, sides):
    spare = sum(j1 - j0 for _, _, j0, j1, _, _ in sides)
    pairs, ends = jnp.int32(0), []
    for i in range(by):
        start, found, last = pairs, jnp.int32(0), jnp.int32(0)
        most = 0
        for side, exists, j0, j1, tile0, own in sides:
            for b in (0, -1, 1):
                j = i + b
                if not j0 <= j < j1:
                    continue
                tile = tile0 + j - j0
                items[1, 2 * start + found] = tile
                items[2, 2 * start + found] = tile
                most += 1
                if own and b == 0:
                    found = found + 1
                    last = jnp.int32(tile)
                    continue
                on = masks[0, i, 0, column(side, b)] == 1
                on = on if exists is None else on & exists
                found = found + on.astype(jnp.int32)
                last = jnp.where(on, tile, last)
        items[1, 2 * start + found] = last
        items[2, 2 * start + found] = spare
        for u in range((most + 1) // 2):
            items[0, start + u] = i
        pairs = start + ((found + 1) >> 1)
        ends.append(pairs)
    items[0, pairs] = 0
    for u in range(2):
        items[1, 2 * pairs + u] = 0
    return pairs, ends


def attend(items, low, high, keys, vals, qt, top, acc, scores, peaks):
    groups, depth, lanes = qt.shape[1:]
    hd, p = depth // 2, lanes // 2

    def score(t, g):
        i, k0, k1 = items[0, t], items[1, 2 * t], items[1, 2 * t + 1]
        rows = slice(g * depth, (g + 1) * depth)
        cols = slice(g * lanes, (g + 1) * lanes)
        s0 = nn(keys[k0, :, rows], qt[i, g])
        s1 = nn(keys[k1, :, rows], qt[i, g])
        scores[:p, cols] = s0
        scores[p:, cols] = s1
        peaks[:, cols] = jnp.max(jnp.maximum(s0, s1), axis=0, keepdims=True)

    def weigh(t, g):
        i, v0, v1 = items[0, t], items[2, 2 * t], items[2, 2 * t + 1]
        cols = slice(g * lanes, (g + 1) * lanes)
        old = top[i, :, cols]
        new = jnp.maximum(old, peaks[:, cols])
        probs = jnp.exp(scores[:, cols] - new).astype(BF16)
        fade = jnp.exp(old - new)
        both, sums = [], []
        for h in range(2):
            rows = slice(h * (hd + ONES), (h + 1) * (hd + ONES))
            val = jnp.concatenate([vals[v0, g, rows], vals[v1, g, rows]], axis=1)
            out = nn(val, probs[:, h * p : (h + 1) * p])
            both.append(out[:hd])
            sums.append(out[hd : hd + 8])
        return cols, new, fade, jnp.concatenate(both, axis=1), jnp.concatenate(sums, axis=1)

    lead = groups // 2

    def step(t, carry):
        made = []
        for g in range(0, groups, lead):
            for u in range(g, g + lead):
                score(t + (u + lead) // groups, (u + lead) % groups)
            for u in range(g, g + lead):
                made.append(weigh(t, u))
        i = items[0, t]
        for cols, new, fade, both, sums in made:
            top[i, :, cols] = new
            acc[i, :hd, cols] = acc[i, :hd, cols] * fade + both
            acc[i, hd:, cols] = acc[i, hd:, cols] * fade + sums
        return carry

    for g in range(lead):
        score(low, g)
    lax.fori_loop(low, high, step, 0)


def put_values(vals, tile, g0, v, live):
    p = vals.shape[3]
    hd = vals.shape[2] // 2 - ONES
    flag = jnp.broadcast_to(live.astype(F32).astype(BF16), (ONES, p))
    vt = jnp.where(live, v.T, 0.0).astype(BF16)
    for h in range(v.shape[1] // hd):
        g, r = g0 + h // 2, h % 2 * (hd + ONES)
        vals[tile, g, r : r + hd] = vt[h * hd : (h + 1) * hd]
        vals[tile, g, r + hd : r + hd + ONES] = flag


def put_blocks(tile0, x, w_all, keys, vals, lives):
    p, width = keys.shape[1:]
    wide = min(256, width)
    groups = vals.shape[1]
    for c in range(0, width, wide):
        k = nn(x, w_all[:, width + c : width + c + wide]).astype(BF16)
        v = nn(x, w_all[:, 2 * width + c : 2 * width + c + wide])
        for u, live in enumerate(lives):
            rows = slice(u * p, (u + 1) * p)
            keys[tile0 + u, :, c : c + wide] = k[rows]
            put_values(vals, tile0 + u, c * groups // width, v[rows], live)


def finish(i, tiled, acc, w_out, alive):
    hd = acc.shape[1] - 8
    p = tiled.shape[1]
    heads = acc.shape[2] // p
    attn = acc[i, :hd] * (1.0 / acc[i, hd : hd + 1])
    attn = jnp.concatenate([attn[:, h * p : (h + 1) * p] for h in range(heads)], axis=0).astype(BF16)
    mixed = tiled[i].astype(F32) + tn(attn, w_out[...])
    place = lax.broadcasted_iota(jnp.int32, (p, 1), 0)
    return jnp.where(place < alive, mixed, 0.0).astype(BF16)


def main_kernel(
    n, split, own, near, masks, counts, w_qkv, w_out, qt, top, acc, w_all, w_last, plan0, plan1, keys, vals, items,
    flags, live, scores, peaks, sems
):
    by, p, width = own.shape
    _, depth = qt.shape[1:3]
    hd = depth // 2
    copies = [
        pltpu.make_async_copy(masks, flags, sems.at[0]),
        pltpu.make_async_copy(counts, live, sems.at[1]),
        pltpu.make_async_copy(w_qkv, w_all, sems.at[2]),
        pltpu.make_async_copy(w_out, w_last, sems.at[3]),
    ]
    for copy in copies:
        copy.start()
    me = lax.axis_index("gx")
    side = toward_near()
    partner = me + side
    exists = (partner >= 0) & (partner < n)
    slab = jnp.clip(partner, 0, n - 1)
    place = lax.broadcasted_iota(jnp.int32, (1, p), 1)
    top[...] = jnp.full_like(top, NEG)
    acc[...] = jnp.zeros_like(acc)
    vals[2 * by] = jnp.zeros(vals.shape[1:], BF16)
    copies[0].wait()
    copies[1].wait()
    pairs, _ = list_pairs(
        items, flags, by, [(0, None, 0, by, 0, True), (side, exists, 0, by, by, False)]
    )
    other = me - side
    there = (other >= 0) & (other < n)
    beyond = jnp.clip(other, 0, n - 1)
    for plan, j0, j1 in ((plan0, 0, split), (plan1, split, by)):
        plan[3, 0], _ = list_pairs(plan, flags, by, [(-side, there, j0, j1, 0, False)])
        for i in range(by):
            plan[3, 1 + i] = live[i, 0, me]
        for j in range(j0, j1):
            plan[3, 1 + by + j - j0] = live[j, 0, beyond]
    zeros = jnp.zeros((hd, p), BF16)
    copies[2].wait()
    mine, theirs = own[...].reshape(by * p, width), near[...].reshape(by * p, width)
    wide = min(256, width)
    for c in range(0, width, wide):
        q = (nn(mine, w_all[:, c : c + wide]).astype(BF16) * BF16(1.0 / hd**0.5)).astype(F32)
        for i in range(by):
            t = q[i * p : (i + 1) * p].T.astype(BF16)
            for u in range(wide // depth):
                g, mid = c // depth + u, u * depth + hd
                qt[i, g, :hd, :p] = t[mid - hd : mid]
                qt[i, g, :hd, p:] = zeros
                qt[i, g, hd:, :p] = zeros
                qt[i, g, hd:, p:] = t[mid : mid + hd]
    put_blocks(0, mine, w_all, keys, vals, [place < live[i, 0, me] for i in range(by)])
    put_blocks(by, theirs, w_all, keys, vals, [place < live[i, 0, slab] for i in range(by)])
    items[3, 0] = (pairs * 11) >> 4
    items[3, 1] = pairs
    attend(items, 0, items[3, 0], keys, vals, qt, top, acc, scores, peaks)
    copies[3].wait()


def more_kernel(qt, keys, vals, top_in, acc_in, items, top, acc, scores, peaks):
    attend(items, items[3, 0], items[3, 1], keys, vals, qt, top, acc, scores, peaks)


def far_work(rim, w_all, qt, plan, top, acc, keys, vals, scores, peaks):
    by = qt.shape[0]
    blocks, p, width = rim.shape
    place = lax.broadcasted_iota(jnp.int32, (1, p), 1)
    vals[blocks] = jnp.zeros(vals.shape[1:], BF16)
    put_blocks(0, rim[...].reshape(blocks * p, width), w_all, keys, vals, [place < plan[3, 1 + by + j] for j in range(blocks)])
    attend(plan, 0, plan[3, 0], keys, vals, qt, top, acc, scores, peaks)


def far_kernel(
    rim, norm, w_all, qt, top_in, acc_in, tiled, w_out, plan, top, acc, held, keys, vals, scores, peaks, nrm
):
    for j in range(rim.shape[0]):
        nrm[j] = normalise(rim[j], norm[0:1], norm[1:2])
    far_work(nrm, w_all, qt, plan, top, acc, keys, vals, scores, peaks)
    for i in range(held.shape[0]):
        held[i] = finish(i, tiled, acc, w_out, plan[3, 1 + i])


def last_kernel(
    rim_a, rim_b, w_all, qt, top_in, acc_in, tiled, w_out, held, plan, top, acc, result, keys, vals, scores, peaks, out,
    rim, sems
):
    by, early = tiled.shape[0], held.shape[0]
    copies = [pltpu.make_async_copy(held.at[i], result.at[0, i, 0], sems.at[i]) for i in range(early)]
    for copy in copies:
        copy.start()
    rim[...] = jnp.where(in_first_class(lax.axis_index("gx")), rim_a[...], rim_b[...])
    far_work(rim, w_all, qt, plan, top, acc, keys, vals, scores, peaks)
    for i in range(early, by):
        out[i - early] = finish(i, tiled, acc, w_out, plan[3, 1 + i])
        copies.append(pltpu.make_async_copy(out.at[i - early], result.at[0, i, 0], sems.at[i]))
        copies[-1].start()
    for copy in copies:
        copy.wait()


def vmem(x):
    return pltpu.with_memory_space_constraint(x, pltpu.VMEM)


def smem(x):
    return pltpu.with_memory_space_constraint(x, pltpu.SMEM)


def hbm(x):
    return pltpu.with_memory_space_constraint(x, pltpu.HBM)


def shards(n, points, order, masks, counts, gain, shift_bias, w_qkv, w_out):
    _, by, bz, p, width = points.shape
    hd = width // HEADS
    groups, depth, lanes = HEADS // 2, 2 * hd, 2 * p
    split = max(by - 2, 1)
    early = max(split - 1, 1)
    whole = pl.BlockSpec(memory_space=pltpu.VMEM)
    apart = pl.BlockSpec(memory_space=pltpu.HBM)
    words = pl.BlockSpec(memory_space=pltpu.SMEM)
    plan = pltpu.SMEM((4, 8 * by), jnp.int32)
    params = pltpu.CompilerParams(vmem_limit_bytes=LIMIT)
    points, order, masks, w_qkv, w_out = map(hbm, (points, order, masks, w_qkv, w_out))
    counts = hbm(jnp.transpose(counts, (1, 2, 0)))
    live = pltpu.SMEM(counts.shape, jnp.int32)
    flags = pltpu.SMEM(masks.shape, jnp.int32)

    first, rest, places, norm = pl.pallas_call(
        gather_kernel,
        out_shape=(
            pltpu.VMEM((split, p, width), BF16),
            pltpu.VMEM((by - split, p, width), BF16),
            pltpu.VMEM((by - split, 1, p), jnp.int32),
            pltpu.VMEM((2, width), F32),
        ),
        in_specs=[apart] * 5,
        out_specs=(whole,) * 4,
        scratch_shapes=[
            pltpu.VMEM((split, p, width), BF16),
            pltpu.VMEM(order.shape, jnp.int32),
            live,
            pltpu.SemaphoreType.DMA((by + 4,)),
        ],
        compiler_params=params,
        name="gather",
    )(points, order, counts, hbm(gain[None]), hbm(shift_bias[None]))
    tile_rest = pl.pallas_call(
        rest_kernel,
        out_shape=(
            pltpu.VMEM((by, p, width), BF16),
            pltpu.VMEM((by, p, width), BF16),
            pltpu.VMEM((by - split, p, width), BF16),
        ),
        in_specs=[whole] * 4,
        out_specs=(whole,) * 3,
        compiler_params=params,
        name="rest",
    )
    tiled, normed, second = tile_rest(vmem(first), vmem(rest), vmem(places), vmem(norm))
    near_pairs = [(i, i ^ 1) for i in range(n) if i ^ 1 < n]
    far_pairs = [(i, i + 1) for i in range(1, n - 1, 2)] + [(i + 1, i) for i in range(1, n - 1, 2)]

    def moved(value, pairs):
        return lax.ppermute(value, "gx", pairs)

    far0 = moved(first, far_pairs)
    near = moved(normed, near_pairs)
    far_a = moved(second, [pair for pair in far_pairs if in_first_class(pair[0])])
    far_b = moved(second, [pair for pair in far_pairs if not in_first_class(pair[0])])

    state = (
        pltpu.VMEM((by, 1, groups * lanes), F32),
        pltpu.VMEM((by, hd + 8, groups * lanes), F32),
    )

    def scratch(tiles):
        return [
            pltpu.VMEM((tiles, p, width), BF16),
            pltpu.VMEM((tiles + 1, groups, depth + 2 * ONES, p), BF16),
        ]

    ahead = [
        pltpu.VMEM((2 * p, groups * lanes), F32),
        pltpu.VMEM((1, groups * lanes), F32),
    ]
    main = pl.pallas_call(
        functools.partial(main_kernel, n, split),
        out_shape=(
            pltpu.VMEM((by, groups, depth, lanes), BF16),
            *state,
            pltpu.VMEM(w_qkv.shape, BF16),
            pltpu.VMEM(w_out.shape, BF16),
            plan,
            plan,
            *scratch(2 * by),
            plan,
        ),
        in_specs=[whole, whole, apart, apart, apart, apart],
        out_specs=(*(whole,) * 5, words, words, whole, whole, words),
        scratch_shapes=[flags, live, *ahead, pltpu.SemaphoreType.DMA((4,))],
        compiler_params=params,
        name="main",
    )
    more = pl.pallas_call(
        more_kernel,
        out_shape=state,
        in_specs=[*(whole,) * 5, words],
        out_specs=(whole,) * 2,
        scratch_shapes=ahead,
        input_output_aliases={3: 0, 4: 1},
        compiler_params=params,
        name="more",
    )
    qt, top, acc, w_all, w_last, plan0, plan1, keys, vals, items = main(
        vmem(normed), vmem(near), masks, counts, w_qkv, w_out
    )
    top, acc = more(*map(vmem, (qt, keys, vals, top, acc)), smem(items))
    ins = [far0, norm, w_all, qt, top, acc, tiled, w_last]
    top, acc, held = pl.pallas_call(
        far_kernel,
        out_shape=(*state, pltpu.VMEM((early, p, width), BF16)),
        in_specs=[*(whole,) * len(ins), words],
        out_specs=(whole,) * 3,
        scratch_shapes=[*scratch(split), *ahead, pltpu.VMEM((split, p, width), BF16)],
        input_output_aliases={4: 0, 5: 1},
        compiler_params=params,
        name="far",
    )(*map(vmem, ins), smem(plan0))
    ins = [far_a, far_b, w_all, qt, top, acc, tiled, w_last, held]
    _, _, result = pl.pallas_call(
        last_kernel,
        out_shape=(*state, pltpu.HBM((1, by, bz, p, width), BF16)),
        in_specs=[*(whole,) * len(ins), words],
        out_specs=(whole, whole, apart),
        scratch_shapes=[
            *scratch(by - split),
            *ahead,
            pltpu.VMEM((by - early, p, width), BF16),
            pltpu.VMEM((by - split, p, width), BF16),
            pltpu.SemaphoreType.DMA((by,)),
        ],
        input_output_aliases={4: 0, 5: 1},
        compiler_params=params,
        name="last",
    )(*map(vmem, ins), smem(plan1))
    return result


def solution(mesh):
    placed = (
        P(("groups", "gx"), None, None, None, None),
        P(("groups", "gx"), None, None, None),
        P(("groups", "gx"), None, None, None),
        P("groups", None, None),
        P(),
        P(),
        P(),
        P(),
    )
    return jax.shard_map(
        functools.partial(shards, mesh.shape["gx"]),
        mesh=mesh,
        in_specs=placed,
        out_specs=P(("groups", "gx"), None, None, None, None),
        check_vma=False,
    )
```

```python
import functools

import jax
import jax.numpy as jnp
from jax import lax
from jax.experimental import pallas as pl
from jax.experimental.pallas import tpu as pltpu
from jax.sharding import PartitionSpec as P


HEADS = 8
NEG = -1e30
ONES = 16
LIMIT = 24 * 1024 * 1024
BF16, F32 = jnp.bfloat16, jnp.float32


def tn(a, b):
    return lax.dot_general(a, b, (((0,), (0,)), ((), ())), preferred_element_type=F32)


def nn(a, b):
    return jnp.dot(a, b, preferred_element_type=F32)


def normalise(tiled, gain, shift):
    values = tiled.astype(F32)
    mean = jnp.mean(values, axis=-1, keepdims=True)
    var = jnp.mean((values - mean) ** 2, axis=-1, keepdims=True)
    return ((values - mean) * lax.rsqrt(var + 1e-05) * gain + shift).astype(BF16)


def select(row, raw):
    p = raw.shape[0]
    slot = lax.broadcasted_iota(jnp.int32, (p, p), 0)
    return tn((slot == row).astype(F32).astype(BF16), raw).astype(BF16)


def gather_kernel(points, order, counts, gain, shift, first, rest, places, norm, raw, rows, live, sems):
    _, by, _, p, _ = points.shape
    split = first.shape[0]
    me = lax.axis_index("gx")
    small = [
        pltpu.make_async_copy(order, rows, sems.at[by]),
        pltpu.make_async_copy(counts, live, sems.at[by + 1]),
        pltpu.make_async_copy(gain, norm.at[0:1], sems.at[by + 2]),
        pltpu.make_async_copy(shift, norm.at[1:2], sems.at[by + 3]),
    ]
    large = [
        pltpu.make_async_copy(
            points.at[0, j, 0], raw.at[j] if j < split else rest.at[j - split], sems.at[j]
        )
        for j in range(by)
    ]
    for copy in (*small[:2], *large, *small[2:]):
        copy.start()
    place = lax.broadcasted_iota(jnp.int32, (1, p), 1)
    small[0].wait()
    small[1].wait()
    picks = []
    for j in range(by):
        row = rows[0, j]
        picks.append(jnp.where(place < live[j, 0, me], row, row[:, :1]))
        if j >= split:
            places[j - split] = picks[j]
    for j in range(split):
        large[j].wait()
    for j in range(split):
        first[j] = select(picks[j], raw[j])
    for copy in (*large[split:], *small[2:]):
        copy.wait()


def rest_kernel(first, rest, places, norm, tiled, normed, second):
    split = first.shape[0]
    gain, shift = norm[0:1], norm[1:2]
    for j in range(rest.shape[0]):
        got = select(places[j], rest[j])
        tiled[split + j] = got
        got = normalise(got, gain, shift)
        second[j] = got
        normed[split + j] = got
    for j in range(split):
        got = first[j]
        tiled[j] = got
        normed[j] = normalise(got, gain, shift)


def toward_near():
    return 1 - 2 * (lax.axis_index("gx") & 1)


def column(side, b):
    index = 9 * (side + 1) + 3 * (b + 1) + 1
    if isinstance(index, int):
        return index if index < 13 else index - 1
    return jnp.where(index > 13, index - 1, index)


def list_pairs(items, masks, by, sides):
    spare = sum(j1 - j0 for _, _, j0, j1, _, _ in sides)
    pairs = jnp.int32(0)
    for i in range(by):
        start, found, last = pairs, jnp.int32(0), jnp.int32(0)
        most = 0
        for side, exists, j0, j1, tile0, own in sides:
            for b in (0, -1, 1):
                j = i + b
                if not j0 <= j < j1:
                    continue
                tile = tile0 + j - j0
                items[1, 2 * start + found] = tile
                items[2, 2 * start + found] = tile
                most += 1
                if own and b == 0:
                    found = found + 1
                    last = jnp.int32(tile)
                    continue
                on = masks[0, i, 0, column(side, b)] == 1
                on = on if exists is None else on & exists
                found = found + on.astype(jnp.int32)
                last = jnp.where(on, tile, last)
        items[1, 2 * start + found] = last
        items[2, 2 * start + found] = spare
        for u in range((most + 1) // 2):
            items[0, start + u] = i
        pairs = start + ((found + 1) >> 1)
    items[0, pairs] = 0
    for u in range(2):
        items[1, 2 * pairs + u] = 0
    return pairs


def attend(items, high, keys, vals, qt, top, acc, scores, peaks):
    groups, depth, lanes = qt.shape[1:]
    hd, p = depth // 2, lanes // 2

    def score(t, g):
        i, k0, k1 = items[0, t], items[1, 2 * t], items[1, 2 * t + 1]
        rows = slice(g * depth, (g + 1) * depth)
        cols = slice(g * lanes, (g + 1) * lanes)
        s0 = nn(keys[k0, :, rows], qt[i, g])
        s1 = nn(keys[k1, :, rows], qt[i, g])
        scores[:p, cols] = s0
        scores[p:, cols] = s1
        peaks[:, cols] = jnp.max(jnp.maximum(s0, s1), axis=0, keepdims=True)

    def weigh(t, g):
        i, v0, v1 = items[0, t], items[2, 2 * t], items[2, 2 * t + 1]
        cols = slice(g * lanes, (g + 1) * lanes)
        old = top[i, :, cols]
        new = jnp.maximum(old, peaks[:, cols])
        probs = jnp.exp(scores[:, cols] - new).astype(BF16)
        fade = jnp.exp(old - new)
        both, sums = [], []
        for h in range(2):
            rows = slice(h * (hd + ONES), (h + 1) * (hd + ONES))
            val = jnp.concatenate([vals[v0, g, rows], vals[v1, g, rows]], axis=1)
            out = nn(val, probs[:, h * p : (h + 1) * p])
            both.append(out[:hd])
            sums.append(out[hd : hd + 8])
        return cols, new, fade, jnp.concatenate(both, axis=1), jnp.concatenate(sums, axis=1)

    lead = groups // 2

    def step(t, carry):
        made = []
        for g in range(0, groups, lead):
            for u in range(g, g + lead):
                score(t + (u + lead) // groups, (u + lead) % groups)
            for u in range(g, g + lead):
                made.append(weigh(t, u))
        i = items[0, t]
        for cols, new, fade, both, sums in made:
            top[i, :, cols] = new
            acc[i, :hd, cols] = acc[i, :hd, cols] * fade + both
            acc[i, hd:, cols] = acc[i, hd:, cols] * fade + sums
        return carry

    for g in range(lead):
        score(0, g)
    lax.fori_loop(0, high, step, 0)


def put_values(vals, tile, g0, v, live):
    p = vals.shape[3]
    hd = vals.shape[2] // 2 - ONES
    flag = jnp.broadcast_to(live.astype(F32).astype(BF16), (ONES, p))
    vt = jnp.where(live, v.T, 0.0).astype(BF16)
    for h in range(v.shape[1] // hd):
        g, r = g0 + h // 2, h % 2 * (hd + ONES)
        vals[tile, g, r : r + hd] = vt[h * hd : (h + 1) * hd]
        vals[tile, g, r + hd : r + hd + ONES] = flag


def put_blocks(tile0, x, w_all, keys, vals, lives):
    p, width = keys.shape[1:]
    wide = min(256, width)
    groups = vals.shape[1]
    for c in range(0, width, wide):
        k = nn(x, w_all[:, width + c : width + c + wide]).astype(BF16)
        v = nn(x, w_all[:, 2 * width + c : 2 * width + c + wide])
        for u, live in enumerate(lives):
            rows = slice(u * p, (u + 1) * p)
            keys[tile0 + u, :, c : c + wide] = k[rows]
            put_values(vals, tile0 + u, c * groups // width, v[rows], live)


def finish(i, tiled, acc, w_out, alive):
    hd = acc.shape[1] - 8
    p = tiled.shape[1]
    heads = acc.shape[2] // p
    attn = acc[i, :hd] * (1.0 / acc[i, hd : hd + 1])
    attn = jnp.concatenate([attn[:, h * p : (h + 1) * p] for h in range(heads)], axis=0).astype(BF16)
    mixed = tiled[i].astype(F32) + tn(attn, w_out[...])
    place = lax.broadcasted_iota(jnp.int32, (p, 1), 0)
    return jnp.where(place < alive, mixed, 0.0).astype(BF16)


def own_kernel(
    n, split, own, masks, counts, w_qkv, w_out, qt, top, acc, w_all, w_last, plan_near, plan0, plan1, keys, vals,
    items, flags, live, scores, peaks, sems
):
    by, p, width = own.shape
    _, depth = qt.shape[1:3]
    hd = depth // 2
    copies = [
        pltpu.make_async_copy(masks, flags, sems.at[0]),
        pltpu.make_async_copy(counts, live, sems.at[1]),
        pltpu.make_async_copy(w_qkv, w_all, sems.at[2]),
        pltpu.make_async_copy(w_out, w_last, sems.at[3]),
    ]
    for copy in copies:
        copy.start()
    me = lax.axis_index("gx")
    side = toward_near()
    place = lax.broadcasted_iota(jnp.int32, (1, p), 1)
    top[...] = jnp.full_like(top, NEG)
    acc[...] = jnp.zeros_like(acc)
    vals[by] = jnp.zeros(vals.shape[1:], BF16)
    copies[0].wait()
    copies[1].wait()
    pairs = list_pairs(items, flags, by, [(0, None, 0, by, 0, True)])
    for plan, a, j0, j1 in ((plan_near, side, 0, by), (plan0, -side, 0, split), (plan1, -side, split, by)):
        there = (me + a >= 0) & (me + a < n)
        slab = jnp.clip(me + a, 0, n - 1)
        plan[3, 0] = list_pairs(plan, flags, by, [(a, there, j0, j1, 0, False)])
        for i in range(by):
            plan[3, 1 + i] = live[i, 0, me]
        for j in range(j0, j1):
            plan[3, 1 + by + j - j0] = live[j, 0, slab]
    zeros = jnp.zeros((hd, p), BF16)
    copies[2].wait()
    mine = own[...].reshape(by * p, width)
    wide = min(256, width)
    for c in range(0, width, wide):
        q = (nn(mine, w_all[:, c : c + wide]).astype(BF16) * BF16(1.0 / hd**0.5)).astype(F32)
        for i in range(by):
            t = q[i * p : (i + 1) * p].T.astype(BF16)
            for u in range(wide // depth):
                g, mid = c // depth + u, u * depth + hd
                qt[i, g, :hd, :p] = t[mid - hd : mid]
                qt[i, g, :hd, p:] = zeros
                qt[i, g, hd:, :p] = zeros
                qt[i, g, hd:, p:] = t[mid : mid + hd]
    put_blocks(0, mine, w_all, keys, vals, [place < live[i, 0, me] for i in range(by)])
    attend(items, pairs, keys, vals, qt, top, acc, scores, peaks)
    copies[3].wait()


def far_work(rim, w_all, qt, plan, top, acc, keys, vals, scores, peaks):
    by = qt.shape[0]
    blocks, p, width = rim.shape
    place = lax.broadcasted_iota(jnp.int32, (1, p), 1)
    vals[blocks] = jnp.zeros(vals.shape[1:], BF16)
    put_blocks(0, rim[...].reshape(blocks * p, width), w_all, keys, vals, [place < plan[3, 1 + by + j] for j in range(blocks)])
    attend(plan, plan[3, 0], keys, vals, qt, top, acc, scores, peaks)


def near_kernel(rim, w_all, qt, top_in, acc_in, plan, top, acc, keys, vals, scores, peaks):
    far_work(rim, w_all, qt, plan, top, acc, keys, vals, scores, peaks)


def far_kernel(
    rim, norm, w_all, qt, top_in, acc_in, tiled, w_out, plan, top, acc, held, keys, vals, scores, peaks, nrm
):
    for j in range(rim.shape[0]):
        nrm[j] = normalise(rim[j], norm[0:1], norm[1:2])
    far_work(nrm, w_all, qt, plan, top, acc, keys, vals, scores, peaks)
    for i in range(held.shape[0]):
        held[i] = finish(i, tiled, acc, w_out, plan[3, 1 + i])


def last_kernel(
    rim, w_all, qt, top_in, acc_in, tiled, w_out, held, plan, top, acc, result, keys, vals, scores, peaks, out,
    sems
):
    by, early = tiled.shape[0], held.shape[0]
    copies = [pltpu.make_async_copy(held.at[i], result.at[0, i, 0], sems.at[i]) for i in range(early)]
    for copy in copies:
        copy.start()
    far_work(rim, w_all, qt, plan, top, acc, keys, vals, scores, peaks)
    for i in range(early, by):
        out[i - early] = finish(i, tiled, acc, w_out, plan[3, 1 + i])
        copies.append(pltpu.make_async_copy(out.at[i - early], result.at[0, i, 0], sems.at[i]))
        copies[-1].start()
    for copy in copies:
        copy.wait()


def vmem(x):
    return pltpu.with_memory_space_constraint(x, pltpu.VMEM)


def smem(x):
    return pltpu.with_memory_space_constraint(x, pltpu.SMEM)


def hbm(x):
    return pltpu.with_memory_space_constraint(x, pltpu.HBM)


def shards(n, points, order, masks, counts, gain, shift_bias, w_qkv, w_out):
    _, by, bz, p, width = points.shape
    hd = width // HEADS
    groups, depth, lanes = HEADS // 2, 2 * hd, 2 * p
    split = max(by - 2, 1)
    early = max(split - 1, 1)
    whole = pl.BlockSpec(memory_space=pltpu.VMEM)
    apart = pl.BlockSpec(memory_space=pltpu.HBM)
    words = pl.BlockSpec(memory_space=pltpu.SMEM)
    plan = pltpu.SMEM((4, 8 * by), jnp.int32)
    params = pltpu.CompilerParams(vmem_limit_bytes=LIMIT)
    points, order, masks, w_qkv, w_out = map(hbm, (points, order, masks, w_qkv, w_out))
    counts = hbm(jnp.transpose(counts, (1, 2, 0)))
    live = pltpu.SMEM(counts.shape, jnp.int32)
    flags = pltpu.SMEM(masks.shape, jnp.int32)

    first, rest, places, norm = pl.pallas_call(
        gather_kernel,
        out_shape=(
            pltpu.VMEM((split, p, width), BF16),
            pltpu.VMEM((by - split, p, width), BF16),
            pltpu.VMEM((by - split, 1, p), jnp.int32),
            pltpu.VMEM((2, width), F32),
        ),
        in_specs=[apart] * 5,
        out_specs=(whole,) * 4,
        scratch_shapes=[
            pltpu.VMEM((split, p, width), BF16),
            pltpu.VMEM(order.shape, jnp.int32),
            live,
            pltpu.SemaphoreType.DMA((by + 4,)),
        ],
        compiler_params=params,
        name="gather",
    )(points, order, counts, hbm(gain[None]), hbm(shift_bias[None]))
    tile_rest = pl.pallas_call(
        rest_kernel,
        out_shape=(
            pltpu.VMEM((by, p, width), BF16),
            pltpu.VMEM((by, p, width), BF16),
            pltpu.VMEM((by - split, p, width), BF16),
        ),
        in_specs=[whole] * 4,
        out_specs=(whole,) * 3,
        compiler_params=params,
        name="rest",
    )
    tiled, normed, second = tile_rest(vmem(first), vmem(rest), vmem(places), vmem(norm))
    near_pairs = [(i, i ^ 1) for i in range(n) if i ^ 1 < n]
    far_pairs = [(i, i + 1) for i in range(1, n - 1, 2)] + [(i + 1, i) for i in range(1, n - 1, 2)]

    def moved(value, pairs):
        return lax.ppermute(value, "gx", pairs)

    far0 = moved(first, far_pairs)
    near = moved(normed, near_pairs)
    far1 = moved(second, far_pairs)

    state = (
        pltpu.VMEM((by, 1, groups * lanes), F32),
        pltpu.VMEM((by, hd + 8, groups * lanes), F32),
    )

    def scratch(tiles):
        return [
            pltpu.VMEM((tiles, p, width), BF16),
            pltpu.VMEM((tiles + 1, groups, depth + 2 * ONES, p), BF16),
        ]

    ahead = [
        pltpu.VMEM((2 * p, groups * lanes), F32),
        pltpu.VMEM((1, groups * lanes), F32),
    ]
    own_work = pl.pallas_call(
        functools.partial(own_kernel, n, split),
        out_shape=(
            pltpu.VMEM((by, groups, depth, lanes), BF16),
            *state,
            pltpu.VMEM(w_qkv.shape, BF16),
            pltpu.VMEM(w_out.shape, BF16),
            *(plan,) * 3,
        ),
        in_specs=[whole, apart, apart, apart, apart],
        out_specs=(whole,) * 5 + (words,) * 3,
        scratch_shapes=[*scratch(by), plan, flags, live, *ahead, pltpu.SemaphoreType.DMA((4,))],
        compiler_params=params,
        name="own",
    )
    near_work = pl.pallas_call(
        near_kernel,
        out_shape=state,
        in_specs=[*(whole,) * 5, words],
        out_specs=(whole,) * 2,
        scratch_shapes=[*scratch(by), *ahead],
        input_output_aliases={3: 0, 4: 1},
        compiler_params=params,
        name="near",
    )
    qt, top, acc, w_all, w_last, plan_near, plan0, plan1 = own_work(
        vmem(normed), masks, counts, w_qkv, w_out
    )
    top, acc = near_work(*map(vmem, (near, w_all, qt, top, acc)), smem(plan_near))
    ins = [far0, norm, w_all, qt, top, acc, tiled, w_last]
    top, acc, held = pl.pallas_call(
        far_kernel,
        out_shape=(*state, pltpu.VMEM((early, p, width), BF16)),
        in_specs=[*(whole,) * len(ins), words],
        out_specs=(whole,) * 3,
        scratch_shapes=[*scratch(split), *ahead, pltpu.VMEM((split, p, width), BF16)],
        input_output_aliases={4: 0, 5: 1},
        compiler_params=params,
        name="far",
    )(*map(vmem, ins), smem(plan0))
    ins = [far1, w_all, qt, top, acc, tiled, w_last, held]
    _, _, result = pl.pallas_call(
        last_kernel,
        out_shape=(*state, pltpu.HBM((1, by, bz, p, width), BF16)),
        in_specs=[*(whole,) * len(ins), words],
        out_specs=(whole, whole, apart),
        scratch_shapes=[
            *scratch(by - split),
            *ahead,
            pltpu.VMEM((by - early, p, width), BF16),
            pltpu.SemaphoreType.DMA((by,)),
        ],
        input_output_aliases={3: 0, 4: 1},
        compiler_params=params,
        name="last",
    )(*map(vmem, ins), smem(plan1))
    return result


def solution(mesh):
    placed = (
        P(("groups", "gx"), None, None, None, None),
        P(("groups", "gx"), None, None, None),
        P(("groups", "gx"), None, None, None),
        P("groups", None, None),
        P(),
        P(),
        P(),
        P(),
    )
    return jax.shard_map(
        functools.partial(shards, mesh.shape["gx"]),
        mesh=mesh,
        in_specs=placed,
        out_specs=P(("groups", "gx"), None, None, None, None),
        check_vma=False,
    )
```

```python
import functools

import jax
import jax.numpy as jnp
from jax import lax
from jax.experimental import pallas as pl
from jax.experimental.pallas import tpu as pltpu
from jax.sharding import PartitionSpec as P


HEADS = 8
NEG = -1e30
ONES = 16
LIMIT = 24 * 1024 * 1024
BF16, F32 = jnp.bfloat16, jnp.float32


def tn(a, b):
    return lax.dot_general(a, b, (((0,), (0,)), ((), ())), preferred_element_type=F32)


def nn(a, b):
    return jnp.dot(a, b, preferred_element_type=F32)


def normalise(tiled, gain, shift):
    values = tiled.astype(F32)
    mean = jnp.mean(values, axis=-1, keepdims=True)
    var = jnp.mean((values - mean) ** 2, axis=-1, keepdims=True)
    return ((values - mean) * lax.rsqrt(var + 1e-05) * gain + shift).astype(BF16)


def select(row, raw):
    p = raw.shape[0]
    slot = lax.broadcasted_iota(jnp.int32, (p, p), 0)
    return tn((slot == row).astype(F32).astype(BF16), raw).astype(BF16)


def gather_kernel(points, order, counts, gain, shift, first, rest, places, norm, raw, rows, live, sems):
    _, by, _, p, _ = points.shape
    split = first.shape[0]
    me = lax.axis_index("gx")
    small = [
        pltpu.make_async_copy(order, rows, sems.at[by]),
        pltpu.make_async_copy(counts, live, sems.at[by + 1]),
        pltpu.make_async_copy(gain, norm.at[0:1], sems.at[by + 2]),
        pltpu.make_async_copy(shift, norm.at[1:2], sems.at[by + 3]),
    ]
    large = [
        pltpu.make_async_copy(
            points.at[0, j, 0], raw.at[j] if j < split else rest.at[j - split], sems.at[j]
        )
        for j in range(by)
    ]
    for copy in (*small[:2], *large, *small[2:]):
        copy.start()
    place = lax.broadcasted_iota(jnp.int32, (1, p), 1)
    small[0].wait()
    small[1].wait()
    picks = []
    for j in range(by):
        row = rows[0, j]
        picks.append(jnp.where(place < live[j, 0, me], row, row[:, :1]))
        if j >= split:
            places[j - split] = picks[j]
    for j in range(split):
        large[j].wait()
    for j in range(split):
        first[j] = select(picks[j], raw[j])
    for copy in (*large[split:], *small[2:]):
        copy.wait()


def rest_kernel(first, rest, places, norm, tiled, normed, second):
    split = first.shape[0]
    gain, shift = norm[0:1], norm[1:2]
    for j in range(rest.shape[0]):
        got = select(places[j], rest[j])
        tiled[split + j] = got
        got = normalise(got, gain, shift)
        second[j] = got
        normed[split + j] = got
    for j in range(split):
        got = first[j]
        tiled[j] = got
        normed[j] = normalise(got, gain, shift)


def toward_near():
    return 1 - 2 * (lax.axis_index("gx") & 1)


def column(side, b):
    index = 9 * (side + 1) + 3 * (b + 1) + 1
    if isinstance(index, int):
        return index if index < 13 else index - 1
    return jnp.where(index > 13, index - 1, index)


def list_pairs(items, masks, by, sides):
    pairs, singles = jnp.int32(0), jnp.int32(0)
    for i in range(by):
        found, last, most = jnp.int32(0), jnp.int32(0), 0
        for side, exists, j0, j1, tile0, own in sides:
            for b in (0, -1, 1):
                j = i + b
                if not j0 <= j < j1:
                    continue
                tile = tile0 + j - j0
                items[1, 2 * pairs + found] = tile
                most += 1
                if own and b == 0:
                    found = found + 1
                    last = jnp.int32(tile)
                    continue
                on = masks[0, i, 0, column(side, b)] == 1
                on = on if exists is None else on & exists
                found = found + on.astype(jnp.int32)
                last = jnp.where(on, tile, last)
        items[2, 2 * singles] = i
        items[2, 2 * singles + 1] = last
        for u in range(most // 2):
            items[0, pairs + u] = i
        pairs = pairs + (found >> 1)
        singles = singles + (found & 1)
    items[0, pairs] = 0
    for u in range(2):
        items[1, 2 * pairs + u] = 0
        items[2, 2 * singles + u] = 0
    return pairs, singles


def attend(items, pairs, singles, keys, vals, qt, top, acc, scores, peaks):
    groups, depth, lanes = qt.shape[1:]
    hd, p = depth // 2, lanes // 2
    lead = groups // 2

    def run(count, tiles, entry):
        def score(t, g):
            i, picked = entry(t)
            rows = slice(g * depth, (g + 1) * depth)
            cols = slice(g * lanes, (g + 1) * lanes)
            peak = None
            for u, k in enumerate(picked):
                made = nn(keys[k, :, rows], qt[i, g])
                scores[u * p : (u + 1) * p, cols] = made
                peak = made if peak is None else jnp.maximum(peak, made)
            peaks[:, cols] = jnp.max(peak, axis=0, keepdims=True)

        def weigh(t, g):
            i, picked = entry(t)
            cols = slice(g * lanes, (g + 1) * lanes)
            old = top[i, :, cols]
            new = jnp.maximum(old, peaks[:, cols])
            probs = jnp.exp(scores[: tiles * p, cols] - new).astype(BF16)
            fade = jnp.exp(old - new)
            both, sums = [], []
            for h in range(2):
                rows = slice(h * (hd + ONES), (h + 1) * (hd + ONES))
                val = jnp.concatenate([vals[k, g, rows] for k in picked], axis=1)
                out = nn(val, probs[:, h * p : (h + 1) * p])
                both.append(out[:hd])
                sums.append(out[hd : hd + 8])
            return cols, new, fade, jnp.concatenate(both, axis=1), jnp.concatenate(sums, axis=1)

        def step(t, carry):
            made = []
            for g in range(0, groups, lead):
                for u in range(g, g + lead):
                    score(t + (u + lead) // groups, (u + lead) % groups)
                for u in range(g, g + lead):
                    made.append(weigh(t, u))
            i, _ = entry(t)
            for cols, new, fade, both, sums in made:
                top[i, :, cols] = new
                acc[i, :hd, cols] = acc[i, :hd, cols] * fade + both
                acc[i, hd:, cols] = acc[i, hd:, cols] * fade + sums
            return carry

        for g in range(lead):
            score(0, g)
        lax.fori_loop(0, count, step, 0)

    run(pairs, 2, lambda t: (items[0, t], (items[1, 2 * t], items[1, 2 * t + 1])))
    run(singles, 1, lambda t: (items[2, 2 * t], (items[2, 2 * t + 1],)))


def put_values(vals, tile, g0, v, live):
    p = vals.shape[3]
    hd = vals.shape[2] // 2 - ONES
    flag = jnp.broadcast_to(live.astype(F32).astype(BF16), (ONES, p))
    vt = jnp.where(live, v.T, 0.0).astype(BF16)
    for h in range(v.shape[1] // hd):
        g, r = g0 + h // 2, h % 2 * (hd + ONES)
        vals[tile, g, r : r + hd] = vt[h * hd : (h + 1) * hd]
        vals[tile, g, r + hd : r + hd + ONES] = flag


def put_blocks(tile0, x, w_all, keys, vals, lives):
    p, width = keys.shape[1:]
    wide = min(256, width)
    groups = vals.shape[1]
    for c in range(0, width, wide):
        k = nn(x, w_all[:, width + c : width + c + wide]).astype(BF16)
        v = nn(x, w_all[:, 2 * width + c : 2 * width + c + wide])
        for u, live in enumerate(lives):
            rows = slice(u * p, (u + 1) * p)
            keys[tile0 + u, :, c : c + wide] = k[rows]
            put_values(vals, tile0 + u, c * groups // width, v[rows], live)


def finish(i, tiled, acc, w_out, alive):
    hd = acc.shape[1] - 8
    p = tiled.shape[1]
    heads = acc.shape[2] // p
    attn = acc[i, :hd] * (1.0 / acc[i, hd : hd + 1])
    attn = jnp.concatenate([attn[:, h * p : (h + 1) * p] for h in range(heads)], axis=0).astype(BF16)
    mixed = tiled[i].astype(F32) + tn(attn, w_out[...])
    place = lax.broadcasted_iota(jnp.int32, (p, 1), 0)
    return jnp.where(place < alive, mixed, 0.0).astype(BF16)


def own_kernel(
    n, split, own, masks, counts, w_qkv, w_out, qt, top, acc, w_all, w_last, plan_near, plan0, plan1, keys, vals,
    items, flags, live, scores, peaks, sems
):
    by, p, width = own.shape
    _, depth = qt.shape[1:3]
    hd = depth // 2
    copies = [
        pltpu.make_async_copy(masks, flags, sems.at[0]),
        pltpu.make_async_copy(counts, live, sems.at[1]),
        pltpu.make_async_copy(w_qkv, w_all, sems.at[2]),
        pltpu.make_async_copy(w_out, w_last, sems.at[3]),
    ]
    for copy in copies:
        copy.start()
    me = lax.axis_index("gx")
    side = toward_near()
    place = lax.broadcasted_iota(jnp.int32, (1, p), 1)
    top[...] = jnp.full_like(top, NEG)
    acc[...] = jnp.zeros_like(acc)
    copies[0].wait()
    copies[1].wait()
    pairs, singles = list_pairs(items, flags, by, [(0, None, 0, by, 0, True)])
    for plan, a, j0, j1 in ((plan_near, side, 0, by), (plan0, -side, 0, split), (plan1, -side, split, by)):
        there = (me + a >= 0) & (me + a < n)
        slab = jnp.clip(me + a, 0, n - 1)
        plan[3, 0], plan[3, 1 + 2 * by] = list_pairs(plan, flags, by, [(a, there, j0, j1, 0, False)])
        for i in range(by):
            plan[3, 1 + i] = live[i, 0, me]
        for j in range(j0, j1):
            plan[3, 1 + by + j - j0] = live[j, 0, slab]
    zeros = jnp.zeros((hd, p), BF16)
    copies[2].wait()
    mine = own[...].reshape(by * p, width)
    wide = min(256, width)
    for c in range(0, width, wide):
        q = (nn(mine, w_all[:, c : c + wide]).astype(BF16) * BF16(1.0 / hd**0.5)).astype(F32)
        for i in range(by):
            t = q[i * p : (i + 1) * p].T.astype(BF16)
            for u in range(wide // depth):
                g, mid = c // depth + u, u * depth + hd
                qt[i, g, :hd, :p] = t[mid - hd : mid]
                qt[i, g, :hd, p:] = zeros
                qt[i, g, hd:, :p] = zeros
                qt[i, g, hd:, p:] = t[mid : mid + hd]
    put_blocks(0, mine, w_all, keys, vals, [place < live[i, 0, me] for i in range(by)])
    attend(items, pairs, singles, keys, vals, qt, top, acc, scores, peaks)
    copies[3].wait()


def far_work(rim, w_all, qt, plan, top, acc, keys, vals, scores, peaks):
    by = qt.shape[0]
    blocks, p, width = rim.shape
    place = lax.broadcasted_iota(jnp.int32, (1, p), 1)
    put_blocks(0, rim[...].reshape(blocks * p, width), w_all, keys, vals, [place < plan[3, 1 + by + j] for j in range(blocks)])
    attend(plan, plan[3, 0], plan[3, 1 + 2 * by], keys, vals, qt, top, acc, scores, peaks)


def near_kernel(rim, w_all, qt, top_in, acc_in, plan, top, acc, keys, vals, scores, peaks):
    far_work(rim, w_all, qt, plan, top, acc, keys, vals, scores, peaks)


def far_kernel(
    rim, norm, w_all, qt, top_in, acc_in, tiled, w_out, plan, top, acc, held, keys, vals, scores, peaks, nrm
):
    for j in range(rim.shape[0]):
        nrm[j] = normalise(rim[j], norm[0:1], norm[1:2])
    far_work(nrm, w_all, qt, plan, top, acc, keys, vals, scores, peaks)
    for i in range(held.shape[0]):
        held[i] = finish(i, tiled, acc, w_out, plan[3, 1 + i])


def last_kernel(
    rim, w_all, qt, top_in, acc_in, tiled, w_out, held, plan, top, acc, result, keys, vals, scores, peaks, out,
    sems
):
    by, early = tiled.shape[0], held.shape[0]
    copies = [pltpu.make_async_copy(held.at[i], result.at[0, i, 0], sems.at[i]) for i in range(early)]
    for copy in copies:
        copy.start()
    far_work(rim, w_all, qt, plan, top, acc, keys, vals, scores, peaks)
    for i in range(early, by):
        out[i - early] = finish(i, tiled, acc, w_out, plan[3, 1 + i])
        copies.append(pltpu.make_async_copy(out.at[i - early], result.at[0, i, 0], sems.at[i]))
        copies[-1].start()
    for copy in copies:
        copy.wait()


def vmem(x):
    return pltpu.with_memory_space_constraint(x, pltpu.VMEM)


def smem(x):
    return pltpu.with_memory_space_constraint(x, pltpu.SMEM)


def hbm(x):
    return pltpu.with_memory_space_constraint(x, pltpu.HBM)


def shards(n, points, order, masks, counts, gain, shift_bias, w_qkv, w_out):
    _, by, bz, p, width = points.shape
    hd = width // HEADS
    groups, depth, lanes = HEADS // 2, 2 * hd, 2 * p
    split = max(by - 2, 1)
    early = max(split - 1, 1)
    whole = pl.BlockSpec(memory_space=pltpu.VMEM)
    apart = pl.BlockSpec(memory_space=pltpu.HBM)
    words = pl.BlockSpec(memory_space=pltpu.SMEM)
    plan = pltpu.SMEM((4, 8 * by), jnp.int32)
    params = pltpu.CompilerParams(vmem_limit_bytes=LIMIT)
    points, order, masks, w_qkv, w_out = map(hbm, (points, order, masks, w_qkv, w_out))
    counts = hbm(jnp.transpose(counts, (1, 2, 0)))
    live = pltpu.SMEM(counts.shape, jnp.int32)
    flags = pltpu.SMEM(masks.shape, jnp.int32)

    first, rest, places, norm = pl.pallas_call(
        gather_kernel,
        out_shape=(
            pltpu.VMEM((split, p, width), BF16),
            pltpu.VMEM((by - split, p, width), BF16),
            pltpu.VMEM((by - split, 1, p), jnp.int32),
            pltpu.VMEM((2, width), F32),
        ),
        in_specs=[apart] * 5,
        out_specs=(whole,) * 4,
        scratch_shapes=[
            pltpu.VMEM((split, p, width), BF16),
            pltpu.VMEM(order.shape, jnp.int32),
            live,
            pltpu.SemaphoreType.DMA((by + 4,)),
        ],
        compiler_params=params,
        name="gather",
    )(points, order, counts, hbm(gain[None]), hbm(shift_bias[None]))
    tile_rest = pl.pallas_call(
        rest_kernel,
        out_shape=(
            pltpu.VMEM((by, p, width), BF16),
            pltpu.VMEM((by, p, width), BF16),
            pltpu.VMEM((by - split, p, width), BF16),
        ),
        in_specs=[whole] * 4,
        out_specs=(whole,) * 3,
        compiler_params=params,
        name="rest",
    )
    tiled, normed, second = tile_rest(vmem(first), vmem(rest), vmem(places), vmem(norm))
    near_pairs = [(i, i ^ 1) for i in range(n) if i ^ 1 < n]
    far_pairs = [(i, i + 1) for i in range(1, n - 1, 2)] + [(i + 1, i) for i in range(1, n - 1, 2)]

    def moved(value, pairs):
        return lax.ppermute(value, "gx", pairs)

    far0 = moved(first, far_pairs)
    near = moved(normed, near_pairs)
    far1 = moved(second, far_pairs)

    state = (
        pltpu.VMEM((by, 1, groups * lanes), F32),
        pltpu.VMEM((by, hd + 8, groups * lanes), F32),
    )

    def scratch(tiles):
        return [
            pltpu.VMEM((tiles, p, width), BF16),
            pltpu.VMEM((tiles, groups, depth + 2 * ONES, p), BF16),
        ]

    ahead = [
        pltpu.VMEM((2 * p, groups * lanes), F32),
        pltpu.VMEM((1, groups * lanes), F32),
    ]
    own_work = pl.pallas_call(
        functools.partial(own_kernel, n, split),
        out_shape=(
            pltpu.VMEM((by, groups, depth, lanes), BF16),
            *state,
            pltpu.VMEM(w_qkv.shape, BF16),
            pltpu.VMEM(w_out.shape, BF16),
            *(plan,) * 3,
        ),
        in_specs=[whole, apart, apart, apart, apart],
        out_specs=(whole,) * 5 + (words,) * 3,
        scratch_shapes=[*scratch(by), plan, flags, live, *ahead, pltpu.SemaphoreType.DMA((4,))],
        compiler_params=params,
        name="own",
    )
    near_work = pl.pallas_call(
        near_kernel,
        out_shape=state,
        in_specs=[*(whole,) * 5, words],
        out_specs=(whole,) * 2,
        scratch_shapes=[*scratch(by), *ahead],
        input_output_aliases={3: 0, 4: 1},
        compiler_params=params,
        name="near",
    )
    qt, top, acc, w_all, w_last, plan_near, plan0, plan1 = own_work(
        vmem(normed), masks, counts, w_qkv, w_out
    )
    top, acc = near_work(*map(vmem, (near, w_all, qt, top, acc)), smem(plan_near))
    ins = [far0, norm, w_all, qt, top, acc, tiled, w_last]
    top, acc, held = pl.pallas_call(
        far_kernel,
        out_shape=(*state, pltpu.VMEM((early, p, width), BF16)),
        in_specs=[*(whole,) * len(ins), words],
        out_specs=(whole,) * 3,
        scratch_shapes=[*scratch(split), *ahead, pltpu.VMEM((split, p, width), BF16)],
        input_output_aliases={4: 0, 5: 1},
        compiler_params=params,
        name="far",
    )(*map(vmem, ins), smem(plan0))
    ins = [far1, w_all, qt, top, acc, tiled, w_last, held]
    _, _, result = pl.pallas_call(
        last_kernel,
        out_shape=(*state, pltpu.HBM((1, by, bz, p, width), BF16)),
        in_specs=[*(whole,) * len(ins), words],
        out_specs=(whole, whole, apart),
        scratch_shapes=[
            *scratch(by - split),
            *ahead,
            pltpu.VMEM((by - early, p, width), BF16),
            pltpu.SemaphoreType.DMA((by,)),
        ],
        input_output_aliases={3: 0, 4: 1},
        compiler_params=params,
        name="last",
    )(*map(vmem, ins), smem(plan1))
    return result


def solution(mesh):
    placed = (
        P(("groups", "gx"), None, None, None, None),
        P(("groups", "gx"), None, None, None),
        P(("groups", "gx"), None, None, None),
        P("groups", None, None),
        P(),
        P(),
        P(),
        P(),
    )
    return jax.shard_map(
        functools.partial(shards, mesh.shape["gx"]),
        mesh=mesh,
        in_specs=placed,
        out_specs=P(("groups", "gx"), None, None, None, None),
        check_vma=False,
    )
```

```python
import functools

import jax
import jax.numpy as jnp
from jax import lax
from jax.experimental import pallas as pl
from jax.experimental.pallas import tpu as pltpu
from jax.sharding import PartitionSpec as P


HEADS = 8
NEG = -1e30
ONES = 16
LIMIT = 24 * 1024 * 1024
BF16, F32 = jnp.bfloat16, jnp.float32


def tn(a, b):
    return lax.dot_general(a, b, (((0,), (0,)), ((), ())), preferred_element_type=F32)


def nn(a, b):
    return jnp.dot(a, b, preferred_element_type=F32)


def normalise(tiled, gain, shift):
    values = tiled.astype(F32)
    mean = jnp.mean(values, axis=-1, keepdims=True)
    var = jnp.mean((values - mean) ** 2, axis=-1, keepdims=True)
    return ((values - mean) * lax.rsqrt(var + 1e-05) * gain + shift).astype(BF16)


def select(row, raw):
    p = raw.shape[0]
    slot = lax.broadcasted_iota(jnp.int32, (p, p), 0)
    return tn((slot == row).astype(F32).astype(BF16), raw).astype(BF16)


def gather_kernel(points, order, counts, gain, shift, first, rest, places, norm, raw, rows, live, sems):
    _, by, _, p, _ = points.shape
    split = first.shape[0]
    me = lax.axis_index("gx")
    small = [
        pltpu.make_async_copy(order, rows, sems.at[by]),
        pltpu.make_async_copy(counts, live, sems.at[by + 1]),
        pltpu.make_async_copy(gain, norm.at[0:1], sems.at[by + 2]),
        pltpu.make_async_copy(shift, norm.at[1:2], sems.at[by + 3]),
    ]
    large = [
        pltpu.make_async_copy(
            points.at[0, j, 0], raw.at[j] if j < split else rest.at[j - split], sems.at[j]
        )
        for j in range(by)
    ]
    for copy in (*small[:2], *large, *small[2:]):
        copy.start()
    place = lax.broadcasted_iota(jnp.int32, (1, p), 1)
    small[0].wait()
    small[1].wait()
    picks = []
    for j in range(by):
        row = rows[0, j]
        picks.append(jnp.where(place < live[j, 0, me], row, row[:, :1]))
        if j >= split:
            places[j - split] = picks[j]
    for j in range(split):
        large[j].wait()
    for j in range(split):
        first[j] = select(picks[j], raw[j])
    for copy in (*large[split:], *small[2:]):
        copy.wait()


def rest_kernel(first, rest, places, norm, tiled, normed, second):
    split = first.shape[0]
    gain, shift = norm[0:1], norm[1:2]
    for j in range(rest.shape[0]):
        got = select(places[j], rest[j])
        tiled[split + j] = got
        got = normalise(got, gain, shift)
        second[j] = got
        normed[split + j] = got
    for j in range(split):
        got = first[j]
        tiled[j] = got
        normed[j] = normalise(got, gain, shift)


def toward_near():
    return 1 - 2 * (lax.axis_index("gx") & 1)


def column(side, b):
    index = 9 * (side + 1) + 3 * (b + 1) + 1
    if isinstance(index, int):
        return index if index < 13 else index - 1
    return jnp.where(index > 13, index - 1, index)


def list_pairs(items, masks, by, sides):
    pairs, singles = jnp.int32(0), jnp.int32(0)
    for i in range(by):
        found, last, most = jnp.int32(0), jnp.int32(0), 0
        for side, exists, j0, j1, tile0, own in sides:
            for b in (0, -1, 1):
                j = i + b
                if not j0 <= j < j1:
                    continue
                tile = tile0 + j - j0
                items[1, 2 * pairs + found] = tile
                most += 1
                if own and b == 0:
                    found = found + 1
                    last = jnp.int32(tile)
                    continue
                on = masks[0, i, 0, column(side, b)] == 1
                on = on if exists is None else on & exists
                found = found + on.astype(jnp.int32)
                last = jnp.where(on, tile, last)
        items[2, 2 * singles] = i
        items[2, 2 * singles + 1] = last
        for u in range(most // 2):
            items[0, pairs + u] = i
        pairs = pairs + (found >> 1)
        singles = singles + (found & 1)
    items[0, pairs] = 0
    for u in range(2):
        items[1, 2 * pairs + u] = 0
        items[2, 2 * singles + u] = 0
    return pairs, singles


def attend(items, pairs, singles, keys, vals, qt, top, acc, scores, peaks):
    groups, depth, lanes = qt.shape[1:]
    hd, p = depth // 2, lanes // 2
    lead = groups // 2

    def run(count, tiles, entry):
        def score(t, g):
            i, picked = entry(t)
            rows = slice(g * depth, (g + 1) * depth)
            cols = slice(g * lanes, (g + 1) * lanes)
            peak = None
            for u, k in enumerate(picked):
                made = nn(keys[k, :, rows], qt[i, g])
                scores[u * p : (u + 1) * p, cols] = made
                peak = made if peak is None else jnp.maximum(peak, made)
            peaks[:, cols] = jnp.max(peak, axis=0, keepdims=True)

        def weigh(t, g):
            i, picked = entry(t)
            cols = slice(g * lanes, (g + 1) * lanes)
            old = top[i, :, cols]
            new = jnp.maximum(old, peaks[:, cols])
            probs = jnp.exp(scores[: tiles * p, cols] - new).astype(BF16)
            fade = jnp.exp(old - new)
            both, sums = [], []
            for h in range(2):
                rows = slice(h * (hd + ONES), (h + 1) * (hd + ONES))
                val = jnp.concatenate([vals[k, g, rows] for k in picked], axis=1)
                out = nn(val, probs[:, h * p : (h + 1) * p])
                both.append(out[:hd])
                sums.append(out[hd : hd + 8])
            return cols, new, fade, jnp.concatenate(both, axis=1), jnp.concatenate(sums, axis=1)

        def step(t, carry):
            made = []
            for g in range(0, groups, lead):
                for u in range(g, g + lead):
                    score(t + (u + lead) // groups, (u + lead) % groups)
                for u in range(g, g + lead):
                    made.append(weigh(t, u))
            i, _ = entry(t)
            for cols, new, fade, both, sums in made:
                top[i, :, cols] = new
                acc[i, :hd, cols] = acc[i, :hd, cols] * fade + both
                acc[i, hd:, cols] = acc[i, hd:, cols] * fade + sums
            return carry

        for g in range(lead):
            score(0, g)
        lax.fori_loop(0, count, step, 0)

    run(pairs, 2, lambda t: (items[0, t], (items[1, 2 * t], items[1, 2 * t + 1])))
    run(singles, 1, lambda t: (items[2, 2 * t], (items[2, 2 * t + 1],)))


def put_values(vals, tile, g0, v, live):
    p = vals.shape[3]
    hd = vals.shape[2] // 2 - ONES
    flag = jnp.broadcast_to(live.astype(F32).astype(BF16), (ONES, p))
    vt = jnp.where(live, v.T, 0.0).astype(BF16)
    for h in range(v.shape[1] // hd):
        g, r = g0 + h // 2, h % 2 * (hd + ONES)
        vals[tile, g, r : r + hd] = vt[h * hd : (h + 1) * hd]
        vals[tile, g, r + hd : r + hd + ONES] = flag


def put_blocks(tile0, x, w_all, keys, vals, lives):
    p, width = keys.shape[1:]
    wide = min(512, width)
    groups = vals.shape[1]
    for c in range(0, width, wide):
        k = nn(x, w_all[:, width + c : width + c + wide]).astype(BF16)
        v = nn(x, w_all[:, 2 * width + c : 2 * width + c + wide])
        for u, live in enumerate(lives):
            rows = slice(u * p, (u + 1) * p)
            keys[tile0 + u, :, c : c + wide] = k[rows]
            put_values(vals, tile0 + u, c * groups // width, v[rows], live)


def finish(blocks, tiled, acc, w_out, plan):
    hd = acc.shape[1] - 8
    p = tiled.shape[1]
    heads = acc.shape[2] // p
    columns = []
    for i in blocks:
        attn = acc[i, :hd] * (1.0 / acc[i, hd : hd + 1])
        attn = [attn[:, h * p : (h + 1) * p] for h in range(heads)]
        columns.append(jnp.concatenate(attn, axis=0).astype(BF16))
    mixed = tn(jnp.concatenate(columns, axis=1), w_out[...])
    place = lax.broadcasted_iota(jnp.int32, (p, 1), 0)
    made = []
    for u, i in enumerate(blocks):
        value = tiled[i].astype(F32) + mixed[u * p : (u + 1) * p]
        made.append(jnp.where(place < plan[3, 1 + i], value, 0.0).astype(BF16))
    return made


def own_kernel(
    n, split, own, masks, counts, w_qkv, w_out, qt, top, acc, w_all, w_last, plan_near, plan0, plan1, keys, vals,
    items, flags, live, scores, peaks, sems
):
    by, p, width = own.shape
    _, depth = qt.shape[1:3]
    hd = depth // 2
    copies = [
        pltpu.make_async_copy(masks, flags, sems.at[0]),
        pltpu.make_async_copy(counts, live, sems.at[1]),
        pltpu.make_async_copy(w_qkv, w_all, sems.at[2]),
        pltpu.make_async_copy(w_out, w_last, sems.at[3]),
    ]
    for copy in copies:
        copy.start()
    me = lax.axis_index("gx")
    side = toward_near()
    place = lax.broadcasted_iota(jnp.int32, (1, p), 1)
    top[...] = jnp.full_like(top, NEG)
    acc[...] = jnp.zeros_like(acc)
    copies[0].wait()
    copies[1].wait()
    pairs, singles = list_pairs(items, flags, by, [(0, None, 0, by, 0, True)])
    for plan, a, j0, j1 in ((plan_near, side, 0, by), (plan0, -side, 0, split), (plan1, -side, split, by)):
        there = (me + a >= 0) & (me + a < n)
        slab = jnp.clip(me + a, 0, n - 1)
        plan[3, 0], plan[3, 1 + 2 * by] = list_pairs(plan, flags, by, [(a, there, j0, j1, 0, False)])
        for i in range(by):
            plan[3, 1 + i] = live[i, 0, me]
        for j in range(j0, j1):
            plan[3, 1 + by + j - j0] = live[j, 0, slab]
    zeros = jnp.zeros((hd, p), BF16)
    copies[2].wait()
    mine = own[...].reshape(by * p, width)
    wide = min(512, width)
    for c in range(0, width, wide):
        q = (nn(mine, w_all[:, c : c + wide]).astype(BF16) * BF16(1.0 / hd**0.5)).astype(F32)
        for i in range(by):
            t = q[i * p : (i + 1) * p].T.astype(BF16)
            for u in range(wide // depth):
                g, mid = c // depth + u, u * depth + hd
                qt[i, g, :hd, :p] = t[mid - hd : mid]
                qt[i, g, :hd, p:] = zeros
                qt[i, g, hd:, :p] = zeros
                qt[i, g, hd:, p:] = t[mid : mid + hd]
    put_blocks(0, mine, w_all, keys, vals, [place < live[i, 0, me] for i in range(by)])
    attend(items, pairs, singles, keys, vals, qt, top, acc, scores, peaks)
    copies[3].wait()


def far_work(rim, w_all, qt, plan, top, acc, keys, vals, scores, peaks):
    by = qt.shape[0]
    blocks, p, width = rim.shape
    place = lax.broadcasted_iota(jnp.int32, (1, p), 1)
    put_blocks(0, rim[...].reshape(blocks * p, width), w_all, keys, vals, [place < plan[3, 1 + by + j] for j in range(blocks)])
    attend(plan, plan[3, 0], plan[3, 1 + 2 * by], keys, vals, qt, top, acc, scores, peaks)


def near_kernel(rim, w_all, qt, top_in, acc_in, plan, top, acc, keys, vals, scores, peaks):
    far_work(rim, w_all, qt, plan, top, acc, keys, vals, scores, peaks)


def far_kernel(
    rim, norm, w_all, qt, top_in, acc_in, tiled, w_out, plan, top, acc, held, keys, vals, scores, peaks, nrm
):
    for j in range(rim.shape[0]):
        nrm[j] = normalise(rim[j], norm[0:1], norm[1:2])
    far_work(nrm, w_all, qt, plan, top, acc, keys, vals, scores, peaks)
    for i, value in enumerate(finish(range(held.shape[0]), tiled, acc, w_out, plan)):
        held[i] = value


def last_kernel(
    rim, w_all, qt, top_in, acc_in, tiled, w_out, held, plan, top, acc, result, keys, vals, scores, peaks, out,
    sems
):
    by, early = tiled.shape[0], held.shape[0]
    copies = [pltpu.make_async_copy(held.at[i], result.at[0, i, 0], sems.at[i]) for i in range(early)]
    for copy in copies:
        copy.start()
    far_work(rim, w_all, qt, plan, top, acc, keys, vals, scores, peaks)
    for i, value in enumerate(finish(range(early, by), tiled, acc, w_out, plan), early):
        out[i - early] = value
        copies.append(pltpu.make_async_copy(out.at[i - early], result.at[0, i, 0], sems.at[i]))
        copies[-1].start()
    for copy in copies:
        copy.wait()


def vmem(x):
    return pltpu.with_memory_space_constraint(x, pltpu.VMEM)


def smem(x):
    return pltpu.with_memory_space_constraint(x, pltpu.SMEM)


def hbm(x):
    return pltpu.with_memory_space_constraint(x, pltpu.HBM)


def shards(n, points, order, masks, counts, gain, shift_bias, w_qkv, w_out):
    _, by, bz, p, width = points.shape
    hd = width // HEADS
    groups, depth, lanes = HEADS // 2, 2 * hd, 2 * p
    split = max(by - 2, 1)
    early = max(split - 1, 1)
    whole = pl.BlockSpec(memory_space=pltpu.VMEM)
    apart = pl.BlockSpec(memory_space=pltpu.HBM)
    words = pl.BlockSpec(memory_space=pltpu.SMEM)
    plan = pltpu.SMEM((4, 8 * by), jnp.int32)
    params = pltpu.CompilerParams(vmem_limit_bytes=LIMIT)
    points, order, masks, w_qkv, w_out = map(hbm, (points, order, masks, w_qkv, w_out))
    counts = hbm(jnp.transpose(counts, (1, 2, 0)))
    live = pltpu.SMEM(counts.shape, jnp.int32)
    flags = pltpu.SMEM(masks.shape, jnp.int32)

    first, rest, places, norm = pl.pallas_call(
        gather_kernel,
        out_shape=(
            pltpu.VMEM((split, p, width), BF16),
            pltpu.VMEM((by - split, p, width), BF16),
            pltpu.VMEM((by - split, 1, p), jnp.int32),
            pltpu.VMEM((2, width), F32),
        ),
        in_specs=[apart] * 5,
        out_specs=(whole,) * 4,
        scratch_shapes=[
            pltpu.VMEM((split, p, width), BF16),
            pltpu.VMEM(order.shape, jnp.int32),
            live,
            pltpu.SemaphoreType.DMA((by + 4,)),
        ],
        compiler_params=params,
        name="gather",
    )(points, order, counts, hbm(gain[None]), hbm(shift_bias[None]))
    tile_rest = pl.pallas_call(
        rest_kernel,
        out_shape=(
            pltpu.VMEM((by, p, width), BF16),
            pltpu.VMEM((by, p, width), BF16),
            pltpu.VMEM((by - split, p, width), BF16),
        ),
        in_specs=[whole] * 4,
        out_specs=(whole,) * 3,
        compiler_params=params,
        name="rest",
    )
    tiled, normed, second = tile_rest(vmem(first), vmem(rest), vmem(places), vmem(norm))
    near_pairs = [(i, i ^ 1) for i in range(n) if i ^ 1 < n]
    far_pairs = [(i, i + 1) for i in range(1, n - 1, 2)] + [(i + 1, i) for i in range(1, n - 1, 2)]

    def moved(value, pairs):
        return lax.ppermute(value, "gx", pairs)

    far0 = moved(first, far_pairs)
    near = moved(normed, near_pairs)
    far1 = moved(second, far_pairs)

    state = (
        pltpu.VMEM((by, 1, groups * lanes), F32),
        pltpu.VMEM((by, hd + 8, groups * lanes), F32),
    )

    def scratch(tiles):
        return [
            pltpu.VMEM((tiles, p, width), BF16),
            pltpu.VMEM((tiles, groups, depth + 2 * ONES, p), BF16),
        ]

    ahead = [
        pltpu.VMEM((2 * p, groups * lanes), F32),
        pltpu.VMEM((1, groups * lanes), F32),
    ]
    own_work = pl.pallas_call(
        functools.partial(own_kernel, n, split),
        out_shape=(
            pltpu.VMEM((by, groups, depth, lanes), BF16),
            *state,
            pltpu.VMEM(w_qkv.shape, BF16),
            pltpu.VMEM(w_out.shape, BF16),
            *(plan,) * 3,
        ),
        in_specs=[whole, apart, apart, apart, apart],
        out_specs=(whole,) * 5 + (words,) * 3,
        scratch_shapes=[*scratch(by), plan, flags, live, *ahead, pltpu.SemaphoreType.DMA((4,))],
        compiler_params=params,
        name="own",
    )
    near_work = pl.pallas_call(
        near_kernel,
        out_shape=state,
        in_specs=[*(whole,) * 5, words],
        out_specs=(whole,) * 2,
        scratch_shapes=[*scratch(by), *ahead],
        input_output_aliases={3: 0, 4: 1},
        compiler_params=params,
        name="near",
    )
    qt, top, acc, w_all, w_last, plan_near, plan0, plan1 = own_work(
        vmem(normed), masks, counts, w_qkv, w_out
    )
    top, acc = near_work(*map(vmem, (near, w_all, qt, top, acc)), smem(plan_near))
    ins = [far0, norm, w_all, qt, top, acc, tiled, w_last]
    top, acc, held = pl.pallas_call(
        far_kernel,
        out_shape=(*state, pltpu.VMEM((early, p, width), BF16)),
        in_specs=[*(whole,) * len(ins), words],
        out_specs=(whole,) * 3,
        scratch_shapes=[*scratch(split), *ahead, pltpu.VMEM((split, p, width), BF16)],
        input_output_aliases={4: 0, 5: 1},
        compiler_params=params,
        name="far",
    )(*map(vmem, ins), smem(plan0))
    ins = [far1, w_all, qt, top, acc, tiled, w_last, held]
    _, _, result = pl.pallas_call(
        last_kernel,
        out_shape=(*state, pltpu.HBM((1, by, bz, p, width), BF16)),
        in_specs=[*(whole,) * len(ins), words],
        out_specs=(whole, whole, apart),
        scratch_shapes=[
            *scratch(by - split),
            *ahead,
            pltpu.VMEM((by - early, p, width), BF16),
            pltpu.SemaphoreType.DMA((by,)),
        ],
        input_output_aliases={3: 0, 4: 1},
        compiler_params=params,
        name="last",
    )(*map(vmem, ins), smem(plan1))
    return result


def solution(mesh):
    placed = (
        P(("groups", "gx"), None, None, None, None),
        P(("groups", "gx"), None, None, None),
        P(("groups", "gx"), None, None, None),
        P("groups", None, None),
        P(),
        P(),
        P(),
        P(),
    )
    return jax.shard_map(
        functools.partial(shards, mesh.shape["gx"]),
        mesh=mesh,
        in_specs=placed,
        out_specs=P(("groups", "gx"), None, None, None, None),
        check_vma=False,
    )
```

```python
import functools

import jax
import jax.numpy as jnp
from jax import lax
from jax.experimental import pallas as pl
from jax.experimental.pallas import tpu as pltpu
from jax.sharding import PartitionSpec as P


HEADS = 8
NEG = -1e30
ONES = 16
LIMIT = 24 * 1024 * 1024
BF16, F32 = jnp.bfloat16, jnp.float32


def tn(a, b):
    return lax.dot_general(a, b, (((0,), (0,)), ((), ())), preferred_element_type=F32)


def nn(a, b):
    return jnp.dot(a, b, preferred_element_type=F32)


def normalise(tiled, gain, shift):
    values = tiled.astype(F32)
    mean = jnp.mean(values, axis=-1, keepdims=True)
    var = jnp.mean((values - mean) ** 2, axis=-1, keepdims=True)
    return ((values - mean) * lax.rsqrt(var + 1e-05) * gain + shift).astype(BF16)


def select(row, raw):
    p = raw.shape[0]
    slot = lax.broadcasted_iota(jnp.int32, (p, p), 0)
    return tn((slot == row).astype(F32).astype(BF16), raw).astype(BF16)


def gather_kernel(points, order, counts, gain, shift, first, rest, places, norm, raw, rows, live, sems):
    _, by, _, p, _ = points.shape
    split = first.shape[0]
    me = lax.axis_index("gx")
    small = [
        pltpu.make_async_copy(order, rows, sems.at[by]),
        pltpu.make_async_copy(counts, live, sems.at[by + 1]),
        pltpu.make_async_copy(gain, norm.at[0:1], sems.at[by + 2]),
        pltpu.make_async_copy(shift, norm.at[1:2], sems.at[by + 3]),
    ]
    large = [
        pltpu.make_async_copy(
            points.at[0, j, 0], raw.at[j] if j < split else rest.at[j - split], sems.at[j]
        )
        for j in range(by)
    ]
    for copy in (*small[:2], *large, *small[2:]):
        copy.start()
    place = lax.broadcasted_iota(jnp.int32, (1, p), 1)
    small[0].wait()
    small[1].wait()
    picks = []
    for j in range(by):
        row = rows[0, j]
        picks.append(jnp.where(place < live[j, 0, me], row, row[:, :1]))
        if j >= split:
            places[j - split] = picks[j]
    for j in range(split):
        large[j].wait()
    for j in range(split):
        first[j] = select(picks[j], raw[j])
    for copy in (*large[split:], *small[2:]):
        copy.wait()


def rest_kernel(first, rest, places, norm, tiled, normed, second):
    split = first.shape[0]
    gain, shift = norm[0:1], norm[1:2]
    for j in range(rest.shape[0]):
        got = select(places[j], rest[j])
        tiled[split + j] = got
        got = normalise(got, gain, shift)
        second[j] = got
        normed[split + j] = got
    for j in range(split):
        got = first[j]
        tiled[j] = got
        normed[j] = normalise(got, gain, shift)


def toward_near():
    return 1 - 2 * (lax.axis_index("gx") & 1)


def column(side, b):
    index = 9 * (side + 1) + 3 * (b + 1) + 1
    if isinstance(index, int):
        return index if index < 13 else index - 1
    return jnp.where(index > 13, index - 1, index)


def list_pairs(items, masks, by, sides):
    pairs, singles = jnp.int32(0), jnp.int32(0)
    for i in range(by):
        found, last, most = jnp.int32(0), jnp.int32(0), 0
        for side, exists, j0, j1, tile0, own in sides:
            for b in (0, -1, 1):
                j = i + b
                if not j0 <= j < j1:
                    continue
                tile = tile0 + j - j0
                items[1, 2 * pairs + found] = tile
                most += 1
                if own and b == 0:
                    found = found + 1
                    last = jnp.int32(tile)
                    continue
                on = masks[0, i, 0, column(side, b)] == 1
                on = on if exists is None else on & exists
                found = found + on.astype(jnp.int32)
                last = jnp.where(on, tile, last)
        items[2, 2 * singles] = i
        items[2, 2 * singles + 1] = last
        for u in range(most // 2):
            items[0, pairs + u] = i
        pairs = pairs + (found >> 1)
        singles = singles + (found & 1)
    items[0, pairs] = 0
    for u in range(2):
        items[1, 2 * pairs + u] = 0
        items[2, 2 * singles + u] = 0
    return pairs, singles


def attend(items, pairs, singles, keys, vals, qt, top, acc, scores, peaks):
    groups, depth, lanes = qt.shape[1:]
    hd, p = depth // 2, lanes // 2
    lead = groups // 2

    def run(count, tiles, entry):
        def score(t, g):
            i, picked = entry(t)
            rows = slice(g * depth, (g + 1) * depth)
            cols = slice(g * lanes, (g + 1) * lanes)
            peak = None
            for u, k in enumerate(picked):
                made = nn(keys[k, :, rows], qt[i, g])
                scores[u * p : (u + 1) * p, cols] = made
                peak = made if peak is None else jnp.maximum(peak, made)
            peaks[:, cols] = jnp.max(peak, axis=0, keepdims=True)

        def weigh(t, g):
            i, picked = entry(t)
            cols = slice(g * lanes, (g + 1) * lanes)
            old = top[i, :, cols]
            new = jnp.maximum(old, peaks[:, cols])
            probs = jnp.exp(scores[: tiles * p, cols] - new).astype(BF16)
            fade = jnp.exp(old - new)
            both, sums = [], []
            for h in range(2):
                rows = slice(h * (hd + ONES), (h + 1) * (hd + ONES))
                val = jnp.concatenate([vals[k, g, rows] for k in picked], axis=1)
                out = nn(val, probs[:, h * p : (h + 1) * p])
                both.append(out[:hd])
                sums.append(out[hd : hd + 8])
            return cols, new, fade, jnp.concatenate(both, axis=1), jnp.concatenate(sums, axis=1)

        def step(t, carry):
            made = []
            for g in range(0, groups, lead):
                for u in range(g, g + lead):
                    score(t + (u + lead) // groups, (u + lead) % groups)
                for u in range(g, g + lead):
                    made.append(weigh(t, u))
            i, _ = entry(t)
            for cols, new, fade, both, sums in made:
                top[i, :, cols] = new
                acc[i, :hd, cols] = acc[i, :hd, cols] * fade + both
                acc[i, hd:, cols] = acc[i, hd:, cols] * fade + sums
            return carry

        for g in range(lead):
            score(0, g)
        lax.fori_loop(0, count, step, 0)

    run(pairs, 2, lambda t: (items[0, t], (items[1, 2 * t], items[1, 2 * t + 1])))
    run(singles, 1, lambda t: (items[2, 2 * t], (items[2, 2 * t + 1],)))


def put_values(vals, tile, g0, v, live):
    p = vals.shape[3]
    hd = vals.shape[2] // 2 - ONES
    flag = jnp.broadcast_to(live.astype(F32).astype(BF16), (ONES, p))
    vt = jnp.where(live, v.T, 0.0).astype(BF16)
    for h in range(v.shape[1] // hd):
        g, r = g0 + h // 2, h % 2 * (hd + ONES)
        vals[tile, g, r : r + hd] = vt[h * hd : (h + 1) * hd]
        vals[tile, g, r + hd : r + hd + ONES] = flag


def put_blocks(tile0, x, w_all, keys, vals, lives):
    p, width = keys.shape[1:]
    wide = min(512, width)
    groups = vals.shape[1]
    for c in range(0, width, wide):
        k = nn(x, w_all[:, width + c : width + c + wide]).astype(BF16)
        v = nn(x, w_all[:, 2 * width + c : 2 * width + c + wide])
        for u, live in enumerate(lives):
            rows = slice(u * p, (u + 1) * p)
            keys[tile0 + u, :, c : c + wide] = k[rows]
            put_values(vals, tile0 + u, c * groups // width, v[rows], live)


def finish(blocks, tiled, acc, w_out, plan):
    hd = acc.shape[1] - 8
    p = tiled.shape[1]
    heads = acc.shape[2] // p
    columns = []
    for i in blocks:
        attn = acc[i, :hd] * (1.0 / acc[i, hd : hd + 1])
        attn = [attn[:, h * p : (h + 1) * p] for h in range(heads)]
        columns.append(jnp.concatenate(attn, axis=0).astype(BF16))
    mixed = tn(jnp.concatenate(columns, axis=1), w_out[...])
    place = lax.broadcasted_iota(jnp.int32, (p, 1), 0)
    made = []
    for u, i in enumerate(blocks):
        value = tiled[i].astype(F32) + mixed[u * p : (u + 1) * p]
        made.append(jnp.where(place < plan[3, 1 + i], value, 0.0).astype(BF16))
    return made


def own_kernel(
    n, split, own, masks, counts, w_qkv, w_out, qt, top, acc, w_all, w_last, plan_near, plan0, plan1, keys, vals,
    items, flags, live, scores, peaks, sems
):
    by, p, width = own.shape
    _, depth = qt.shape[1:3]
    hd = depth // 2
    copies = [
        pltpu.make_async_copy(masks, flags, sems.at[0]),
        pltpu.make_async_copy(counts, live, sems.at[1]),
        pltpu.make_async_copy(w_qkv, w_all, sems.at[2]),
        pltpu.make_async_copy(w_out, w_last, sems.at[3]),
    ]
    for copy in copies:
        copy.start()
    me = lax.axis_index("gx")
    side = toward_near()
    place = lax.broadcasted_iota(jnp.int32, (1, p), 1)
    top[...] = jnp.full_like(top, NEG)
    acc[...] = jnp.zeros_like(acc)
    copies[0].wait()
    copies[1].wait()
    pairs, singles = list_pairs(items, flags, by, [(0, None, 0, by, 0, True)])
    for plan, a, j0, j1 in ((plan_near, side, 0, by), (plan0, -side, 0, split), (plan1, -side, split, by)):
        there = (me + a >= 0) & (me + a < n)
        slab = jnp.clip(me + a, 0, n - 1)
        plan[3, 0], plan[3, 1 + 2 * by] = list_pairs(plan, flags, by, [(a, there, j0, j1, 0, False)])
        for i in range(by):
            plan[3, 1 + i] = live[i, 0, me]
        for j in range(j0, j1):
            plan[3, 1 + by + j - j0] = live[j, 0, slab]
    zeros = jnp.zeros((hd, p), BF16)
    copies[2].wait()
    mine = own[...].reshape(by * p, width)
    wide = min(512, width)
    for c in range(0, width, wide):
        q = (nn(mine, w_all[:, c : c + wide]).astype(BF16) * BF16(1.0 / hd**0.5)).astype(F32)
        for i in range(by):
            t = q[i * p : (i + 1) * p].T.astype(BF16)
            for u in range(wide // depth):
                g, mid = c // depth + u, u * depth + hd
                qt[i, g, :hd, :p] = t[mid - hd : mid]
                qt[i, g, :hd, p:] = zeros
                qt[i, g, hd:, :p] = zeros
                qt[i, g, hd:, p:] = t[mid : mid + hd]
    put_blocks(0, mine, w_all, keys, vals, [place < live[i, 0, me] for i in range(by)])
    attend(items, pairs, singles, keys, vals, qt, top, acc, scores, peaks)
    copies[3].wait()


def far_work(rim, w_all, qt, plan, top, acc, keys, vals, scores, peaks):
    by = qt.shape[0]
    blocks, p, width = rim.shape
    place = lax.broadcasted_iota(jnp.int32, (1, p), 1)
    put_blocks(0, rim[...].reshape(blocks * p, width), w_all, keys, vals, [place < plan[3, 1 + by + j] for j in range(blocks)])
    attend(plan, plan[3, 0], plan[3, 1 + 2 * by], keys, vals, qt, top, acc, scores, peaks)


def near_kernel(rim, w_all, qt, top_in, acc_in, plan, top, acc, keys, vals, scores, peaks):
    far_work(rim, w_all, qt, plan, top, acc, keys, vals, scores, peaks)


def far_kernel(
    rim, norm, w_all, qt, top_in, acc_in, tiled, w_out, plan, top, acc, held, keys, vals, scores, peaks, nrm
):
    for j in range(rim.shape[0]):
        nrm[j] = normalise(rim[j], norm[0:1], norm[1:2])
    far_work(nrm, w_all, qt, plan, top, acc, keys, vals, scores, peaks)
    for i, value in enumerate(finish(range(held.shape[0]), tiled, acc, w_out, plan)):
        held[i] = value


def last_kernel(
    rim, w_all, qt, top_in, acc_in, tiled, w_out, held, plan, top, acc, result, keys, vals, scores, peaks, out,
    sems
):
    by, early = tiled.shape[0], held.shape[0]
    copies = [pltpu.make_async_copy(held.at[i], result.at[0, i, 0], sems.at[i]) for i in range(early)]
    for copy in copies:
        copy.start()
    far_work(rim, w_all, qt, plan, top, acc, keys, vals, scores, peaks)
    for i in range(early, by):
        (out[i - early],) = finish([i], tiled, acc, w_out, plan)
        copies.append(pltpu.make_async_copy(out.at[i - early], result.at[0, i, 0], sems.at[i]))
        copies[-1].start()
    for copy in copies:
        copy.wait()


def vmem(x):
    return pltpu.with_memory_space_constraint(x, pltpu.VMEM)


def smem(x):
    return pltpu.with_memory_space_constraint(x, pltpu.SMEM)


def hbm(x):
    return pltpu.with_memory_space_constraint(x, pltpu.HBM)


def shards(n, points, order, masks, counts, gain, shift_bias, w_qkv, w_out):
    _, by, bz, p, width = points.shape
    hd = width // HEADS
    groups, depth, lanes = HEADS // 2, 2 * hd, 2 * p
    split = max(by // 2, 1)
    early = max(split - 1, 1)
    whole = pl.BlockSpec(memory_space=pltpu.VMEM)
    apart = pl.BlockSpec(memory_space=pltpu.HBM)
    words = pl.BlockSpec(memory_space=pltpu.SMEM)
    plan = pltpu.SMEM((4, 8 * by), jnp.int32)
    params = pltpu.CompilerParams(vmem_limit_bytes=LIMIT)
    points, order, masks, w_qkv, w_out = map(hbm, (points, order, masks, w_qkv, w_out))
    counts = hbm(jnp.transpose(counts, (1, 2, 0)))
    live = pltpu.SMEM(counts.shape, jnp.int32)
    flags = pltpu.SMEM(masks.shape, jnp.int32)

    first, rest, places, norm = pl.pallas_call(
        gather_kernel,
        out_shape=(
            pltpu.VMEM((split, p, width), BF16),
            pltpu.VMEM((by - split, p, width), BF16),
            pltpu.VMEM((by - split, 1, p), jnp.int32),
            pltpu.VMEM((2, width), F32),
        ),
        in_specs=[apart] * 5,
        out_specs=(whole,) * 4,
        scratch_shapes=[
            pltpu.VMEM((split, p, width), BF16),
            pltpu.VMEM(order.shape, jnp.int32),
            live,
            pltpu.SemaphoreType.DMA((by + 4,)),
        ],
        compiler_params=params,
        name="gather",
    )(points, order, counts, hbm(gain[None]), hbm(shift_bias[None]))
    tile_rest = pl.pallas_call(
        rest_kernel,
        out_shape=(
            pltpu.VMEM((by, p, width), BF16),
            pltpu.VMEM((by, p, width), BF16),
            pltpu.VMEM((by - split, p, width), BF16),
        ),
        in_specs=[whole] * 4,
        out_specs=(whole,) * 3,
        compiler_params=params,
        name="rest",
    )
    tiled, normed, second = tile_rest(vmem(first), vmem(rest), vmem(places), vmem(norm))
    near_pairs = [(i, i ^ 1) for i in range(n) if i ^ 1 < n]
    far_pairs = [(i, i + 1) for i in range(1, n - 1, 2)] + [(i + 1, i) for i in range(1, n - 1, 2)]

    def moved(value, pairs):
        return lax.ppermute(value, "gx", pairs)

    far0 = moved(first, far_pairs)
    near = moved(normed, near_pairs)
    far1 = moved(second, far_pairs)

    state = (
        pltpu.VMEM((by, 1, groups * lanes), F32),
        pltpu.VMEM((by, hd + 8, groups * lanes), F32),
    )

    def scratch(tiles):
        return [
            pltpu.VMEM((tiles, p, width), BF16),
            pltpu.VMEM((tiles, groups, depth + 2 * ONES, p), BF16),
        ]

    ahead = [
        pltpu.VMEM((2 * p, groups * lanes), F32),
        pltpu.VMEM((1, groups * lanes), F32),
    ]
    own_work = pl.pallas_call(
        functools.partial(own_kernel, n, split),
        out_shape=(
            pltpu.VMEM((by, groups, depth, lanes), BF16),
            *state,
            pltpu.VMEM(w_qkv.shape, BF16),
            pltpu.VMEM(w_out.shape, BF16),
            *(plan,) * 3,
        ),
        in_specs=[whole, apart, apart, apart, apart],
        out_specs=(whole,) * 5 + (words,) * 3,
        scratch_shapes=[*scratch(by), plan, flags, live, *ahead, pltpu.SemaphoreType.DMA((4,))],
        compiler_params=params,
        name="own",
    )
    near_work = pl.pallas_call(
        near_kernel,
        out_shape=state,
        in_specs=[*(whole,) * 5, words],
        out_specs=(whole,) * 2,
        scratch_shapes=[*scratch(by), *ahead],
        input_output_aliases={3: 0, 4: 1},
        compiler_params=params,
        name="near",
    )
    qt, top, acc, w_all, w_last, plan_near, plan0, plan1 = own_work(
        vmem(normed), masks, counts, w_qkv, w_out
    )
    top, acc = near_work(*map(vmem, (near, w_all, qt, top, acc)), smem(plan_near))
    ins = [far0, norm, w_all, qt, top, acc, tiled, w_last]
    top, acc, held = pl.pallas_call(
        far_kernel,
        out_shape=(*state, pltpu.VMEM((early, p, width), BF16)),
        in_specs=[*(whole,) * len(ins), words],
        out_specs=(whole,) * 3,
        scratch_shapes=[*scratch(split), *ahead, pltpu.VMEM((split, p, width), BF16)],
        input_output_aliases={4: 0, 5: 1},
        compiler_params=params,
        name="far",
    )(*map(vmem, ins), smem(plan0))
    ins = [far1, w_all, qt, top, acc, tiled, w_last, held]
    _, _, result = pl.pallas_call(
        last_kernel,
        out_shape=(*state, pltpu.HBM((1, by, bz, p, width), BF16)),
        in_specs=[*(whole,) * len(ins), words],
        out_specs=(whole, whole, apart),
        scratch_shapes=[
            *scratch(by - split),
            *ahead,
            pltpu.VMEM((by - early, p, width), BF16),
            pltpu.SemaphoreType.DMA((by,)),
        ],
        input_output_aliases={3: 0, 4: 1},
        compiler_params=params,
        name="last",
    )(*map(vmem, ins), smem(plan1))
    return result


def solution(mesh):
    placed = (
        P(("groups", "gx"), None, None, None, None),
        P(("groups", "gx"), None, None, None),
        P(("groups", "gx"), None, None, None),
        P("groups", None, None),
        P(),
        P(),
        P(),
        P(),
    )
    return jax.shard_map(
        functools.partial(shards, mesh.shape["gx"]),
        mesh=mesh,
        in_specs=placed,
        out_specs=P(("groups", "gx"), None, None, None, None),
        check_vma=False,
    )
```

```python
import functools

import jax
import jax.numpy as jnp
from jax import lax
from jax.experimental import pallas as pl
from jax.experimental.pallas import tpu as pltpu
from jax.sharding import PartitionSpec as P


HEADS = 8
NEG = -1e30
ONES = 16
LIMIT = 24 * 1024 * 1024
BF16, F32 = jnp.bfloat16, jnp.float32


def tn(a, b):
    return lax.dot_general(a, b, (((0,), (0,)), ((), ())), preferred_element_type=F32)


def nn(a, b):
    return jnp.dot(a, b, preferred_element_type=F32)


def normalise(tiled, gain, shift):
    values = tiled.astype(F32)
    mean = jnp.mean(values, axis=-1, keepdims=True)
    var = jnp.mean((values - mean) ** 2, axis=-1, keepdims=True)
    return ((values - mean) * lax.rsqrt(var + 1e-05) * gain + shift).astype(BF16)


def select(row, raw):
    p = raw.shape[0]
    slot = lax.broadcasted_iota(jnp.int32, (p, p), 0)
    return tn((slot == row).astype(F32).astype(BF16), raw).astype(BF16)


def gather_kernel(points, order, counts, gain, shift, first, rest, places, norm, raw, rows, live, sems):
    _, by, _, p, _ = points.shape
    split = first.shape[0]
    me = lax.axis_index("gx")
    small = [
        pltpu.make_async_copy(order, rows, sems.at[by]),
        pltpu.make_async_copy(counts, live, sems.at[by + 1]),
        pltpu.make_async_copy(gain, norm.at[0:1], sems.at[by + 2]),
        pltpu.make_async_copy(shift, norm.at[1:2], sems.at[by + 3]),
    ]
    large = [
        pltpu.make_async_copy(
            points.at[0, j, 0], raw.at[j] if j < split else rest.at[j - split], sems.at[j]
        )
        for j in range(by)
    ]
    for copy in (*small[:2], *large, *small[2:]):
        copy.start()
    place = lax.broadcasted_iota(jnp.int32, (1, p), 1)
    small[0].wait()
    small[1].wait()
    picks = []
    for j in range(by):
        row = rows[0, j]
        picks.append(jnp.where(place < live[j, 0, me], row, row[:, :1]))
        if j >= split:
            places[j - split] = picks[j]
    for j in range(split):
        large[j].wait()
    for j in range(split):
        first[j] = select(picks[j], raw[j])
    for copy in (*large[split:], *small[2:]):
        copy.wait()


def rest_kernel(first, rest, places, norm, tiled, normed, second):
    split = first.shape[0]
    gain, shift = norm[0:1], norm[1:2]
    for j in range(rest.shape[0]):
        got = select(places[j], rest[j])
        tiled[split + j] = got
        got = normalise(got, gain, shift)
        second[j] = got
        normed[split + j] = got
    for j in range(split):
        got = first[j]
        tiled[j] = got
        normed[j] = normalise(got, gain, shift)


def toward_near():
    return 1 - 2 * (lax.axis_index("gx") & 1)


def column(side, b):
    index = 9 * (side + 1) + 3 * (b + 1) + 1
    if isinstance(index, int):
        return index if index < 13 else index - 1
    return jnp.where(index > 13, index - 1, index)


def list_pairs(items, masks, by, sides):
    pairs, singles = jnp.int32(0), jnp.int32(0)
    for i in range(by):
        found, last, most = jnp.int32(0), jnp.int32(0), 0
        for side, exists, j0, j1, tile0, own in sides:
            for b in (0, -1, 1):
                j = i + b
                if not j0 <= j < j1:
                    continue
                tile = tile0 + j - j0
                items[1, 2 * pairs + found] = tile
                most += 1
                if own and b == 0:
                    found = found + 1
                    last = jnp.int32(tile)
                    continue
                on = masks[0, i, 0, column(side, b)] == 1
                on = on if exists is None else on & exists
                found = found + on.astype(jnp.int32)
                last = jnp.where(on, tile, last)
        items[2, 2 * singles] = i
        items[2, 2 * singles + 1] = last
        for u in range(most // 2):
            items[0, pairs + u] = i
        pairs = pairs + (found >> 1)
        singles = singles + (found & 1)
    items[0, pairs] = 0
    for u in range(2):
        items[1, 2 * pairs + u] = 0
        items[2, 2 * singles + u] = 0
    return pairs, singles


def attend(items, pairs, singles, keys, vals, qt, top, acc, scores, peaks):
    groups, depth, lanes = qt.shape[1:]
    hd, p = depth // 2, lanes // 2
    lead = groups // 2

    def run(count, tiles, entry):
        def score(t, g):
            i, picked = entry(t)
            rows = slice(g * depth, (g + 1) * depth)
            cols = slice(g * lanes, (g + 1) * lanes)
            peak = None
            for u, k in enumerate(picked):
                made = nn(keys[k, :, rows], qt[i, g])
                scores[u * p : (u + 1) * p, cols] = made
                peak = made if peak is None else jnp.maximum(peak, made)
            peaks[:, cols] = jnp.max(peak, axis=0, keepdims=True)

        def weigh(t, g):
            i, picked = entry(t)
            cols = slice(g * lanes, (g + 1) * lanes)
            old = top[i, :, cols]
            new = jnp.maximum(old, peaks[:, cols])
            probs = jnp.exp(scores[: tiles * p, cols] - new).astype(BF16)
            fade = jnp.exp(old - new)
            both, sums = [], []
            for h in range(2):
                rows = slice(h * (hd + ONES), (h + 1) * (hd + ONES))
                val = jnp.concatenate([vals[k, g, rows] for k in picked], axis=1)
                out = nn(val, probs[:, h * p : (h + 1) * p])
                both.append(out[:hd])
                sums.append(out[hd : hd + 8])
            return cols, new, fade, jnp.concatenate(both, axis=1), jnp.concatenate(sums, axis=1)

        def step(t, carry):
            made = []
            for g in range(0, groups, lead):
                for u in range(g, g + lead):
                    score(t + (u + lead) // groups, (u + lead) % groups)
                for u in range(g, g + lead):
                    made.append(weigh(t, u))
            i, _ = entry(t)
            for cols, new, fade, both, sums in made:
                top[i, :, cols] = new
                acc[i, :hd, cols] = acc[i, :hd, cols] * fade + both
                acc[i, hd:, cols] = acc[i, hd:, cols] * fade + sums
            return carry

        for g in range(lead):
            score(0, g)
        lax.fori_loop(0, count, step, 0)

    run(pairs, 2, lambda t: (items[0, t], (items[1, 2 * t], items[1, 2 * t + 1])))
    run(singles, 1, lambda t: (items[2, 2 * t], (items[2, 2 * t + 1],)))


def put_values(vals, tile, g0, v, live):
    p = vals.shape[3]
    hd = vals.shape[2] // 2 - ONES
    flag = jnp.broadcast_to(live.astype(F32).astype(BF16), (ONES, p))
    vt = jnp.where(live, v.T, 0.0).astype(BF16)
    for h in range(v.shape[1] // hd):
        g, r = g0 + h // 2, h % 2 * (hd + ONES)
        vals[tile, g, r : r + hd] = vt[h * hd : (h + 1) * hd]
        vals[tile, g, r + hd : r + hd + ONES] = flag


def put_blocks(tile0, x, w_all, keys, vals, lives):
    p, width = keys.shape[1:]
    wide = min(512, width)
    groups = vals.shape[1]
    for c in range(0, width, wide):
        k = nn(x, w_all[:, width + c : width + c + wide]).astype(BF16)
        v = nn(x, w_all[:, 2 * width + c : 2 * width + c + wide])
        for u, live in enumerate(lives):
            rows = slice(u * p, (u + 1) * p)
            keys[tile0 + u, :, c : c + wide] = k[rows]
            put_values(vals, tile0 + u, c * groups // width, v[rows], live)


def finish(blocks, tiled, acc, w_out, plan):
    hd = acc.shape[1] - 8
    p = tiled.shape[1]
    heads = acc.shape[2] // p
    columns = []
    for i in blocks:
        attn = acc[i, :hd] * (1.0 / acc[i, hd : hd + 1])
        attn = [attn[:, h * p : (h + 1) * p] for h in range(heads)]
        columns.append(jnp.concatenate(attn, axis=0).astype(BF16))
    mixed = tn(jnp.concatenate(columns, axis=1), w_out[...])
    place = lax.broadcasted_iota(jnp.int32, (p, 1), 0)
    made = []
    for u, i in enumerate(blocks):
        value = tiled[i].astype(F32) + mixed[u * p : (u + 1) * p]
        made.append(jnp.where(place < plan[3, 1 + i], value, 0.0).astype(BF16))
    return made


def own_kernel(
    n, split, own, masks, counts, w_qkv, w_out, qt, top, acc, w_all, w_last, plan_near, plan0, plan1, keys, vals,
    items, flags, live, scores, peaks, sems
):
    by, p, width = own.shape
    _, depth = qt.shape[1:3]
    hd = depth // 2
    copies = [
        pltpu.make_async_copy(masks, flags, sems.at[0]),
        pltpu.make_async_copy(counts, live, sems.at[1]),
        pltpu.make_async_copy(w_qkv, w_all, sems.at[2]),
        pltpu.make_async_copy(w_out, w_last, sems.at[3]),
    ]
    for copy in copies:
        copy.start()
    me = lax.axis_index("gx")
    side = toward_near()
    place = lax.broadcasted_iota(jnp.int32, (1, p), 1)
    top[...] = jnp.full_like(top, NEG)
    acc[...] = jnp.zeros_like(acc)
    copies[0].wait()
    copies[1].wait()
    pairs, singles = list_pairs(items, flags, by, [(0, None, 0, by, 0, True)])
    for plan, a, j0, j1 in ((plan_near, side, 0, by), (plan0, -side, 0, split), (plan1, -side, split, by)):
        there = (me + a >= 0) & (me + a < n)
        slab = jnp.clip(me + a, 0, n - 1)
        plan[3, 0], plan[3, 1 + 2 * by] = list_pairs(plan, flags, by, [(a, there, j0, j1, 0, False)])
        for i in range(by):
            plan[3, 1 + i] = live[i, 0, me]
        for j in range(j0, j1):
            plan[3, 1 + by + j - j0] = live[j, 0, slab]
    zeros = jnp.zeros((hd, p), BF16)
    copies[2].wait()
    mine = own[...].reshape(by * p, width)
    wide = min(512, width)
    for c in range(0, width, wide):
        q = (nn(mine, w_all[:, c : c + wide]).astype(BF16) * BF16(1.0 / hd**0.5)).astype(F32)
        for i in range(by):
            t = q[i * p : (i + 1) * p].T.astype(BF16)
            for u in range(wide // depth):
                g, mid = c // depth + u, u * depth + hd
                qt[i, g, :hd, :p] = t[mid - hd : mid]
                qt[i, g, :hd, p:] = zeros
                qt[i, g, hd:, :p] = zeros
                qt[i, g, hd:, p:] = t[mid : mid + hd]
    put_blocks(0, mine, w_all, keys, vals, [place < live[i, 0, me] for i in range(by)])
    attend(items, pairs, singles, keys, vals, qt, top, acc, scores, peaks)
    copies[3].wait()


def far_work(rim, w_all, qt, plan, top, acc, keys, vals, scores, peaks):
    by = qt.shape[0]
    blocks, p, width = rim.shape
    place = lax.broadcasted_iota(jnp.int32, (1, p), 1)
    put_blocks(0, rim[...].reshape(blocks * p, width), w_all, keys, vals, [place < plan[3, 1 + by + j] for j in range(blocks)])
    attend(plan, plan[3, 0], plan[3, 1 + 2 * by], keys, vals, qt, top, acc, scores, peaks)


def near_kernel(rim, w_all, qt, top_in, acc_in, plan, top, acc, keys, vals, scores, peaks):
    far_work(rim, w_all, qt, plan, top, acc, keys, vals, scores, peaks)


def far_kernel(
    rim, norm, w_all, qt, top_in, acc_in, tiled, w_out, plan, top, acc, held, keys, vals, scores, peaks, nrm
):
    for j in range(rim.shape[0]):
        nrm[j] = normalise(rim[j], norm[0:1], norm[1:2])
    far_work(nrm, w_all, qt, plan, top, acc, keys, vals, scores, peaks)
    for i, value in enumerate(finish(range(held.shape[0]), tiled, acc, w_out, plan)):
        held[i] = value


def last_kernel(
    rim, w_all, qt, top_in, acc_in, tiled, w_out, held, plan, top, acc, result, keys, vals, scores, peaks, out,
    sems
):
    by, early = tiled.shape[0], held.shape[0]
    parts = 4
    tall = tiled.shape[1] // parts
    copies = [pltpu.make_async_copy(held.at[i], result.at[0, i, 0], sems.at[i]) for i in range(early)]
    for copy in copies:
        copy.start()
    far_work(rim, w_all, qt, plan, top, acc, keys, vals, scores, peaks)
    for i in range(early, by):
        (out[i - early],) = finish([i], tiled, acc, w_out, plan)
        for c in range(parts):
            rows = pl.ds(c * tall, tall)
            copies.append(
                pltpu.make_async_copy(
                    out.at[i - early, rows], result.at[0, i, 0, rows], sems.at[early + (i - early) * parts + c]
                )
            )
            copies[-1].start()
    for copy in copies:
        copy.wait()


def vmem(x):
    return pltpu.with_memory_space_constraint(x, pltpu.VMEM)


def smem(x):
    return pltpu.with_memory_space_constraint(x, pltpu.SMEM)


def hbm(x):
    return pltpu.with_memory_space_constraint(x, pltpu.HBM)


def shards(n, points, order, masks, counts, gain, shift_bias, w_qkv, w_out):
    _, by, bz, p, width = points.shape
    hd = width // HEADS
    groups, depth, lanes = HEADS // 2, 2 * hd, 2 * p
    split = max(by // 2, 1)
    early = max(split - 1, 1)
    whole = pl.BlockSpec(memory_space=pltpu.VMEM)
    apart = pl.BlockSpec(memory_space=pltpu.HBM)
    words = pl.BlockSpec(memory_space=pltpu.SMEM)
    plan = pltpu.SMEM((4, 8 * by), jnp.int32)
    params = pltpu.CompilerParams(vmem_limit_bytes=LIMIT)
    points, order, masks, w_qkv, w_out = map(hbm, (points, order, masks, w_qkv, w_out))
    counts = hbm(jnp.transpose(counts, (1, 2, 0)))
    live = pltpu.SMEM(counts.shape, jnp.int32)
    flags = pltpu.SMEM(masks.shape, jnp.int32)

    first, rest, places, norm = pl.pallas_call(
        gather_kernel,
        out_shape=(
            pltpu.VMEM((split, p, width), BF16),
            pltpu.VMEM((by - split, p, width), BF16),
            pltpu.VMEM((by - split, 1, p), jnp.int32),
            pltpu.VMEM((2, width), F32),
        ),
        in_specs=[apart] * 5,
        out_specs=(whole,) * 4,
        scratch_shapes=[
            pltpu.VMEM((split, p, width), BF16),
            pltpu.VMEM(order.shape, jnp.int32),
            live,
            pltpu.SemaphoreType.DMA((by + 4,)),
        ],
        compiler_params=params,
        name="gather",
    )(points, order, counts, hbm(gain[None]), hbm(shift_bias[None]))
    tile_rest = pl.pallas_call(
        rest_kernel,
        out_shape=(
            pltpu.VMEM((by, p, width), BF16),
            pltpu.VMEM((by, p, width), BF16),
            pltpu.VMEM((by - split, p, width), BF16),
        ),
        in_specs=[whole] * 4,
        out_specs=(whole,) * 3,
        compiler_params=params,
        name="rest",
    )
    tiled, normed, second = tile_rest(vmem(first), vmem(rest), vmem(places), vmem(norm))
    near_pairs = [(i, i ^ 1) for i in range(n) if i ^ 1 < n]
    far_pairs = [(i, i + 1) for i in range(1, n - 1, 2)] + [(i + 1, i) for i in range(1, n - 1, 2)]

    def moved(value, pairs):
        return lax.ppermute(value, "gx", pairs)

    far0 = moved(first, far_pairs)
    near = moved(normed, near_pairs)
    far1 = moved(second, far_pairs)

    state = (
        pltpu.VMEM((by, 1, groups * lanes), F32),
        pltpu.VMEM((by, hd + 8, groups * lanes), F32),
    )

    def scratch(tiles):
        return [
            pltpu.VMEM((tiles, p, width), BF16),
            pltpu.VMEM((tiles, groups, depth + 2 * ONES, p), BF16),
        ]

    ahead = [
        pltpu.VMEM((2 * p, groups * lanes), F32),
        pltpu.VMEM((1, groups * lanes), F32),
    ]
    own_work = pl.pallas_call(
        functools.partial(own_kernel, n, split),
        out_shape=(
            pltpu.VMEM((by, groups, depth, lanes), BF16),
            *state,
            pltpu.VMEM(w_qkv.shape, BF16),
            pltpu.VMEM(w_out.shape, BF16),
            *(plan,) * 3,
        ),
        in_specs=[whole, apart, apart, apart, apart],
        out_specs=(whole,) * 5 + (words,) * 3,
        scratch_shapes=[*scratch(by), plan, flags, live, *ahead, pltpu.SemaphoreType.DMA((4,))],
        compiler_params=params,
        name="own",
    )
    near_work = pl.pallas_call(
        near_kernel,
        out_shape=state,
        in_specs=[*(whole,) * 5, words],
        out_specs=(whole,) * 2,
        scratch_shapes=[*scratch(by), *ahead],
        input_output_aliases={3: 0, 4: 1},
        compiler_params=params,
        name="near",
    )
    qt, top, acc, w_all, w_last, plan_near, plan0, plan1 = own_work(
        vmem(normed), masks, counts, w_qkv, w_out
    )
    top, acc = near_work(*map(vmem, (near, w_all, qt, top, acc)), smem(plan_near))
    ins = [far0, norm, w_all, qt, top, acc, tiled, w_last]
    top, acc, held = pl.pallas_call(
        far_kernel,
        out_shape=(*state, pltpu.VMEM((early, p, width), BF16)),
        in_specs=[*(whole,) * len(ins), words],
        out_specs=(whole,) * 3,
        scratch_shapes=[*scratch(split), *ahead, pltpu.VMEM((split, p, width), BF16)],
        input_output_aliases={4: 0, 5: 1},
        compiler_params=params,
        name="far",
    )(*map(vmem, ins), smem(plan0))
    ins = [far1, w_all, qt, top, acc, tiled, w_last, held]
    _, _, result = pl.pallas_call(
        last_kernel,
        out_shape=(*state, pltpu.HBM((1, by, bz, p, width), BF16)),
        in_specs=[*(whole,) * len(ins), words],
        out_specs=(whole, whole, apart),
        scratch_shapes=[
            *scratch(by - split),
            *ahead,
            pltpu.VMEM((by - early, p, width), BF16),
            pltpu.SemaphoreType.DMA((4 * by,)),
        ],
        input_output_aliases={3: 0, 4: 1},
        compiler_params=params,
        name="last",
    )(*map(vmem, ins), smem(plan1))
    return result


def solution(mesh):
    placed = (
        P(("groups", "gx"), None, None, None, None),
        P(("groups", "gx"), None, None, None),
        P(("groups", "gx"), None, None, None),
        P("groups", None, None),
        P(),
        P(),
        P(),
        P(),
    )
    return jax.shard_map(
        functools.partial(shards, mesh.shape["gx"]),
        mesh=mesh,
        in_specs=placed,
        out_specs=P(("groups", "gx"), None, None, None, None),
        check_vma=False,
    )
```

```python
import functools

import jax
import jax.numpy as jnp
from jax import lax
from jax.experimental import pallas as pl
from jax.experimental.pallas import tpu as pltpu
from jax.sharding import PartitionSpec as P


HEADS = 8
NEG = -1e30
ONES = 16
LIMIT = 24 * 1024 * 1024
BF16, F32 = jnp.bfloat16, jnp.float32


def tn(a, b):
    return lax.dot_general(a, b, (((0,), (0,)), ((), ())), preferred_element_type=F32)


def nn(a, b):
    return jnp.dot(a, b, preferred_element_type=F32)


def normalise(tiled, gain, shift):
    values = tiled.astype(F32)
    mean = jnp.mean(values, axis=-1, keepdims=True)
    var = jnp.mean((values - mean) ** 2, axis=-1, keepdims=True)
    return ((values - mean) * lax.rsqrt(var + 1e-05) * gain + shift).astype(BF16)


def select(row, raw):
    p = raw.shape[0]
    slot = lax.broadcasted_iota(jnp.int32, (p, p), 0)
    return tn((slot == row).astype(F32).astype(BF16), raw).astype(BF16)


def gather_kernel(points, order, counts, gain, shift, first, rest, places, norm, raw, rows, live, sems):
    _, by, _, p, _ = points.shape
    split = first.shape[0]
    me = lax.axis_index("gx")
    small = [
        pltpu.make_async_copy(order, rows, sems.at[by]),
        pltpu.make_async_copy(counts, live, sems.at[by + 1]),
        pltpu.make_async_copy(gain, norm.at[0:1], sems.at[by + 2]),
        pltpu.make_async_copy(shift, norm.at[1:2], sems.at[by + 3]),
    ]
    large = [
        pltpu.make_async_copy(
            points.at[0, j, 0], raw.at[j] if j < split else rest.at[j - split], sems.at[j]
        )
        for j in range(by)
    ]
    for copy in (*small[:2], *large, *small[2:]):
        copy.start()
    place = lax.broadcasted_iota(jnp.int32, (1, p), 1)
    small[0].wait()
    small[1].wait()
    picks = []
    for j in range(by):
        row = rows[0, j]
        picks.append(jnp.where(place < live[j, 0, me], row, row[:, :1]))
        if j >= split:
            places[j - split] = picks[j]
    for j in range(split):
        large[j].wait()
    for j in range(split):
        first[j] = select(picks[j], raw[j])
    for copy in (*large[split:], *small[2:]):
        copy.wait()


def rest_kernel(first, rest, places, norm, tiled, normed, second):
    split = first.shape[0]
    gain, shift = norm[0:1], norm[1:2]
    for j in range(rest.shape[0]):
        got = select(places[j], rest[j])
        tiled[split + j] = got
        got = normalise(got, gain, shift)
        second[j] = got
        normed[split + j] = got
    for j in range(split):
        got = first[j]
        tiled[j] = got
        normed[j] = normalise(got, gain, shift)


def toward_near():
    return 1 - 2 * (lax.axis_index("gx") & 1)


def column(side, b):
    index = 9 * (side + 1) + 3 * (b + 1) + 1
    if isinstance(index, int):
        return index if index < 13 else index - 1
    return jnp.where(index > 13, index - 1, index)


def list_pairs(items, masks, by, sides):
    pairs, singles = jnp.int32(0), jnp.int32(0)
    for i in range(by):
        found, last, most = jnp.int32(0), jnp.int32(0), 0
        for side, exists, j0, j1, tile0, own in sides:
            for b in (0, -1, 1):
                j = i + b
                if not j0 <= j < j1:
                    continue
                tile = tile0 + j - j0
                items[1, 2 * pairs + found] = tile
                most += 1
                if own and b == 0:
                    found = found + 1
                    last = jnp.int32(tile)
                    continue
                on = masks[0, i, 0, column(side, b)] == 1
                on = on if exists is None else on & exists
                found = found + on.astype(jnp.int32)
                last = jnp.where(on, tile, last)
        items[2, 2 * singles] = i
        items[2, 2 * singles + 1] = last
        for u in range(most // 2):
            items[0, pairs + u] = i
        pairs = pairs + (found >> 1)
        singles = singles + (found & 1)
    items[0, pairs] = 0
    for u in range(2):
        items[1, 2 * pairs + u] = 0
        items[2, 2 * singles + u] = 0
    return pairs, singles


def meetings(by, j0, j1):
    found, number = {}, 0
    for i in range(by):
        for b in (0, -1, 1):
            if j0 <= i + b < j1:
                found.setdefault(i, []).append((number, i + b))
                number += 1
    return found


def mark(plan, masks, by, side, exists, j0, j1):
    for i, ends in meetings(by, j0, j1).items():
        for number, j in ends:
            on = (masks[0, i, 0, column(side, j - i)] == 1) & exists
            plan[1, number] = on.astype(jnp.int32)
            plan[0, number] = jnp.where(on, j - j0, j1 - j0)


def attend(items, pairs, singles, keys, vals, qt, top, acc, scores, peaks):
    groups, depth, lanes = qt.shape[1:]
    hd, p = depth // 2, lanes // 2
    lead = groups // 2

    def run(count, tiles, entry):
        def score(t, g):
            i, picked = entry(t)
            rows = slice(g * depth, (g + 1) * depth)
            cols = slice(g * lanes, (g + 1) * lanes)
            peak = None
            for u, k in enumerate(picked):
                made = nn(keys[k, :, rows], qt[i, g])
                scores[u * p : (u + 1) * p, cols] = made
                peak = made if peak is None else jnp.maximum(peak, made)
            peaks[:, cols] = jnp.max(peak, axis=0, keepdims=True)

        def weigh(t, g):
            i, picked = entry(t)
            cols = slice(g * lanes, (g + 1) * lanes)
            old = top[i, :, cols]
            new = jnp.maximum(old, peaks[:, cols])
            probs = jnp.exp(scores[: tiles * p, cols] - new).astype(BF16)
            fade = jnp.exp(old - new)
            both, sums = [], []
            for h in range(2):
                rows = slice(h * (hd + ONES), (h + 1) * (hd + ONES))
                val = jnp.concatenate([vals[k, g, rows] for k in picked], axis=1)
                out = nn(val, probs[:, h * p : (h + 1) * p])
                both.append(out[:hd])
                sums.append(out[hd : hd + 8])
            return cols, new, fade, jnp.concatenate(both, axis=1), jnp.concatenate(sums, axis=1)

        def step(t, carry):
            made = []
            for g in range(0, groups, lead):
                for u in range(g, g + lead):
                    score(t + (u + lead) // groups, (u + lead) % groups)
                for u in range(g, g + lead):
                    made.append(weigh(t, u))
            i, _ = entry(t)
            for cols, new, fade, both, sums in made:
                top[i, :, cols] = new
                acc[i, :hd, cols] = acc[i, :hd, cols] * fade + both
                acc[i, hd:, cols] = acc[i, hd:, cols] * fade + sums
            return carry

        for g in range(lead):
            score(0, g)
        lax.fori_loop(0, count, step, 0)

    run(pairs, 2, lambda t: (items[0, t], (items[1, 2 * t], items[1, 2 * t + 1])))
    run(singles, 1, lambda t: (items[2, 2 * t], (items[2, 2 * t + 1],)))


def put_values(vals, tile, g0, v, live):
    p = vals.shape[3]
    hd = vals.shape[2] // 2 - ONES
    flag = jnp.broadcast_to(live.astype(F32).astype(BF16), (ONES, p))
    vt = jnp.where(live, v.T, 0.0).astype(BF16)
    for h in range(v.shape[1] // hd):
        g, r = g0 + h // 2, h % 2 * (hd + ONES)
        vals[tile, g, r : r + hd] = vt[h * hd : (h + 1) * hd]
        vals[tile, g, r + hd : r + hd + ONES] = flag


def put_blocks(tile0, x, w_all, keys, vals, lives):
    p, width = keys.shape[1:]
    wide = min(512, width)
    groups = vals.shape[1]
    for c in range(0, width, wide):
        k = nn(x, w_all[:, width + c : width + c + wide]).astype(BF16)
        v = nn(x, w_all[:, 2 * width + c : 2 * width + c + wide])
        for u, live in enumerate(lives):
            rows = slice(u * p, (u + 1) * p)
            keys[tile0 + u, :, c : c + wide] = k[rows]
            put_values(vals, tile0 + u, c * groups // width, v[rows], live)


def finish(blocks, tiled, acc, w_out, plan):
    hd = acc.shape[1] - 8
    p = tiled.shape[1]
    heads = acc.shape[2] // p
    columns = []
    for i in blocks:
        attn = acc[i, :hd] * (1.0 / acc[i, hd : hd + 1])
        attn = [attn[:, h * p : (h + 1) * p] for h in range(heads)]
        columns.append(jnp.concatenate(attn, axis=0).astype(BF16))
    mixed = tn(jnp.concatenate(columns, axis=1), w_out[...])
    place = lax.broadcasted_iota(jnp.int32, (p, 1), 0)
    made = []
    for u, i in enumerate(blocks):
        value = tiled[i].astype(F32) + mixed[u * p : (u + 1) * p]
        made.append(jnp.where(place < plan[3, 1 + i], value, 0.0).astype(BF16))
    return made


def own_kernel(
    n, split, own, masks, counts, w_qkv, w_out, qt, top, acc, w_all, w_last, plan_near, plan0, plan1, keys, vals,
    items, flags, live, scores, peaks, sems
):
    by, p, width = own.shape
    _, depth = qt.shape[1:3]
    hd = depth // 2
    copies = [
        pltpu.make_async_copy(masks, flags, sems.at[0]),
        pltpu.make_async_copy(counts, live, sems.at[1]),
        pltpu.make_async_copy(w_qkv, w_all, sems.at[2]),
        pltpu.make_async_copy(w_out, w_last, sems.at[3]),
    ]
    for copy in copies:
        copy.start()
    me = lax.axis_index("gx")
    side = toward_near()
    place = lax.broadcasted_iota(jnp.int32, (1, p), 1)
    top[...] = jnp.full_like(top, NEG)
    acc[...] = jnp.zeros_like(acc)
    copies[0].wait()
    copies[1].wait()
    pairs, singles = list_pairs(items, flags, by, [(0, None, 0, by, 0, True)])
    for plan, a, j0, j1 in ((plan_near, side, 0, by), (plan0, -side, 0, split), (plan1, -side, split, by)):
        there = (me + a >= 0) & (me + a < n)
        slab = jnp.clip(me + a, 0, n - 1)
        if plan is plan1:
            mark(plan, flags, by, a, there, j0, j1)
        else:
            plan[3, 0], plan[3, 1 + 2 * by] = list_pairs(plan, flags, by, [(a, there, j0, j1, 0, False)])
        for i in range(by):
            plan[3, 1 + i] = live[i, 0, me]
        for j in range(j0, j1):
            plan[3, 1 + by + j - j0] = live[j, 0, slab]
    zeros = jnp.zeros((hd, p), BF16)
    copies[2].wait()
    mine = own[...].reshape(by * p, width)
    wide = min(512, width)
    for c in range(0, width, wide):
        q = (nn(mine, w_all[:, c : c + wide]).astype(BF16) * BF16(1.0 / hd**0.5)).astype(F32)
        for i in range(by):
            t = q[i * p : (i + 1) * p].T.astype(BF16)
            for u in range(wide // depth):
                g, mid = c // depth + u, u * depth + hd
                qt[i, g, :hd, :p] = t[mid - hd : mid]
                qt[i, g, :hd, p:] = zeros
                qt[i, g, hd:, :p] = zeros
                qt[i, g, hd:, p:] = t[mid : mid + hd]
    put_blocks(0, mine, w_all, keys, vals, [place < live[i, 0, me] for i in range(by)])
    attend(items, pairs, singles, keys, vals, qt, top, acc, scores, peaks)
    copies[3].wait()


def far_work(rim, w_all, qt, plan, top, acc, keys, vals, scores, peaks):
    by = qt.shape[0]
    blocks, p, width = rim.shape
    place = lax.broadcasted_iota(jnp.int32, (1, p), 1)
    put_blocks(0, rim[...].reshape(blocks * p, width), w_all, keys, vals, [place < plan[3, 1 + by + j] for j in range(blocks)])
    attend(plan, plan[3, 0], plan[3, 1 + 2 * by], keys, vals, qt, top, acc, scores, peaks)


def near_kernel(rim, w_all, qt, top_in, acc_in, plan, top, acc, keys, vals, scores, peaks):
    far_work(rim, w_all, qt, plan, top, acc, keys, vals, scores, peaks)


def far_kernel(
    rim, norm, w_all, qt, top_in, acc_in, tiled, w_out, plan, top, acc, held, keys, vals, scores, peaks, nrm
):
    for j in range(rim.shape[0]):
        nrm[j] = normalise(rim[j], norm[0:1], norm[1:2])
    far_work(nrm, w_all, qt, plan, top, acc, keys, vals, scores, peaks)
    for i, value in enumerate(finish(range(held.shape[0]), tiled, acc, w_out, plan)):
        held[i] = value


def last_kernel(
    rim, w_all, qt, top, acc, tiled, w_out, held, plan, result, keys, vals, scores, out, sems
):
    by, early = tiled.shape[0], held.shape[0]
    blocks, p, width = rim.shape
    groups, depth, lanes = qt.shape[1:]
    hd = depth // 2
    copies = [pltpu.make_async_copy(held.at[i], result.at[0, i, 0], sems.at[i]) for i in range(early)]
    for copy in copies:
        copy.start()
    place = lax.broadcasted_iota(jnp.int32, (1, p), 1)
    vals[blocks] = jnp.zeros(vals.shape[1:], BF16)
    lives = [place < plan[3, 1 + by + j] for j in range(blocks)]
    put_blocks(0, rim[...].reshape(blocks * p, width), w_all, keys, vals, lives)
    met = meetings(by, by - blocks, by)
    units = [(i, g) for i in met for g in range(groups)]
    peaks, parts = {}, {}

    def score(u):
        i, g = units[u]
        rows = slice(g * depth, (g + 1) * depth)
        peak = None
        for t, (number, j) in enumerate(met[i]):
            made = nn(keys[j - (by - blocks), :, rows], qt[i, g])
            scores[u % 4, t * p : (t + 1) * p] = made
            high = jnp.where(plan[1, number] == 1, jnp.max(made, axis=0, keepdims=True), NEG)
            peak = high if peak is None else jnp.maximum(peak, high)
        peaks[u] = peak

    def weigh(u):
        i, g = units[u]
        cols = slice(g * lanes, (g + 1) * lanes)
        old = top[i, :, cols]
        new = jnp.maximum(old, peaks[u])
        probs = jnp.exp(jnp.minimum(scores[u % 4, : len(met[i]) * p] - new, 0.0)).astype(BF16)
        fade = jnp.exp(old - new)
        for h in range(2):
            rows = slice(h * (hd + ONES), (h + 1) * (hd + ONES))
            mine = slice(h * p, (h + 1) * p)
            val = jnp.concatenate([vals[plan[0, number], g, rows] for number, _ in met[i]], axis=1)
            made = nn(val, probs[:, mine])
            there = slice(g * lanes + h * p, g * lanes + (h + 1) * p)
            total = acc[i, hd : hd + 1, there] * fade[:, mine] + made[hd : hd + 1]
            value = acc[i, :hd, there] * fade[:, mine] + made[:hd]
            parts[i, 2 * g + h] = (value * (1.0 / total)).astype(BF16)

    def deliver(i):
        attn = jnp.concatenate([parts[i, h] for h in range(2 * groups)], axis=0)
        mixed = tiled[i].astype(F32) + tn(attn, w_out[...])
        rows = lax.broadcasted_iota(jnp.int32, (p, 1), 0)
        out[i - early] = jnp.where(rows < plan[3, 1 + i], mixed, 0.0).astype(BF16)
        copies.append(pltpu.make_async_copy(out.at[i - early], result.at[0, i, 0], sems.at[i]))
        copies[-1].start()

    ahead = 3
    for u in range(ahead):
        score(u)
    for u in range(len(units)):
        if u + ahead < len(units):
            score(u + ahead)
        weigh(u)
    for i in met:
        deliver(i)
    for copy in copies:
        copy.wait()


def vmem(x):
    return pltpu.with_memory_space_constraint(x, pltpu.VMEM)


def smem(x):
    return pltpu.with_memory_space_constraint(x, pltpu.SMEM)


def hbm(x):
    return pltpu.with_memory_space_constraint(x, pltpu.HBM)


def shards(n, points, order, masks, counts, gain, shift_bias, w_qkv, w_out):
    _, by, bz, p, width = points.shape
    hd = width // HEADS
    groups, depth, lanes = HEADS // 2, 2 * hd, 2 * p
    split = max(by - 2, 1)
    early = max(split - 1, 1)
    whole = pl.BlockSpec(memory_space=pltpu.VMEM)
    apart = pl.BlockSpec(memory_space=pltpu.HBM)
    words = pl.BlockSpec(memory_space=pltpu.SMEM)
    plan = pltpu.SMEM((4, 8 * by), jnp.int32)
    params = pltpu.CompilerParams(vmem_limit_bytes=LIMIT)
    points, order, masks, w_qkv, w_out = map(hbm, (points, order, masks, w_qkv, w_out))
    counts = hbm(jnp.transpose(counts, (1, 2, 0)))
    live = pltpu.SMEM(counts.shape, jnp.int32)
    flags = pltpu.SMEM(masks.shape, jnp.int32)

    first, rest, places, norm = pl.pallas_call(
        gather_kernel,
        out_shape=(
            pltpu.VMEM((split, p, width), BF16),
            pltpu.VMEM((by - split, p, width), BF16),
            pltpu.VMEM((by - split, 1, p), jnp.int32),
            pltpu.VMEM((2, width), F32),
        ),
        in_specs=[apart] * 5,
        out_specs=(whole,) * 4,
        scratch_shapes=[
            pltpu.VMEM((split, p, width), BF16),
            pltpu.VMEM(order.shape, jnp.int32),
            live,
            pltpu.SemaphoreType.DMA((by + 4,)),
        ],
        compiler_params=params,
        name="gather",
    )(points, order, counts, hbm(gain[None]), hbm(shift_bias[None]))
    tile_rest = pl.pallas_call(
        rest_kernel,
        out_shape=(
            pltpu.VMEM((by, p, width), BF16),
            pltpu.VMEM((by, p, width), BF16),
            pltpu.VMEM((by - split, p, width), BF16),
        ),
        in_specs=[whole] * 4,
        out_specs=(whole,) * 3,
        compiler_params=params,
        name="rest",
    )
    tiled, normed, second = tile_rest(vmem(first), vmem(rest), vmem(places), vmem(norm))
    near_pairs = [(i, i ^ 1) for i in range(n) if i ^ 1 < n]
    far_pairs = [(i, i + 1) for i in range(1, n - 1, 2)] + [(i + 1, i) for i in range(1, n - 1, 2)]

    def moved(value, pairs):
        return lax.ppermute(value, "gx", pairs)

    far0 = moved(first, far_pairs)
    near = moved(normed, near_pairs)
    far1 = moved(second, far_pairs)

    state = (
        pltpu.VMEM((by, 1, groups * lanes), F32),
        pltpu.VMEM((by, hd + 8, groups * lanes), F32),
    )

    def scratch(tiles):
        return [
            pltpu.VMEM((tiles, p, width), BF16),
            pltpu.VMEM((tiles, groups, depth + 2 * ONES, p), BF16),
        ]

    ahead = [
        pltpu.VMEM((2 * p, groups * lanes), F32),
        pltpu.VMEM((1, groups * lanes), F32),
    ]
    own_work = pl.pallas_call(
        functools.partial(own_kernel, n, split),
        out_shape=(
            pltpu.VMEM((by, groups, depth, lanes), BF16),
            *state,
            pltpu.VMEM(w_qkv.shape, BF16),
            pltpu.VMEM(w_out.shape, BF16),
            *(plan,) * 3,
        ),
        in_specs=[whole, apart, apart, apart, apart],
        out_specs=(whole,) * 5 + (words,) * 3,
        scratch_shapes=[*scratch(by), plan, flags, live, *ahead, pltpu.SemaphoreType.DMA((4,))],
        compiler_params=params,
        name="own",
    )
    near_work = pl.pallas_call(
        near_kernel,
        out_shape=state,
        in_specs=[*(whole,) * 5, words],
        out_specs=(whole,) * 2,
        scratch_shapes=[*scratch(by), *ahead],
        input_output_aliases={3: 0, 4: 1},
        compiler_params=params,
        name="near",
    )
    qt, top, acc, w_all, w_last, plan_near, plan0, plan1 = own_work(
        vmem(normed), masks, counts, w_qkv, w_out
    )
    top, acc = near_work(*map(vmem, (near, w_all, qt, top, acc)), smem(plan_near))
    ins = [far0, norm, w_all, qt, top, acc, tiled, w_last]
    top, acc, held = pl.pallas_call(
        far_kernel,
        out_shape=(*state, pltpu.VMEM((early, p, width), BF16)),
        in_specs=[*(whole,) * len(ins), words],
        out_specs=(whole,) * 3,
        scratch_shapes=[*scratch(split), *ahead, pltpu.VMEM((split, p, width), BF16)],
        input_output_aliases={4: 0, 5: 1},
        compiler_params=params,
        name="far",
    )(*map(vmem, ins), smem(plan0))
    ins = [far1, w_all, qt, top, acc, tiled, w_last, held]
    return pl.pallas_call(
        last_kernel,
        out_shape=pltpu.HBM((1, by, bz, p, width), BF16),
        in_specs=[*(whole,) * len(ins), words],
        out_specs=apart,
        scratch_shapes=[
            pltpu.VMEM((by - split, p, width), BF16),
            pltpu.VMEM((by - split + 1, groups, depth + 2 * ONES, p), BF16),
            pltpu.VMEM((4, 3 * p, lanes), F32),
            pltpu.VMEM((by - early, p, width), BF16),
            pltpu.SemaphoreType.DMA((by,)),
        ],
        compiler_params=params,
        name="last",
    )(*map(vmem, ins), smem(plan1))


def solution(mesh):
    placed = (
        P(("groups", "gx"), None, None, None, None),
        P(("groups", "gx"), None, None, None),
        P(("groups", "gx"), None, None, None),
        P("groups", None, None),
        P(),
        P(),
        P(),
        P(),
    )
    return jax.shard_map(
        functools.partial(shards, mesh.shape["gx"]),
        mesh=mesh,
        in_specs=placed,
        out_specs=P(("groups", "gx"), None, None, None, None),
        check_vma=False,
    )
```

```python
import functools

import jax
import jax.numpy as jnp
from jax import lax
from jax.experimental import pallas as pl
from jax.experimental.pallas import tpu as pltpu
from jax.sharding import PartitionSpec as P


HEADS = 8
NEG = -1e30
ONES = 16
LIMIT = 24 * 1024 * 1024
BF16, F32 = jnp.bfloat16, jnp.float32


def tn(a, b):
    return lax.dot_general(a, b, (((0,), (0,)), ((), ())), preferred_element_type=F32)


def nn(a, b):
    return jnp.dot(a, b, preferred_element_type=F32)


def normalise(tiled, gain, shift):
    values = tiled.astype(F32)
    mean = jnp.mean(values, axis=-1, keepdims=True)
    var = jnp.mean((values - mean) ** 2, axis=-1, keepdims=True)
    return ((values - mean) * lax.rsqrt(var + 1e-05) * gain + shift).astype(BF16)


def select(row, raw):
    p = raw.shape[0]
    slot = lax.broadcasted_iota(jnp.int32, (p, p), 0)
    return tn((slot == row).astype(F32).astype(BF16), raw).astype(BF16)


def gather_kernel(points, order, counts, gain, shift, first, rest, places, norm, raw, rows, live, sems):
    _, by, _, p, _ = points.shape
    split = first.shape[0]
    me = lax.axis_index("gx")
    small = [
        pltpu.make_async_copy(order, rows, sems.at[2]),
        pltpu.make_async_copy(counts, live, sems.at[3]),
        pltpu.make_async_copy(gain, norm.at[0:1], sems.at[4]),
        pltpu.make_async_copy(shift, norm.at[1:2], sems.at[5]),
    ]
    large = [
        pltpu.make_async_copy(points.at[0, :split, 0], raw, sems.at[0]),
        pltpu.make_async_copy(points.at[0, split:, 0], rest, sems.at[1]),
    ]
    for copy in (*small[:2], *large, *small[2:]):
        copy.start()
    place = lax.broadcasted_iota(jnp.int32, (1, p), 1)
    small[0].wait()
    small[1].wait()
    picks = []
    for j in range(by):
        row = rows[0, j]
        picks.append(jnp.where(place < live[j, 0, me], row, row[:, :1]))
        if j >= split:
            places[j - split] = picks[j]
    large[0].wait()
    for j in range(split):
        first[j] = select(picks[j], raw[j])
    for copy in (large[1], *small[2:]):
        copy.wait()


def rest_kernel(first, rest, places, norm, tiled, normed, second):
    split = first.shape[0]
    gain, shift = norm[0:1], norm[1:2]
    for j in range(rest.shape[0]):
        got = select(places[j], rest[j])
        tiled[split + j] = got
        got = normalise(got, gain, shift)
        second[j] = got
        normed[split + j] = got
    for j in range(split):
        got = first[j]
        tiled[j] = got
        normed[j] = normalise(got, gain, shift)


def toward_near():
    return 1 - 2 * (lax.axis_index("gx") & 1)


def column(side, b):
    index = 9 * (side + 1) + 3 * (b + 1) + 1
    if isinstance(index, int):
        return index if index < 13 else index - 1
    return jnp.where(index > 13, index - 1, index)


def list_pairs(items, masks, by, sides):
    pairs, singles = jnp.int32(0), jnp.int32(0)
    for i in range(by):
        found, last, most = jnp.int32(0), jnp.int32(0), 0
        for side, exists, j0, j1, tile0, own in sides:
            for b in (0, -1, 1):
                j = i + b
                if not j0 <= j < j1:
                    continue
                tile = tile0 + j - j0
                items[1, 2 * pairs + found] = tile
                most += 1
                if own and b == 0:
                    found = found + 1
                    last = jnp.int32(tile)
                    continue
                on = masks[0, i, 0, column(side, b)] == 1
                on = on if exists is None else on & exists
                found = found + on.astype(jnp.int32)
                last = jnp.where(on, tile, last)
        items[2, 2 * singles] = i
        items[2, 2 * singles + 1] = last
        for u in range(most // 2):
            items[0, pairs + u] = i
        pairs = pairs + (found >> 1)
        singles = singles + (found & 1)
    items[0, pairs] = 0
    for u in range(2):
        items[1, 2 * pairs + u] = 0
        items[2, 2 * singles + u] = 0
    return pairs, singles


def meetings(by, j0, j1):
    found, number = {}, 0
    for i in range(by):
        for b in (0, -1, 1):
            if j0 <= i + b < j1:
                found.setdefault(i, []).append((number, i + b))
                number += 1
    return found


def mark(plan, masks, by, side, exists, j0, j1):
    for i, ends in meetings(by, j0, j1).items():
        for number, j in ends:
            on = (masks[0, i, 0, column(side, j - i)] == 1) & exists
            plan[1, number] = on.astype(jnp.int32)
            plan[0, number] = jnp.where(on, j - j0, j1 - j0)


def attend(items, pairs, singles, keys, vals, qt, top, acc, scores, peaks):
    groups, depth, lanes = qt.shape[1:]
    hd, p = depth // 2, lanes // 2
    lead = groups // 2

    def run(count, tiles, entry):
        def score(t, g):
            i, picked = entry(t)
            rows = slice(g * depth, (g + 1) * depth)
            cols = slice(g * lanes, (g + 1) * lanes)
            peak = None
            for u, k in enumerate(picked):
                made = nn(keys[k, :, rows], qt[i, g])
                scores[u * p : (u + 1) * p, cols] = made
                peak = made if peak is None else jnp.maximum(peak, made)
            peaks[:, cols] = jnp.max(peak, axis=0, keepdims=True)

        def weigh(t, g):
            i, picked = entry(t)
            cols = slice(g * lanes, (g + 1) * lanes)
            old = top[i, :, cols]
            new = jnp.maximum(old, peaks[:, cols])
            probs = jnp.exp(scores[: tiles * p, cols] - new).astype(BF16)
            fade = jnp.exp(old - new)
            both, sums = [], []
            for h in range(2):
                rows = slice(h * (hd + ONES), (h + 1) * (hd + ONES))
                val = jnp.concatenate([vals[k, g, rows] for k in picked], axis=1)
                out = nn(val, probs[:, h * p : (h + 1) * p])
                both.append(out[:hd])
                sums.append(out[hd : hd + 8])
            return cols, new, fade, jnp.concatenate(both, axis=1), jnp.concatenate(sums, axis=1)

        def step(t, carry):
            made = []
            for g in range(0, groups, lead):
                for u in range(g, g + lead):
                    score(t + (u + lead) // groups, (u + lead) % groups)
                for u in range(g, g + lead):
                    made.append(weigh(t, u))
            i, _ = entry(t)
            for cols, new, fade, both, sums in made:
                top[i, :, cols] = new
                acc[i, :hd, cols] = acc[i, :hd, cols] * fade + both
                acc[i, hd:, cols] = acc[i, hd:, cols] * fade + sums
            return carry

        for g in range(lead):
            score(0, g)
        lax.fori_loop(0, count, step, 0)

    run(pairs, 2, lambda t: (items[0, t], (items[1, 2 * t], items[1, 2 * t + 1])))
    run(singles, 1, lambda t: (items[2, 2 * t], (items[2, 2 * t + 1],)))


def put_values(vals, tile, g0, v, live):
    p = vals.shape[3]
    hd = vals.shape[2] // 2 - ONES
    flag = jnp.broadcast_to(live.astype(F32).astype(BF16), (ONES, p))
    vt = jnp.where(live, v.T, 0.0).astype(BF16)
    for h in range(v.shape[1] // hd):
        g, r = g0 + h // 2, h % 2 * (hd + ONES)
        vals[tile, g, r : r + hd] = vt[h * hd : (h + 1) * hd]
        vals[tile, g, r + hd : r + hd + ONES] = flag


def put_blocks(tile0, x, w_all, keys, vals, lives):
    p, width = keys.shape[1:]
    wide = min(512, width)
    groups = vals.shape[1]
    for c in range(0, width, wide):
        k = nn(x, w_all[:, width + c : width + c + wide]).astype(BF16)
        v = nn(x, w_all[:, 2 * width + c : 2 * width + c + wide])
        for u, live in enumerate(lives):
            rows = slice(u * p, (u + 1) * p)
            keys[tile0 + u, :, c : c + wide] = k[rows]
            put_values(vals, tile0 + u, c * groups // width, v[rows], live)


def finish(blocks, tiled, acc, w_out, plan):
    hd = acc.shape[1] - 8
    p = tiled.shape[1]
    heads = acc.shape[2] // p
    columns = []
    for i in blocks:
        attn = acc[i, :hd] * (1.0 / acc[i, hd : hd + 1])
        attn = [attn[:, h * p : (h + 1) * p] for h in range(heads)]
        columns.append(jnp.concatenate(attn, axis=0).astype(BF16))
    mixed = tn(jnp.concatenate(columns, axis=1), w_out[...])
    place = lax.broadcasted_iota(jnp.int32, (p, 1), 0)
    made = []
    for u, i in enumerate(blocks):
        value = tiled[i].astype(F32) + mixed[u * p : (u + 1) * p]
        made.append(jnp.where(place < plan[3, 1 + i], value, 0.0).astype(BF16))
    return made


def own_kernel(
    n, split, own, masks, counts, w_qkv, w_out, qt, top, acc, w_all, w_last, plan_near, plan0, plan1, keys, vals,
    items, flags, live, scores, peaks, sems
):
    by, p, width = own.shape
    _, depth = qt.shape[1:3]
    hd = depth // 2
    copies = [
        pltpu.make_async_copy(masks, flags, sems.at[0]),
        pltpu.make_async_copy(counts, live, sems.at[1]),
        pltpu.make_async_copy(w_qkv, w_all, sems.at[2]),
        pltpu.make_async_copy(w_out, w_last, sems.at[3]),
    ]
    for copy in copies:
        copy.start()
    me = lax.axis_index("gx")
    side = toward_near()
    place = lax.broadcasted_iota(jnp.int32, (1, p), 1)
    top[...] = jnp.full_like(top, NEG)
    acc[...] = jnp.zeros_like(acc)
    copies[0].wait()
    copies[1].wait()
    pairs, singles = list_pairs(items, flags, by, [(0, None, 0, by, 0, True)])
    for plan, a, j0, j1 in ((plan_near, side, 0, by), (plan0, -side, 0, split), (plan1, -side, split, by)):
        there = (me + a >= 0) & (me + a < n)
        slab = jnp.clip(me + a, 0, n - 1)
        if plan is plan1:
            mark(plan, flags, by, a, there, j0, j1)
        else:
            plan[3, 0], plan[3, 1 + 2 * by] = list_pairs(plan, flags, by, [(a, there, j0, j1, 0, False)])
        for i in range(by):
            plan[3, 1 + i] = live[i, 0, me]
        for j in range(j0, j1):
            plan[3, 1 + by + j - j0] = live[j, 0, slab]
    zeros = jnp.zeros((hd, p), BF16)
    copies[2].wait()
    mine = own[...].reshape(by * p, width)
    wide = min(512, width)
    for c in range(0, width, wide):
        q = (nn(mine, w_all[:, c : c + wide]).astype(BF16) * BF16(1.0 / hd**0.5)).astype(F32)
        for i in range(by):
            t = q[i * p : (i + 1) * p].T.astype(BF16)
            for u in range(wide // depth):
                g, mid = c // depth + u, u * depth + hd
                qt[i, g, :hd, :p] = t[mid - hd : mid]
                qt[i, g, :hd, p:] = zeros
                qt[i, g, hd:, :p] = zeros
                qt[i, g, hd:, p:] = t[mid : mid + hd]
    put_blocks(0, mine, w_all, keys, vals, [place < live[i, 0, me] for i in range(by)])
    attend(items, pairs, singles, keys, vals, qt, top, acc, scores, peaks)
    copies[3].wait()


def far_work(rim, w_all, qt, plan, top, acc, keys, vals, scores, peaks):
    by = qt.shape[0]
    blocks, p, width = rim.shape
    place = lax.broadcasted_iota(jnp.int32, (1, p), 1)
    put_blocks(0, rim[...].reshape(blocks * p, width), w_all, keys, vals, [place < plan[3, 1 + by + j] for j in range(blocks)])
    attend(plan, plan[3, 0], plan[3, 1 + 2 * by], keys, vals, qt, top, acc, scores, peaks)


def near_kernel(rim, w_all, qt, top_in, acc_in, plan, top, acc, keys, vals, scores, peaks):
    far_work(rim, w_all, qt, plan, top, acc, keys, vals, scores, peaks)


def far_kernel(
    rim, norm, w_all, qt, top_in, acc_in, tiled, w_out, plan, top, acc, held, keys, vals, scores, peaks, nrm
):
    for j in range(rim.shape[0]):
        nrm[j] = normalise(rim[j], norm[0:1], norm[1:2])
    far_work(nrm, w_all, qt, plan, top, acc, keys, vals, scores, peaks)
    for i, value in enumerate(finish(range(held.shape[0]), tiled, acc, w_out, plan)):
        held[i] = value


def last_kernel(
    rim, w_all, qt, top, acc, tiled, w_out, held, plan, result, keys, vals, scores, out, sems
):
    by, early = tiled.shape[0], held.shape[0]
    blocks, p, width = rim.shape
    groups, depth, lanes = qt.shape[1:]
    hd = depth // 2
    copies = [pltpu.make_async_copy(held.at[i], result.at[0, i, 0], sems.at[i]) for i in range(early)]
    for copy in copies:
        copy.start()
    place = lax.broadcasted_iota(jnp.int32, (1, p), 1)
    vals[blocks] = jnp.zeros(vals.shape[1:], BF16)
    lives = [place < plan[3, 1 + by + j] for j in range(blocks)]
    put_blocks(0, rim[...].reshape(blocks * p, width), w_all, keys, vals, lives)
    met = meetings(by, by - blocks, by)
    units = [(i, g) for i in met for g in range(groups)]
    peaks, parts = {}, {}

    def score(u):
        i, g = units[u]
        rows = slice(g * depth, (g + 1) * depth)
        peak = None
        for t, (number, j) in enumerate(met[i]):
            made = nn(keys[j - (by - blocks), :, rows], qt[i, g])
            scores[u % 8, t * p : (t + 1) * p] = made
            high = jnp.where(plan[1, number] == 1, jnp.max(made, axis=0, keepdims=True), NEG)
            peak = high if peak is None else jnp.maximum(peak, high)
        peaks[u] = peak

    def weigh(u):
        i, g = units[u]
        cols = slice(g * lanes, (g + 1) * lanes)
        old = top[i, :, cols]
        new = jnp.maximum(old, peaks[u])
        probs = jnp.exp(jnp.minimum(scores[u % 8, : len(met[i]) * p] - new, 0.0)).astype(BF16)
        fade = jnp.exp(old - new)
        for h in range(2):
            rows = slice(h * (hd + ONES), (h + 1) * (hd + ONES))
            mine = slice(h * p, (h + 1) * p)
            val = jnp.concatenate([vals[plan[0, number], g, rows] for number, _ in met[i]], axis=1)
            made = nn(val, probs[:, mine])
            there = slice(g * lanes + h * p, g * lanes + (h + 1) * p)
            total = acc[i, hd : hd + 1, there] * fade[:, mine] + made[hd : hd + 1]
            value = acc[i, :hd, there] * fade[:, mine] + made[:hd]
            parts[i, 2 * g + h] = (value * (1.0 / total)).astype(BF16)

    def deliver(i):
        attn = jnp.concatenate([parts[i, h] for h in range(2 * groups)], axis=0)
        mixed = tiled[i].astype(F32) + tn(attn, w_out[...])
        rows = lax.broadcasted_iota(jnp.int32, (p, 1), 0)
        out[i - early] = jnp.where(rows < plan[3, 1 + i], mixed, 0.0).astype(BF16)
        copies.append(pltpu.make_async_copy(out.at[i - early], result.at[0, i, 0], sems.at[i]))
        copies[-1].start()

    ahead = 6
    for u in range(ahead):
        score(u)
    for u in range(len(units)):
        if u + ahead < len(units):
            score(u + ahead)
        weigh(u)
    for i in met:
        deliver(i)
    for copy in copies:
        copy.wait()


def vmem(x):
    return pltpu.with_memory_space_constraint(x, pltpu.VMEM)


def smem(x):
    return pltpu.with_memory_space_constraint(x, pltpu.SMEM)


def hbm(x):
    return pltpu.with_memory_space_constraint(x, pltpu.HBM)


def shards(n, points, order, masks, counts, gain, shift_bias, w_qkv, w_out):
    _, by, bz, p, width = points.shape
    hd = width // HEADS
    groups, depth, lanes = HEADS // 2, 2 * hd, 2 * p
    split = max(by // 2, 1)
    early = max(split - 1, 1)
    whole = pl.BlockSpec(memory_space=pltpu.VMEM)
    apart = pl.BlockSpec(memory_space=pltpu.HBM)
    words = pl.BlockSpec(memory_space=pltpu.SMEM)
    plan = pltpu.SMEM((4, 8 * by), jnp.int32)
    params = pltpu.CompilerParams(vmem_limit_bytes=LIMIT)
    points, order, masks, w_qkv, w_out = map(hbm, (points, order, masks, w_qkv, w_out))
    counts = hbm(jnp.transpose(counts, (1, 2, 0)))
    live = pltpu.SMEM(counts.shape, jnp.int32)
    flags = pltpu.SMEM(masks.shape, jnp.int32)

    first, rest, places, norm = pl.pallas_call(
        gather_kernel,
        out_shape=(
            pltpu.VMEM((split, p, width), BF16),
            pltpu.VMEM((by - split, p, width), BF16),
            pltpu.VMEM((by - split, 1, p), jnp.int32),
            pltpu.VMEM((2, width), F32),
        ),
        in_specs=[apart] * 5,
        out_specs=(whole,) * 4,
        scratch_shapes=[
            pltpu.VMEM((split, p, width), BF16),
            pltpu.VMEM(order.shape, jnp.int32),
            live,
            pltpu.SemaphoreType.DMA((6,)),
        ],
        compiler_params=params,
        name="gather",
    )(points, order, counts, hbm(gain[None]), hbm(shift_bias[None]))
    tile_rest = pl.pallas_call(
        rest_kernel,
        out_shape=(
            pltpu.VMEM((by, p, width), BF16),
            pltpu.VMEM((by, p, width), BF16),
            pltpu.VMEM((by - split, p, width), BF16),
        ),
        in_specs=[whole] * 4,
        out_specs=(whole,) * 3,
        compiler_params=params,
        name="rest",
    )
    tiled, normed, second = tile_rest(vmem(first), vmem(rest), vmem(places), vmem(norm))
    near_pairs = [(i, i ^ 1) for i in range(n) if i ^ 1 < n]
    far_pairs = [(i, i + 1) for i in range(1, n - 1, 2)] + [(i + 1, i) for i in range(1, n - 1, 2)]

    def moved(value, pairs):
        return lax.ppermute(value, "gx", pairs)

    far0 = moved(first, far_pairs)
    near = moved(normed, near_pairs)
    far1 = moved(second, far_pairs)

    state = (
        pltpu.VMEM((by, 1, groups * lanes), F32),
        pltpu.VMEM((by, hd + 8, groups * lanes), F32),
    )

    def scratch(tiles):
        return [
            pltpu.VMEM((tiles, p, width), BF16),
            pltpu.VMEM((tiles, groups, depth + 2 * ONES, p), BF16),
        ]

    ahead = [
        pltpu.VMEM((2 * p, groups * lanes), F32),
        pltpu.VMEM((1, groups * lanes), F32),
    ]
    own_work = pl.pallas_call(
        functools.partial(own_kernel, n, split),
        out_shape=(
            pltpu.VMEM((by, groups, depth, lanes), BF16),
            *state,
            pltpu.VMEM(w_qkv.shape, BF16),
            pltpu.VMEM(w_out.shape, BF16),
            *(plan,) * 3,
        ),
        in_specs=[whole, apart, apart, apart, apart],
        out_specs=(whole,) * 5 + (words,) * 3,
        scratch_shapes=[*scratch(by), plan, flags, live, *ahead, pltpu.SemaphoreType.DMA((4,))],
        compiler_params=params,
        name="own",
    )
    near_work = pl.pallas_call(
        near_kernel,
        out_shape=state,
        in_specs=[*(whole,) * 5, words],
        out_specs=(whole,) * 2,
        scratch_shapes=[*scratch(by), *ahead],
        input_output_aliases={3: 0, 4: 1},
        compiler_params=params,
        name="near",
    )
    qt, top, acc, w_all, w_last, plan_near, plan0, plan1 = own_work(
        vmem(normed), masks, counts, w_qkv, w_out
    )
    top, acc = near_work(*map(vmem, (near, w_all, qt, top, acc)), smem(plan_near))
    ins = [far0, norm, w_all, qt, top, acc, tiled, w_last]
    top, acc, held = pl.pallas_call(
        far_kernel,
        out_shape=(*state, pltpu.VMEM((early, p, width), BF16)),
        in_specs=[*(whole,) * len(ins), words],
        out_specs=(whole,) * 3,
        scratch_shapes=[*scratch(split), *ahead, pltpu.VMEM((split, p, width), BF16)],
        input_output_aliases={4: 0, 5: 1},
        compiler_params=params,
        name="far",
    )(*map(vmem, ins), smem(plan0))
    ins = [far1, w_all, qt, top, acc, tiled, w_last, held]
    return pl.pallas_call(
        last_kernel,
        out_shape=pltpu.HBM((1, by, bz, p, width), BF16),
        in_specs=[*(whole,) * len(ins), words],
        out_specs=apart,
        scratch_shapes=[
            pltpu.VMEM((by - split, p, width), BF16),
            pltpu.VMEM((by - split + 1, groups, depth + 2 * ONES, p), BF16),
            pltpu.VMEM((8, 3 * p, lanes), F32),
            pltpu.VMEM((by - early, p, width), BF16),
            pltpu.SemaphoreType.DMA((by,)),
        ],
        compiler_params=params,
        name="last",
    )(*map(vmem, ins), smem(plan1))


def solution(mesh):
    placed = (
        P(("groups", "gx"), None, None, None, None),
        P(("groups", "gx"), None, None, None),
        P(("groups", "gx"), None, None, None),
        P("groups", None, None),
        P(),
        P(),
        P(),
        P(),
    )
    return jax.shard_map(
        functools.partial(shards, mesh.shape["gx"]),
        mesh=mesh,
        in_specs=placed,
        out_specs=P(("groups", "gx"), None, None, None, None),
        check_vma=False,
    )
```

```python
import functools

import jax
import jax.numpy as jnp
from jax import lax
from jax.experimental import pallas as pl
from jax.experimental.pallas import tpu as pltpu
from jax.sharding import PartitionSpec as P


HEADS = 8
NEG = -1e30
ONES = 16
LIMIT = 24 * 1024 * 1024
BF16, F32 = jnp.bfloat16, jnp.float32


def tn(a, b):
    return lax.dot_general(a, b, (((0,), (0,)), ((), ())), preferred_element_type=F32)


def nn(a, b):
    return jnp.dot(a, b, preferred_element_type=F32)


def normalise(tiled, gain, shift):
    values = tiled.astype(F32)
    mean = jnp.mean(values, axis=-1, keepdims=True)
    var = jnp.mean((values - mean) ** 2, axis=-1, keepdims=True)
    return ((values - mean) * lax.rsqrt(var + 1e-05) * gain + shift).astype(BF16)


def select(row, raw):
    p = raw.shape[0]
    slot = lax.broadcasted_iota(jnp.int32, (p, p), 0)
    return tn((slot == row).astype(F32).astype(BF16), raw).astype(BF16)


def gather_kernel(points, order, counts, gain, shift, first, rest, places, norm, raw, rows, live, sems):
    _, by, _, p, _ = points.shape
    split = first.shape[0]
    me = lax.axis_index("gx")
    small = [
        pltpu.make_async_copy(order, rows, sems.at[2]),
        pltpu.make_async_copy(counts, live, sems.at[3]),
        pltpu.make_async_copy(gain, norm.at[0:1], sems.at[4]),
        pltpu.make_async_copy(shift, norm.at[1:2], sems.at[5]),
    ]
    large = [
        pltpu.make_async_copy(points.at[0, :split, 0], raw, sems.at[0]),
        pltpu.make_async_copy(points.at[0, split:, 0], rest, sems.at[1]),
    ]
    for copy in (large[0], *small[:2], large[1], *small[2:]):
        copy.start()
    place = lax.broadcasted_iota(jnp.int32, (1, p), 1)
    small[0].wait()
    small[1].wait()
    picks = []
    for j in range(by):
        row = rows[0, j]
        picks.append(jnp.where(place < live[j, 0, me], row, row[:, :1]))
        if j >= split:
            places[j - split] = picks[j]
    large[0].wait()
    for j in range(split):
        first[j] = select(picks[j], raw[j])
    for copy in (large[1], *small[2:]):
        copy.wait()


def rest_kernel(first, rest, places, norm, tiled, normed, second):
    split = first.shape[0]
    gain, shift = norm[0:1], norm[1:2]
    for j in range(rest.shape[0]):
        got = select(places[j], rest[j])
        tiled[split + j] = got
        got = normalise(got, gain, shift)
        second[j] = got
        normed[split + j] = got
    for j in range(split):
        got = first[j]
        tiled[j] = got
        normed[j] = normalise(got, gain, shift)


def toward_near():
    return 1 - 2 * (lax.axis_index("gx") & 1)


def column(side, b):
    index = 9 * (side + 1) + 3 * (b + 1) + 1
    if isinstance(index, int):
        return index if index < 13 else index - 1
    return jnp.where(index > 13, index - 1, index)


def list_pairs(items, masks, by, sides):
    pairs, singles = jnp.int32(0), jnp.int32(0)
    for i in range(by):
        found, last, most = jnp.int32(0), jnp.int32(0), 0
        for side, exists, j0, j1, tile0, own in sides:
            for b in (0, -1, 1):
                j = i + b
                if not j0 <= j < j1:
                    continue
                tile = tile0 + j - j0
                items[1, 2 * pairs + found] = tile
                most += 1
                if own and b == 0:
                    found = found + 1
                    last = jnp.int32(tile)
                    continue
                on = masks[0, i, 0, column(side, b)] == 1
                on = on if exists is None else on & exists
                found = found + on.astype(jnp.int32)
                last = jnp.where(on, tile, last)
        items[2, 2 * singles] = i
        items[2, 2 * singles + 1] = last
        for u in range(most // 2):
            items[0, pairs + u] = i
        pairs = pairs + (found >> 1)
        singles = singles + (found & 1)
    items[0, pairs] = 0
    for u in range(2):
        items[1, 2 * pairs + u] = 0
        items[2, 2 * singles + u] = 0
    return pairs, singles


def meetings(by, j0, j1):
    found, number = {}, 0
    for i in range(by):
        for b in (0, -1, 1):
            if j0 <= i + b < j1:
                found.setdefault(i, []).append((number, i + b))
                number += 1
    return found


def mark(plan, masks, by, side, exists, j0, j1):
    for i, ends in meetings(by, j0, j1).items():
        for number, j in ends:
            on = (masks[0, i, 0, column(side, j - i)] == 1) & exists
            plan[1, number] = on.astype(jnp.int32)
            plan[0, number] = jnp.where(on, j - j0, j1 - j0)


def attend(items, pairs, singles, keys, vals, qt, top, acc, scores, peaks):
    groups, depth, lanes = qt.shape[1:]
    hd, p = depth // 2, lanes // 2
    lead = groups // 2

    def run(count, tiles, entry):
        def score(t, g):
            i, picked = entry(t)
            rows = slice(g * depth, (g + 1) * depth)
            cols = slice(g * lanes, (g + 1) * lanes)
            peak = None
            for u, k in enumerate(picked):
                made = nn(keys[k, :, rows], qt[i, g])
                scores[u * p : (u + 1) * p, cols] = made
                peak = made if peak is None else jnp.maximum(peak, made)
            peaks[:, cols] = jnp.max(peak, axis=0, keepdims=True)

        def weigh(t, g):
            i, picked = entry(t)
            cols = slice(g * lanes, (g + 1) * lanes)
            old = top[i, :, cols]
            new = jnp.maximum(old, peaks[:, cols])
            probs = jnp.exp(scores[: tiles * p, cols] - new).astype(BF16)
            fade = jnp.exp(old - new)
            both, sums = [], []
            for h in range(2):
                rows = slice(h * (hd + ONES), (h + 1) * (hd + ONES))
                val = jnp.concatenate([vals[k, g, rows] for k in picked], axis=1)
                out = nn(val, probs[:, h * p : (h + 1) * p])
                both.append(out[:hd])
                sums.append(out[hd : hd + 8])
            return cols, new, fade, jnp.concatenate(both, axis=1), jnp.concatenate(sums, axis=1)

        def step(t, carry):
            made = []
            for g in range(0, groups, lead):
                for u in range(g, g + lead):
                    score(t + (u + lead) // groups, (u + lead) % groups)
                for u in range(g, g + lead):
                    made.append(weigh(t, u))
            i, _ = entry(t)
            for cols, new, fade, both, sums in made:
                top[i, :, cols] = new
                acc[i, :hd, cols] = acc[i, :hd, cols] * fade + both
                acc[i, hd:, cols] = acc[i, hd:, cols] * fade + sums
            return carry

        for g in range(lead):
            score(0, g)
        lax.fori_loop(0, count, step, 0)

    run(pairs, 2, lambda t: (items[0, t], (items[1, 2 * t], items[1, 2 * t + 1])))
    run(singles, 1, lambda t: (items[2, 2 * t], (items[2, 2 * t + 1],)))


def put_values(vals, tile, g0, v, live):
    p = vals.shape[3]
    hd = vals.shape[2] // 2 - ONES
    flag = jnp.broadcast_to(live.astype(F32).astype(BF16), (ONES, p))
    vt = jnp.where(live, v.T, 0.0).astype(BF16)
    for h in range(v.shape[1] // hd):
        g, r = g0 + h // 2, h % 2 * (hd + ONES)
        vals[tile, g, r : r + hd] = vt[h * hd : (h + 1) * hd]
        vals[tile, g, r + hd : r + hd + ONES] = flag


def put_blocks(tile0, x, w_all, keys, vals, lives):
    p, width = keys.shape[1:]
    wide = min(512, width)
    groups = vals.shape[1]
    for c in range(0, width, wide):
        k = nn(x, w_all[:, width + c : width + c + wide]).astype(BF16)
        v = nn(x, w_all[:, 2 * width + c : 2 * width + c + wide])
        for u, live in enumerate(lives):
            rows = slice(u * p, (u + 1) * p)
            keys[tile0 + u, :, c : c + wide] = k[rows]
            put_values(vals, tile0 + u, c * groups // width, v[rows], live)


def finish(blocks, tiled, acc, w_out, plan):
    hd = acc.shape[1] - 8
    p = tiled.shape[1]
    heads = acc.shape[2] // p
    columns = []
    for i in blocks:
        attn = acc[i, :hd] * (1.0 / acc[i, hd : hd + 1])
        attn = [attn[:, h * p : (h + 1) * p] for h in range(heads)]
        columns.append(jnp.concatenate(attn, axis=0).astype(BF16))
    mixed = tn(jnp.concatenate(columns, axis=1), w_out[...])
    place = lax.broadcasted_iota(jnp.int32, (p, 1), 0)
    made = []
    for u, i in enumerate(blocks):
        value = tiled[i].astype(F32) + mixed[u * p : (u + 1) * p]
        made.append(jnp.where(place < plan[3, 1 + i], value, 0.0).astype(BF16))
    return made


def own_kernel(
    n, split, own, masks, counts, w_qkv, w_out, qt, top, acc, w_all, w_last, plan_near, plan0, plan1, keys, vals,
    items, flags, live, scores, peaks, sems
):
    by, p, width = own.shape
    _, depth = qt.shape[1:3]
    hd = depth // 2
    copies = [
        pltpu.make_async_copy(masks, flags, sems.at[0]),
        pltpu.make_async_copy(counts, live, sems.at[1]),
        pltpu.make_async_copy(w_qkv, w_all, sems.at[2]),
        pltpu.make_async_copy(w_out, w_last, sems.at[3]),
    ]
    for copy in copies:
        copy.start()
    me = lax.axis_index("gx")
    side = toward_near()
    place = lax.broadcasted_iota(jnp.int32, (1, p), 1)
    top[...] = jnp.full_like(top, NEG)
    acc[...] = jnp.zeros_like(acc)
    copies[0].wait()
    copies[1].wait()
    pairs, singles = list_pairs(items, flags, by, [(0, None, 0, by, 0, True)])
    for plan, a, j0, j1 in ((plan_near, side, 0, by), (plan0, -side, 0, split), (plan1, -side, split, by)):
        there = (me + a >= 0) & (me + a < n)
        slab = jnp.clip(me + a, 0, n - 1)
        if plan is plan1:
            mark(plan, flags, by, a, there, j0, j1)
        else:
            plan[3, 0], plan[3, 1 + 2 * by] = list_pairs(plan, flags, by, [(a, there, j0, j1, 0, False)])
        for i in range(by):
            plan[3, 1 + i] = live[i, 0, me]
        for j in range(j0, j1):
            plan[3, 1 + by + j - j0] = live[j, 0, slab]
    zeros = jnp.zeros((hd, p), BF16)
    copies[2].wait()
    mine = own[...].reshape(by * p, width)
    wide = min(512, width)
    for c in range(0, width, wide):
        q = (nn(mine, w_all[:, c : c + wide]).astype(BF16) * BF16(1.0 / hd**0.5)).astype(F32)
        for i in range(by):
            t = q[i * p : (i + 1) * p].T.astype(BF16)
            for u in range(wide // depth):
                g, mid = c // depth + u, u * depth + hd
                qt[i, g, :hd, :p] = t[mid - hd : mid]
                qt[i, g, :hd, p:] = zeros
                qt[i, g, hd:, :p] = zeros
                qt[i, g, hd:, p:] = t[mid : mid + hd]
    put_blocks(0, mine, w_all, keys, vals, [place < live[i, 0, me] for i in range(by)])
    attend(items, pairs, singles, keys, vals, qt, top, acc, scores, peaks)
    copies[3].wait()


def far_work(rim, w_all, qt, plan, top, acc, keys, vals, scores, peaks):
    by = qt.shape[0]
    blocks, p, width = rim.shape
    place = lax.broadcasted_iota(jnp.int32, (1, p), 1)
    put_blocks(0, rim[...].reshape(blocks * p, width), w_all, keys, vals, [place < plan[3, 1 + by + j] for j in range(blocks)])
    attend(plan, plan[3, 0], plan[3, 1 + 2 * by], keys, vals, qt, top, acc, scores, peaks)


def near_kernel(rim, w_all, qt, top_in, acc_in, plan, top, acc, keys, vals, scores, peaks):
    far_work(rim, w_all, qt, plan, top, acc, keys, vals, scores, peaks)


def far_kernel(
    rim, norm, w_all, qt, top_in, acc_in, tiled, w_out, plan, top, acc, held, keys, vals, scores, peaks, nrm
):
    for j in range(rim.shape[0]):
        nrm[j] = normalise(rim[j], norm[0:1], norm[1:2])
    far_work(nrm, w_all, qt, plan, top, acc, keys, vals, scores, peaks)
    for i, value in enumerate(finish(range(held.shape[0]), tiled, acc, w_out, plan)):
        held[i] = value


def last_kernel(
    rim, w_all, qt, top, acc, tiled, w_out, held, plan, result, keys, vals, scores, out, sems
):
    by, early = tiled.shape[0], held.shape[0]
    blocks, p, width = rim.shape
    groups, depth, lanes = qt.shape[1:]
    hd = depth // 2
    copies = [pltpu.make_async_copy(held, result.at[0, :early, 0], sems.at[0])]
    copies[0].start()
    place = lax.broadcasted_iota(jnp.int32, (1, p), 1)
    vals[blocks] = jnp.zeros(vals.shape[1:], BF16)
    lives = [place < plan[3, 1 + by + j] for j in range(blocks)]
    put_blocks(0, rim[...].reshape(blocks * p, width), w_all, keys, vals, lives)
    met = meetings(by, by - blocks, by)
    units = [(i, g) for i in met for g in range(groups)]
    peaks, parts = {}, {}

    def score(u):
        i, g = units[u]
        rows = slice(g * depth, (g + 1) * depth)
        peak = None
        for t, (number, j) in enumerate(met[i]):
            made = nn(keys[j - (by - blocks), :, rows], qt[i, g])
            scores[u % 8, t * p : (t + 1) * p] = made
            high = jnp.where(plan[1, number] == 1, jnp.max(made, axis=0, keepdims=True), NEG)
            peak = high if peak is None else jnp.maximum(peak, high)
        peaks[u] = peak

    def weigh(u):
        i, g = units[u]
        cols = slice(g * lanes, (g + 1) * lanes)
        old = top[i, :, cols]
        new = jnp.maximum(old, peaks[u])
        probs = jnp.exp(jnp.minimum(scores[u % 8, : len(met[i]) * p] - new, 0.0)).astype(BF16)
        fade = jnp.exp(old - new)
        for h in range(2):
            rows = slice(h * (hd + ONES), (h + 1) * (hd + ONES))
            mine = slice(h * p, (h + 1) * p)
            val = jnp.concatenate([vals[plan[0, number], g, rows] for number, _ in met[i]], axis=1)
            made = nn(val, probs[:, mine])
            there = slice(g * lanes + h * p, g * lanes + (h + 1) * p)
            total = acc[i, hd : hd + 1, there] * fade[:, mine] + made[hd : hd + 1]
            value = acc[i, :hd, there] * fade[:, mine] + made[:hd]
            parts[i, 2 * g + h] = (value * (1.0 / total)).astype(BF16)

    def deliver(some):
        columns = [jnp.concatenate([parts[i, h] for h in range(2 * groups)], axis=0) for i in some]
        mixed = tn(jnp.concatenate(columns, axis=1), w_out[...])
        rows = lax.broadcasted_iota(jnp.int32, (p, 1), 0)
        for u, i in enumerate(some):
            value = tiled[i].astype(F32) + mixed[u * p : (u + 1) * p]
            out[i - early] = jnp.where(rows < plan[3, 1 + i], value, 0.0).astype(BF16)
            copies.append(pltpu.make_async_copy(out.at[i - early], result.at[0, i, 0], sems.at[i]))
            copies[-1].start()

    ahead = 6
    for u in range(ahead):
        score(u)
    for u in range(len(units)):
        if u + ahead < len(units):
            score(u + ahead)
        weigh(u)
    some = list(met)
    for c in range(0, len(some), 2):
        deliver(some[c : c + 2])
    for copy in copies:
        copy.wait()


def vmem(x):
    return pltpu.with_memory_space_constraint(x, pltpu.VMEM)


def smem(x):
    return pltpu.with_memory_space_constraint(x, pltpu.SMEM)


def hbm(x):
    return pltpu.with_memory_space_constraint(x, pltpu.HBM)


def shards(n, points, order, masks, counts, gain, shift_bias, w_qkv, w_out):
    _, by, bz, p, width = points.shape
    hd = width // HEADS
    groups, depth, lanes = HEADS // 2, 2 * hd, 2 * p
    split = max(by // 2, 1)
    early = max(split - 1, 1)
    whole = pl.BlockSpec(memory_space=pltpu.VMEM)
    apart = pl.BlockSpec(memory_space=pltpu.HBM)
    words = pl.BlockSpec(memory_space=pltpu.SMEM)
    plan = pltpu.SMEM((4, 8 * by), jnp.int32)
    params = pltpu.CompilerParams(vmem_limit_bytes=LIMIT)
    points, order, masks, w_qkv, w_out = map(hbm, (points, order, masks, w_qkv, w_out))
    counts = hbm(jnp.transpose(counts, (1, 2, 0)))
    live = pltpu.SMEM(counts.shape, jnp.int32)
    flags = pltpu.SMEM(masks.shape, jnp.int32)

    first, rest, places, norm = pl.pallas_call(
        gather_kernel,
        out_shape=(
            pltpu.VMEM((split, p, width), BF16),
            pltpu.VMEM((by - split, p, width), BF16),
            pltpu.VMEM((by - split, 1, p), jnp.int32),
            pltpu.VMEM((2, width), F32),
        ),
        in_specs=[apart] * 5,
        out_specs=(whole,) * 4,
        scratch_shapes=[
            pltpu.VMEM((split, p, width), BF16),
            pltpu.VMEM(order.shape, jnp.int32),
            live,
            pltpu.SemaphoreType.DMA((6,)),
        ],
        compiler_params=params,
        name="gather",
    )(points, order, counts, hbm(gain[None]), hbm(shift_bias[None]))
    tile_rest = pl.pallas_call(
        rest_kernel,
        out_shape=(
            pltpu.VMEM((by, p, width), BF16),
            pltpu.VMEM((by, p, width), BF16),
            pltpu.VMEM((by - split, p, width), BF16),
        ),
        in_specs=[whole] * 4,
        out_specs=(whole,) * 3,
        compiler_params=params,
        name="rest",
    )
    tiled, normed, second = tile_rest(vmem(first), vmem(rest), vmem(places), vmem(norm))
    near_pairs = [(i, i ^ 1) for i in range(n) if i ^ 1 < n]
    far_pairs = [(i, i + 1) for i in range(1, n - 1, 2)] + [(i + 1, i) for i in range(1, n - 1, 2)]

    def moved(value, pairs):
        return lax.ppermute(value, "gx", pairs)

    far0 = moved(first, far_pairs)
    near = moved(normed, near_pairs)
    far1 = moved(second, far_pairs)

    state = (
        pltpu.VMEM((by, 1, groups * lanes), F32),
        pltpu.VMEM((by, hd + 8, groups * lanes), F32),
    )

    def scratch(tiles):
        return [
            pltpu.VMEM((tiles, p, width), BF16),
            pltpu.VMEM((tiles, groups, depth + 2 * ONES, p), BF16),
        ]

    ahead = [
        pltpu.VMEM((2 * p, groups * lanes), F32),
        pltpu.VMEM((1, groups * lanes), F32),
    ]
    own_work = pl.pallas_call(
        functools.partial(own_kernel, n, split),
        out_shape=(
            pltpu.VMEM((by, groups, depth, lanes), BF16),
            *state,
            pltpu.VMEM(w_qkv.shape, BF16),
            pltpu.VMEM(w_out.shape, BF16),
            *(plan,) * 3,
        ),
        in_specs=[whole, apart, apart, apart, apart],
        out_specs=(whole,) * 5 + (words,) * 3,
        scratch_shapes=[*scratch(by), plan, flags, live, *ahead, pltpu.SemaphoreType.DMA((4,))],
        compiler_params=params,
        name="own",
    )
    near_work = pl.pallas_call(
        near_kernel,
        out_shape=state,
        in_specs=[*(whole,) * 5, words],
        out_specs=(whole,) * 2,
        scratch_shapes=[*scratch(by), *ahead],
        input_output_aliases={3: 0, 4: 1},
        compiler_params=params,
        name="near",
    )
    qt, top, acc, w_all, w_last, plan_near, plan0, plan1 = own_work(
        vmem(normed), masks, counts, w_qkv, w_out
    )
    top, acc = near_work(*map(vmem, (near, w_all, qt, top, acc)), smem(plan_near))
    ins = [far0, norm, w_all, qt, top, acc, tiled, w_last]
    top, acc, held = pl.pallas_call(
        far_kernel,
        out_shape=(*state, pltpu.VMEM((early, p, width), BF16)),
        in_specs=[*(whole,) * len(ins), words],
        out_specs=(whole,) * 3,
        scratch_shapes=[*scratch(split), *ahead, pltpu.VMEM((split, p, width), BF16)],
        input_output_aliases={4: 0, 5: 1},
        compiler_params=params,
        name="far",
    )(*map(vmem, ins), smem(plan0))
    ins = [far1, w_all, qt, top, acc, tiled, w_last, held]
    return pl.pallas_call(
        last_kernel,
        out_shape=pltpu.HBM((1, by, bz, p, width), BF16),
        in_specs=[*(whole,) * len(ins), words],
        out_specs=apart,
        scratch_shapes=[
            pltpu.VMEM((by - split, p, width), BF16),
            pltpu.VMEM((by - split + 1, groups, depth + 2 * ONES, p), BF16),
            pltpu.VMEM((8, 3 * p, lanes), F32),
            pltpu.VMEM((by - early, p, width), BF16),
            pltpu.SemaphoreType.DMA((by,)),
        ],
        compiler_params=params,
        name="last",
    )(*map(vmem, ins), smem(plan1))


def solution(mesh):
    placed = (
        P(("groups", "gx"), None, None, None, None),
        P(("groups", "gx"), None, None, None),
        P(("groups", "gx"), None, None, None),
        P("groups", None, None),
        P(),
        P(),
        P(),
        P(),
    )
    return jax.shard_map(
        functools.partial(shards, mesh.shape["gx"]),
        mesh=mesh,
        in_specs=placed,
        out_specs=P(("groups", "gx"), None, None, None, None),
        check_vma=False,
    )
```
